32 devices in a mesh: seq: 4 (over x, core), shard: 8 (over z, y).
Axes of the slice: x: 2, y: 2, z: 4, core: 2. Of those that a mesh axis runs over, the one named last changes fastest.
Arguments:
- inputs: bfloat16 [8, 3072, 768], P('shard', 'seq'), may hold values from -6 to 6
- teacher: bfloat16 [8, 3072, 768], P('shard', 'seq'), may hold values from -6 to 6
- seq_lengths: int32 [8, 3], P('shard'), may hold values from 0 to 3072, as said below
- w_qkv: bfloat16 [768, 2304], P('shard'), may hold values from -0.21875 to 0.21875
- q_bias: bfloat16 [768], P('shard'), may hold values from -4 to 4
- v_bias: bfloat16 [768], P('shard'), may hold values from -0.75 to 0.75
- w_out: bfloat16 [768, 768], P('shard'), may hold values from -3.5 to 3.5
- out_bias: bfloat16 [768], P('shard'), may hold values from -4 to 4
- attn_gain: bfloat16 [768], P('shard'), may hold values from 0.5 to 1.5
- attn_shift: bfloat16 [768], P('shard'), may hold values from -4 to 4
- w_up: bfloat16 [768, 3072], P('shard'), may hold values from -0.21875 to 0.21875
- up_bias: bfloat16 [3072], P('shard'), may hold values from -4 to 4
- w_down: bfloat16 [3072, 768], P('shard'), may hold values from -0.109375 to 0.109375
- down_bias: bfloat16 [768], P('shard'), may hold values from -4 to 4
- ffn_gain: bfloat16 [768], P('shard'), may hold values from 0.5 to 1.5
- ffn_shift: bfloat16 [768], P('shard'), may hold values from -4 to 4
Outputs:
- layer_out: bfloat16 [8, 3072, 768], P('shard', 'seq')
- input_grad: bfloat16 [8, 3072, 768], P('shard', 'seq')
- grad_qkv: float32 [768, 2304], P('shard')
- grad_q_bias: float32 [768], P('shard')
- grad_v_bias: float32 [768], P('shard')
- grad_out: float32 [768, 768], P('shard')
- grad_out_bias: float32 [768], P('shard')
- grad_attn_gain: float32 [768], P('shard')
- grad_attn_shift: float32 [768], P('shard')
- grad_up: float32 [768, 3072], P('shard')
- grad_up_bias: float32 [3072], P('shard')
- grad_down: float32 [3072, 768], P('shard')
- grad_down_bias: float32 [768], P('shard')
- grad_ffn_gain: float32 [768], P('shard')
- grad_ffn_shift: float32 [768], P('shard')
The draws below stay inside these ranges and needn't reach their ends.
Inputs may be any that keep to these rules, and one draw needn't show every extreme that they name: `seq_lengths`: each row lists the lengths of the sequences packed from the start of one group's 3072 slots; the used slots come first and each holds 1024 tokens or more, the unused ones are 0; a row sums to at most 3072; some row holds a single sequence of 3072 tokens; the slots after a row's sum are padding.
All inputs are finite; a program needn't handle non-finite values.
Results may differ from the reference program's by a relative error of at most 0.01.
Values may be sent and summed in bfloat16 or wider, within the bound.
A program may use at most 128 MiB of HBM per device.

```python
import jax
import jax.numpy as jnp
from jax import lax

D = 768
HEADS = 12
HD = 64
FF = 3072
SEGS = 3
GROUPS = 8
GTOK = 3072
LEN_MIN = 1024
BLK = 512
TOKENS = 24576


def draw_seq_lengths(key, part):
    key_jitter, key_full, key_share = jax.random.split(jax.random.fold_in(key, 7), 3)
    group_index = jnp.arange(GROUPS, dtype=jnp.int32)
    base_rows = (GTOK + 2 * GTOK * group_index // max(GROUPS - 1, 1)) // 3
    jitter = jax.random.randint(key_jitter, (GROUPS,), -(GTOK // 12), GTOK // 12 + 1)
    totals = jnp.clip(base_rows + jitter, LEN_MIN, GTOK)
    chosen = jax.random.randint(key_full, (), 0, GROUPS)
    is_chosen = group_index == chosen
    totals = jnp.where(is_chosen, GTOK, totals)
    seq_count = jnp.where(is_chosen, 1, jnp.minimum(totals // LEN_MIN, SEGS))
    slot_ids = jnp.arange(SEGS, dtype=jnp.int32)
    in_use = (slot_ids[None, :] < seq_count[:, None]).astype(jnp.int32)
    shares = jax.random.randint(key_share, (GROUPS, SEGS), 1, 8) * in_use
    spare_rows = totals - seq_count * LEN_MIN
    extra_rows = spare_rows[:, None] * shares // jnp.sum(shares, axis=1, keepdims=True)
    leftover = spare_rows - jnp.sum(extra_rows, axis=1)
    lengths = (LEN_MIN + extra_rows) * in_use + leftover[:, None] * (slot_ids[None, :] == 0).astype(jnp.int32)
    return lengths.astype(jnp.int32)


def raised(values, rng, source, target, blocks, factor):
    def block_of(axis_at):
        return (jnp.arange(values.shape[axis_at]) // (values.shape[axis_at] // blocks)).reshape((-1,) + (1,) * (values.ndim - 1 - axis_at))

    first = jax.random.permutation(rng, blocks)[block_of(target)]
    other_side = (block_of(target) + blocks // 2) % blocks
    return jnp.where((block_of(source) == first) | (block_of(source) == other_side), factor * values, values)


def shard_levels(stream_key, shape, pieces, smallest, top_value):
    level, own = 1.0, jax.random.fold_in(stream_key, 6)
    for position, parts in pieces:
        steps = jnp.exp(jax.random.uniform(jax.random.fold_in(own, position), (parts,), jnp.float32, smallest / len(pieces), top_value / len(pieces)))
        level = level * jnp.repeat(steps, shape[position] // parts).reshape([-1 if axis == position else 1 for axis in range(len(shape))])
    return level


def gaussian(stream_key, dims, width, most, cuts=(), held_as=jnp.bfloat16):
    factor_of = shard_levels(stream_key, dims, cuts, -0.22, 0.18) if cuts else 1.0
    values = jax.random.normal(stream_key, dims, jnp.float32) * width * factor_of
    return jnp.minimum(jnp.maximum(values, -most), most).astype(held_as)


def bell_draw_with(own_key, extent, width, most, pieces, heavy, kind=jnp.bfloat16):
    drawn = width * jax.random.normal(own_key, extent, jnp.float32)
    if pieces:
        drawn = drawn * shard_levels(own_key, extent, pieces, -0.22, 0.18)
    return jnp.clip(raised(drawn, jax.random.fold_in(own_key, 3), *heavy), -most, most).astype(kind)


def setup_inputs(seed: int = 0) -> dict:
    arg_keys = jax.random.split(jax.random.key(seed), 17)
    return {
        "inputs": bell_draw_with(arg_keys[0], (GROUPS, GTOK, D), 1.0, 6.0, ((0, 8), (1, 4)), (0, 2, 8, 2.0)),
        "teacher": gaussian(arg_keys[1], (GROUPS, GTOK, D), 1.0, 6.0, ((0, 8), (1, 4))),
        "seq_lengths": draw_seq_lengths(jax.random.fold_in(arg_keys[16], 71), 0),
        "w_qkv": gaussian(arg_keys[3], (D, 3 * D), D ** -0.5, 0.21875, ((0, 8),)),
        "q_bias": gaussian(arg_keys[4], (D,), 0.3, 4.0, ((0, 8),)),
        "v_bias": gaussian(arg_keys[5], (D,), 0.05, 0.75, ((0, 8),)),
        "w_out": gaussian(arg_keys[6], (D, D), (max(1, 4 * D // LEN_MIN)) ** -0.5, 3.5, ((0, 8),)),
        "out_bias": gaussian(arg_keys[7], (D,), 0.3, 4.0, ((0, 8),)),
        "attn_gain": jnp.clip(1.0 + 0.1 * jax.random.normal(arg_keys[8], (D,), jnp.float32), 0.5, 1.5).astype(jnp.bfloat16),
        "attn_shift": gaussian(arg_keys[9], (D,), 0.3, 4.0, ((0, 8),)),
        "w_up": gaussian(arg_keys[10], (D, FF), D ** -0.5, 0.21875, ((0, 8),)),
        "up_bias": gaussian(arg_keys[11], (FF,), 0.3, 4.0, ((0, 8),)),
        "w_down": gaussian(arg_keys[12], (FF, D), FF ** -0.5, 0.109375, ((0, 8),)),
        "down_bias": gaussian(arg_keys[13], (D,), 0.3, 4.0, ((0, 8),)),
        "ffn_gain": jnp.clip(1.0 + 0.1 * jax.random.normal(arg_keys[14], (D,), jnp.float32), 0.5, 1.5).astype(jnp.bfloat16),
        "ffn_shift": gaussian(arg_keys[15], (D,), 0.3, 4.0, ((0, 8),)),
    }


@jax.custom_vjp
def low(v):
    return lax.optimization_barrier(v.astype(jnp.bfloat16)).astype(jnp.float32)

@jax.custom_vjp
def low_back(v):
    return v

def low_keep(v):
    return (low(v), None)

def low_pass(kept, grad):
    return (grad,)

def back_keep(v):
    return (v, None)

def back_low(kept, grad):
    return (low(grad),)
low.defvjp(low_keep, low_pass)
low_back.defvjp(back_keep, back_low)
epsilon = 1e-12
neg_large = -1e+30
highest = lax.Precision.HIGHEST

def layer_norm(value, gain, shift):
    mean_val = lax.optimization_barrier(jnp.mean(value, axis=-1, keepdims=True))
    centred = value - mean_val
    variance = lax.optimization_barrier(jnp.mean(centred * centred, axis=-1, keepdims=True))
    return centred * lax.rsqrt(variance + epsilon) * gain + shift

def exact_gelu(value):
    return jax.nn.gelu(value, approximate=False)

def group_forward(tokens, params, seg_ids):
    w_qkv, q_bias, v_bias, w_out, out_bias, attn_gain, attn_shift, w_up, up_bias, w_down, down_bias, ffn_gain, ffn_shift = params
    bias_row = jnp.concatenate([q_bias, jnp.zeros_like(q_bias), v_bias])
    qkv = low_back(low(jnp.dot(tokens, w_qkv, precision=highest) + bias_row))
    queries = qkv[:, :D].reshape(GTOK, HEADS, HD)
    keys = qkv[:, D:2 * D].reshape(GTOK, HEADS, HD)
    values = qkv[:, 2 * D:].reshape(GTOK, HEADS, HD)
    score_scale = HD ** (-0.5)
    nblocks = GTOK // BLK

    def attend_block(pair):
        q_blk, seg_blk = pair
        raw = jnp.einsum('bhe,khe->hbk', q_blk, keys, precision=highest)
        scores = low_back(raw * score_scale)
        scores = jnp.where(seg_blk[None, :, None] == seg_ids[None, None, :], scores, neg_large)
        row_max = lax.optimization_barrier(jnp.max(scores, axis=2, keepdims=True))
        exp_scores = jnp.exp(scores - row_max)
        probs = exp_scores / lax.optimization_barrier(jnp.sum(exp_scores, axis=2, keepdims=True))
        return jnp.einsum('hbk,khe->bhe', low(probs), values, precision=highest)
    ctx = lax.map(jax.checkpoint(attend_block), (queries.reshape(nblocks, BLK, HEADS, HD), seg_ids.reshape(nblocks, BLK)))
    context = low_back(low(ctx.reshape(GTOK, D)))
    branch = low_back(jnp.dot(context, w_out, precision=highest) + out_bias)
    normed = layer_norm(tokens + branch, attn_gain, attn_shift)
    pre_act = low_back(jnp.dot(low(normed), w_up, precision=highest) + up_bias)
    ffn_out = low_back(jnp.dot(low(exact_gelu(pre_act)), w_down, precision=highest) + down_bias)
    return layer_norm(normed + ffn_out, ffn_gain, ffn_shift)

def reference(inputs, teacher, seq_lengths, w_qkv, q_bias, v_bias, w_out, out_bias, attn_gain, attn_shift, w_up, up_bias, w_down, down_bias, ffn_gain, ffn_shift):
    params = tuple((p.astype(jnp.float32) for p in (w_qkv, q_bias, v_bias, w_out, out_bias, attn_gain, attn_shift, w_up, up_bias, w_down, down_bias, ffn_gain, ffn_shift)))
    seq_ends = jnp.cumsum(seq_lengths, axis=1).astype(jnp.int32)
    positions = jnp.arange(GTOK, dtype=jnp.int32)
    seg_all = lax.optimization_barrier(jnp.sum((positions[None, :, None] >= seq_ends[:, None, :]).astype(jnp.int32), axis=2)).astype(jnp.int32)
    live_total = jnp.sum(seq_ends[:, -1]).astype(jnp.float32)
    loss_scale = float(TOKENS)

    def per_group(totals, group):
        tokens, target, seg_ids = group

        def forward(tok_in, par_in):
            return group_forward(tok_in, par_in, seg_ids)
        result, pull = jax.vjp(forward, tokens, params)
        live_rows = (seg_ids < SEGS).astype(jnp.float32)[:, None]
        grad_result = (result - target) * live_rows * (loss_scale / live_total)
        grad_tokens, grad_params = pull(grad_result)
        totals = jax.tree.map(jnp.add, totals, grad_params)
        return (totals, (result, grad_tokens))
    zero_grads = jax.tree.map(jnp.zeros_like, params)
    totals, (results, grad_inputs) = lax.scan(per_group, zero_grads, (inputs.astype(jnp.float32), teacher.astype(jnp.float32), seg_all))
    return (results.astype(jnp.bfloat16), grad_inputs.astype(jnp.bfloat16), totals[0], totals[1], totals[2], totals[3], totals[4], totals[5], totals[6], totals[7], totals[8], totals[9], totals[10], totals[11], totals[12])
```

```python
import functools
import math

import jax
import jax.numpy as jnp
from jax import lax
from jax.experimental import pallas as pl
from jax.experimental.pallas import tpu as pltpu
from jax.sharding import PartitionSpec as P

HEADS = 12
HD = 64
ROWS = 80
MESH = pl.DeviceIdType.MESH
f32 = jnp.float32
bf16 = jnp.bfloat16
epsilon = 1e-12
neg_large = -1e30
LOG2E = math.log2(math.e)
LN2 = math.log(2.0)
VMEM_LIMIT = 60 << 20

NN = (((1,), (0,)), ((), ()))
NT = (((1,), (1,)), ((), ()))
TN = (((0,), (0,)), ((), ()))


def mm(left, right, dims=NN):
    return lax.dot_general(left, right, dims, preferred_element_type=f32)


class Place:
    def __init__(self, n):
        self.n = n
        self.hi_n = 4 if n % 4 == 0 else 1
        self.lo_n = n // self.hi_n
        self.s = lax.axis_index("seq")
        self.i = lax.axis_index("shard")
        self.core = lax.rem(self.s, 2)
        self.mate = self.s + 1 - 2 * self.core
        self.far = lax.rem(self.s + 2, 4)
        self.hi = self.i // self.lo_n
        self.lo = lax.rem(self.i, self.lo_n)

    def at_hi(self, hi):
        return (self.s, hi * self.lo_n + self.lo)

    def at_lo(self, lo):
        return (self.s, self.hi * self.lo_n + lo)

    def on_seq(self, s):
        return (s, self.i)


def meet(peers):
    bar = pltpu.get_barrier_semaphore()
    for peer in peers:
        pl.semaphore_signal(bar, inc=1, device_id=peer, device_id_type=MESH)
    pl.semaphore_wait(bar, len(peers))


def rcopy(src, dst, send, recv, peer):
    return pltpu.make_async_remote_copy(
        src_ref=src, dst_ref=dst, send_sem=send, recv_sem=recv, device_id=peer, device_id_type=MESH
    )


def half(cols, core):
    return pl.ds(pl.multiple_of(core * (cols // 2), 128), cols // 2)


def gather_sems(n, hi_n, count):
    return [
        pltpu.SemaphoreType.DMA((count, hi_n)),
        pltpu.SemaphoreType.DMA((count, hi_n)),
        pltpu.SemaphoreType.DMA((count, n)),
        pltpu.SemaphoreType.DMA((count, n)),
        pltpu.SemaphoreType.DMA((count, n)),
        pltpu.SemaphoreType.DMA((count, n)),
        pltpu.SemaphoreType.DMA((count,)),
    ]


class Gather:
    def __init__(self, place, idx, src, dst, split, sems):
        self.p, self.a, self.src, self.dst, self.split = place, idx, src, dst, split
        self.s1, self.r1, self.s2, self.r2, self.s3, self.r3, self.own = sems
        self.sent = []

    def view(self, ref, core):
        return ref.at[:, half(ref.shape[-1], core)] if self.split else ref

    def start(self):
        p, a = self.p, self.a
        self.local = pltpu.make_async_copy(self.src, self.dst.at[p.i], self.own.at[a])
        self.local.start()
        mine = self.view(self.src, p.core)
        for k in range(1, p.hi_n):
            hi = lax.rem(p.hi + k, p.hi_n)
            cp = rcopy(mine, self.view(self.dst.at[p.i], p.core), self.s1.at[a, k], self.r1.at[a, p.hi], p.at_hi(hi))
            cp.start()
            self.sent.append(cp)
        self.pass_lo(0)

    def pass_lo(self, k):
        p, a = self.p, self.a
        hi = lax.rem(p.hi + k, p.hi_n)
        blk = hi * p.lo_n + p.lo
        if k:
            here = self.view(self.dst.at[blk], p.core)
            rcopy(here, here, self.s1.at[a, 0], self.r1.at[a, hi], p.at_hi(hi)).wait_recv()
        src = self.view(self.dst.at[blk] if k else self.src, p.core)
        for j in range(1, p.lo_n):
            lo = lax.rem(p.lo + j, p.lo_n)
            cp = rcopy(
                src,
                self.view(self.dst.at[blk], p.core),
                self.s2.at[a, k * p.lo_n + j],
                self.r2.at[a, blk],
                p.at_lo(lo),
            )
            cp.start()
            self.sent.append(cp)
        if k and self.split:
            self.swap(blk, k * p.lo_n)

    def swap(self, blk, slot):
        p, a = self.p, self.a
        here = self.view(self.dst.at[blk], p.core)
        cp = rcopy(here, here, self.s3.at[a, slot], self.r3.at[a, blk], p.on_seq(p.mate))
        cp.start()
        self.sent.append(cp)

    def take_lo(self, k):
        p, a = self.p, self.a
        hi = lax.rem(p.hi + k, p.hi_n)
        for j in range(1, p.lo_n):
            lo = lax.rem(p.lo + j, p.lo_n)
            blk = hi * p.lo_n + lo
            here = self.view(self.dst.at[blk], p.core)
            rcopy(here, here, self.s2.at[a, 0], self.r2.at[a, blk], p.at_lo(lo)).wait_recv()
            if self.split:
                self.swap(blk, k * p.lo_n + j)

    def finish(self):
        p, a = self.p, self.a
        if self.split:
            for k in range(p.hi_n):
                for j in range(p.lo_n):
                    if k or j:
                        blk = lax.rem(p.hi + k, p.hi_n) * p.lo_n + lax.rem(p.lo + j, p.lo_n)
                        there = self.view(self.dst.at[blk], 1 - p.core)
                        rcopy(there, there, self.s3.at[a, 0], self.r3.at[a, blk], p.on_seq(p.mate)).wait_recv()
        for cp in self.sent:
            cp.wait_send()
        self.local.wait()

    def steps(self):
        for k in range(1, self.p.hi_n):
            yield lambda k=k: self.pass_lo(k)
        for k in range(self.p.hi_n):
            yield lambda k=k: self.take_lo(k)


def peers_of(p, seq_mates):
    out = [p.at_hi(lax.rem(p.hi + k, p.hi_n)) for k in range(1, p.hi_n)]
    out += [p.at_lo(lax.rem(p.lo + j, p.lo_n)) for j in range(1, p.lo_n)]
    return out + [p.on_seq(s) for s in seq_mates]


def gather_kernel(n, splits, chunks, *refs):
    count = len(splits)
    x_ref, srcs = refs[0], refs[1 : 1 + count]
    xg_ref, dsts = refs[1 + count], refs[2 + count : 2 + 2 * count]
    sems = refs[2 + 2 * count : 9 + 2 * count]
    xsem, xs1, xr1, xs2, xr2, xown = refs[9 + 2 * count :]
    p = Place(n)
    meet(peers_of(p, (p.mate, p.far)))
    rows = x_ref.shape[0] // chunks
    part = lambda q: pl.ds(q * rows, rows)
    sent = []
    for q in range(chunks):
        cp = rcopy(x_ref.at[part(q)], xg_ref.at[p.s, part(q)], xs1.at[q], xr1.at[q], p.on_seq(p.far))
        cp.start()
        sent.append(cp)
    gathers = [Gather(p, a, srcs[a], dsts[a], splits[a], sems) for a in range(count)]
    for g in gathers:
        g.start()
    own = pltpu.make_async_copy(x_ref, xg_ref.at[p.s], xown)
    own.start()
    cp = rcopy(x_ref, xg_ref.at[p.s], xsem.at[0], xsem.at[1], p.on_seq(p.mate))
    cp.start()
    sent.append(cp)
    todo = [list(g.steps()) for g in gathers]
    first = [step for steps in todo[:2] for step in steps]
    for step in first:
        step()
    late = [step for steps in todo[2:] for step in steps]
    each = -(-len(late) // chunks) if late else 0
    for q in range(chunks):
        here = xg_ref.at[p.far, part(q)]
        rcopy(here, here, xs1.at[q], xr1.at[q], p.on_seq(p.far)).wait_recv()
        cp = rcopy(here, here, xs2.at[q], xr2.at[q], p.on_seq(p.mate))
        cp.start()
        sent.append(cp)
        for step in late[q * each : (q + 1) * each]:
            step()
    there = xg_ref.at[p.mate]
    rcopy(there, there, xsem.at[0], xsem.at[1], p.on_seq(p.mate)).wait_recv()
    for q in range(chunks):
        there = xg_ref.at[3 - p.s, part(q)]
        rcopy(there, there, xs2.at[q], xr2.at[q], p.on_seq(p.mate)).wait_recv()
    for g in gathers:
        g.finish()
    for cp in sent:
        cp.wait_send()
    own.wait()


def gather_all(x, arrays, splits, n, cid):
    hi_n = 4 if n % 4 == 0 else 1
    chunks = 4
    count = len(arrays)
    anywhere = pl.BlockSpec(memory_space=pl.ANY)
    return pl.pallas_call(
        functools.partial(gather_kernel, n, splits, chunks),
        out_shape=[jax.ShapeDtypeStruct((4,) + x.shape, x.dtype)]
        + [jax.ShapeDtypeStruct((n,) + a.shape, a.dtype) for a in arrays],
        in_specs=[anywhere] * (1 + count),
        out_specs=[anywhere] * (1 + count),
        scratch_shapes=gather_sems(n, hi_n, count)
        + [
            pltpu.SemaphoreType.DMA((2,)),
            pltpu.SemaphoreType.DMA((chunks,)),
            pltpu.SemaphoreType.DMA((chunks,)),
            pltpu.SemaphoreType.DMA((chunks,)),
            pltpu.SemaphoreType.DMA((chunks,)),
            pltpu.SemaphoreType.DMA,
        ],
        compiler_params=pltpu.CompilerParams(collective_id=cid, has_side_effects=True),
    )(x, *arrays)


def exchange_kernel(by_rows, src_ref, dst_ref, send, recv, own):
    p = Place(lax.axis_size("shard"))
    meet([p.on_seq(lax.rem(p.s + k, 4)) for k in range(1, 4)])
    if by_rows:
        rows, cols = src_ref.shape[0] // 4, src_ref.shape[1]
        take = lambda ref, k: ref.at[pl.ds(pl.multiple_of(k * rows, 16), rows)]
        put = lambda ref, k: ref.at[:, pl.ds(pl.multiple_of(k * cols, 128), cols)]
    else:
        rows, cols = src_ref.shape[0], src_ref.shape[1] // 4
        take = lambda ref, k: ref.at[:, pl.ds(pl.multiple_of(k * cols, 128), cols)]
        put = lambda ref, k: ref.at[pl.ds(pl.multiple_of(k * rows, 16), rows)]
    sent = []
    for k in (2, 1, 3):
        to = lax.rem(p.s + k, 4)
        cp = rcopy(take(src_ref, to), put(dst_ref, p.s), send.at[k], recv.at[p.s], p.on_seq(to))
        cp.start()
        sent.append(cp)
    local = pltpu.make_async_copy(take(src_ref, p.s), put(dst_ref, p.s), own)
    local.start()
    for k in (1, 2, 3):
        frm = lax.rem(p.s + k, 4)
        there = put(dst_ref, frm)
        rcopy(there, there, send.at[0], recv.at[frm], p.on_seq(frm)).wait_recv()
    for cp in sent:
        cp.wait_send()
    local.wait()


def exchange(x, by_rows, cid):
    rows, cols = x.shape
    shape = (rows // 4, cols * 4) if by_rows else (rows * 4, cols // 4)
    return pl.pallas_call(
        functools.partial(exchange_kernel, by_rows),
        out_shape=jax.ShapeDtypeStruct(shape, x.dtype),
        in_specs=[pl.BlockSpec(memory_space=pl.ANY)],
        out_specs=pl.BlockSpec(memory_space=pl.ANY),
        scratch_shapes=[
            pltpu.SemaphoreType.DMA((4,)),
            pltpu.SemaphoreType.DMA((4,)),
            pltpu.SemaphoreType.DMA,
        ],
        compiler_params=pltpu.CompilerParams(collective_id=cid, has_side_effects=True),
    )(x)


def forward_kernel(x_ref, w_ref, b_ref, augq_ref, augk_ref, augv_ref, q_ref, k_ref, v_ref, ctx_ref, lse_ref):
    toks = x_ref.shape[0]
    step = 512
    proj = mm(w_ref[0], x_ref[...], NT) + b_ref[0]
    scale = LOG2E / math.sqrt(HD)
    q_ref[0, :HD] = (proj[:HD] * scale).astype(bf16)
    q_ref[0, HD:] = augq_ref[...]
    k_ref[0, :HD] = proj[HD : 2 * HD].astype(bf16)
    k_ref[0, HD:] = augk_ref[...]
    v_ref[0, :HD] = proj[2 * HD :].astype(bf16)
    v_ref[0, HD:] = augv_ref[...]
    q = q_ref[0]
    top = jnp.full((1, toks), -3e38, f32)
    acc = jnp.zeros((ROWS, toks), f32)
    for j in range(toks // step):
        part = pl.ds(j * step, step)
        s = mm(k_ref[0, :, part], q, TN)
        new = jnp.maximum(top, jnp.max(s, axis=0, keepdims=True))
        probs = jnp.exp2(s - new).astype(bf16)
        acc = acc * jnp.exp2(top - new) + mm(v_ref[0, :, part], probs)
        top = new
    z = acc[HD : HD + 1]
    ctx_ref[...] = (acc[:HD] / z).astype(bf16)
    lse_ref[0] = jnp.broadcast_to(top + jnp.log2(z), (8, toks))


def attend(x, w_t, bias, augq, augk, augv):
    heads, _, width = w_t.shape
    toks = x.shape[0]
    whole = pl.BlockSpec((toks, width), lambda h: (0, 0))
    aug = pl.BlockSpec((ROWS - HD, toks), lambda h: (0, 0))
    head = pl.BlockSpec((1, ROWS, toks), lambda h: (h, 0, 0))
    return pl.pallas_call(
        forward_kernel,
        grid=(heads,),
        in_specs=[
            whole,
            pl.BlockSpec((1, 3 * HD, width), lambda h: (h, 0, 0)),
            pl.BlockSpec((1, 3 * HD, 1), lambda h: (h, 0, 0)),
            aug,
            aug,
            aug,
        ],
        out_specs=[
            head,
            head,
            head,
            pl.BlockSpec((HD, toks), lambda h: (h, 0)),
            pl.BlockSpec((1, 8, toks), lambda h: (h, 0, 0)),
        ],
        out_shape=[
            jax.ShapeDtypeStruct((heads, ROWS, toks), bf16),
            jax.ShapeDtypeStruct((heads, ROWS, toks), bf16),
            jax.ShapeDtypeStruct((heads, ROWS, toks), bf16),
            jax.ShapeDtypeStruct((heads * HD, toks), bf16),
            jax.ShapeDtypeStruct((heads, 8, toks), f32),
        ],
        compiler_params=pltpu.CompilerParams(vmem_limit_bytes=VMEM_LIMIT),
    )(x, w_t, bias, augq, augk, augv)


def three_parts(row):
    first = row.astype(bf16)
    rest = row - first.astype(f32)
    second = rest.astype(bf16)
    third = (rest - second.astype(f32)).astype(bf16)
    rows = lax.broadcasted_iota(jnp.int32, (8, row.shape[1]), 0)
    pick = lambda k, v: jnp.where(rows == k, jnp.broadcast_to(v.astype(f32), rows.shape), 0.0)
    return pick(0, first) + pick(1, second) + pick(2, third)


def backward_kernel(q_ref, k_ref, v_ref, ctx_ref, lse_ref, dctx_ref, out_ref, qa, da, dq):
    toks = q_ref.shape[2]
    step = 512
    qa[:HD] = q_ref[0, :HD]
    mask = q_ref[0, HD : HD + 8].astype(f32)
    zero = jnp.zeros((8, toks), f32)
    qa[HD:] = jnp.concatenate([mask, three_parts(-lse_ref[0, :1])], axis=0).astype(bf16)
    dctx = dctx_ref[...]
    delta = jnp.sum(dctx.astype(f32) * ctx_ref[...].astype(f32), axis=0, keepdims=True)
    da[:HD] = dctx
    da[HD:] = jnp.concatenate([three_parts(-delta), zero], axis=0).astype(bf16)
    q, do = qa[...], da[...]
    for j in range(toks // step):
        part = pl.ds(j * step, step)
        k = k_ref[0, :, part]
        probs = jnp.exp2(mm(k, q, TN))
        gprobs = mm(v_ref[0, :, part], do, TN)
        ds = (probs * gprobs).astype(bf16)
        probs = probs.astype(bf16)
        out_ref[0, 2 * HD :, part] = mm(do[:HD], probs, NT).astype(bf16)
        out_ref[0, HD : 2 * HD, part] = (mm(q[:HD], ds, NT) * LN2).astype(bf16)
        dq_part = mm(k[:HD], ds)
        dq[...] = dq_part if j == 0 else dq[...] + dq_part
    out_ref[0, :HD] = (dq[...] * (1.0 / math.sqrt(HD))).astype(bf16)


def attend_back(q, k, v, ctx, lse, dctx):
    heads, _, toks = q.shape
    head = pl.BlockSpec((1, ROWS, toks), lambda h: (h, 0, 0))
    rows = pl.BlockSpec((HD, toks), lambda h: (h, 0))
    return pl.pallas_call(
        backward_kernel,
        grid=(heads,),
        in_specs=[head, head, head, rows, pl.BlockSpec((1, 8, toks), lambda h: (h, 0, 0)), rows],
        out_specs=pl.BlockSpec((1, 3 * HD, toks), lambda h: (h, 0, 0)),
        out_shape=jax.ShapeDtypeStruct((heads, 3 * HD, toks), bf16),
        scratch_shapes=[
            pltpu.VMEM((ROWS, toks), bf16),
            pltpu.VMEM((ROWS, toks), bf16),
            pltpu.VMEM((HD, toks), f32),
        ],
        compiler_params=pltpu.CompilerParams(vmem_limit_bytes=VMEM_LIMIT),
    )(q, k, v, ctx, lse, dctx)


class Reduce:
    def __init__(self, p, src, out, bufs, sems, split):
        self.p, self.src, self.out, self.split = p, src, out, split
        self.acc, self.up, self.down, self.side, self.far = bufs
        (self.s0, self.r0, self.su, self.ru, self.sd, self.rd, self.sl, self.rl, self.sx) = sems
        self.sent = []

    @staticmethod
    def scratch(n, hi_n, rows, cols, split, out_seq):
        lo_n = n // hi_n
        w = cols // 2 if split else cols
        bufs = [
            pltpu.VMEM((n, rows, w), bf16),
            pltpu.VMEM((hi_n, lo_n, rows, w), bf16),
            pltpu.VMEM((hi_n, lo_n, rows, w), bf16),
            pltpu.VMEM((lo_n, rows, w), bf16),
            pltpu.VMEM((2, rows, w), bf16),
        ]
        dma = pltpu.SemaphoreType.DMA
        sems = [
            dma((hi_n,)), dma((hi_n,)), dma((hi_n,)), dma((hi_n,)), dma((hi_n,)),
            dma((hi_n,)), dma((lo_n,)), dma((lo_n,)), dma((8,)),
        ]
        return bufs, sems

    def blocks(self, ref, d):
        return ref.at[pl.ds(d * self.p.lo_n, self.p.lo_n)]

    def mine(self, ref, core):
        return ref.at[:, :, half(self.src.shape[-1], core)] if self.split else ref

    def start(self):
        p = self.p
        if self.split:
            for d in self.order():
                cp = rcopy(
                    self.mine(self.blocks(self.src, d), 1 - p.core),
                    self.blocks(self.acc, d),
                    self.s0.at[d],
                    self.r0.at[d],
                    p.on_seq(p.mate),
                )
                cp.start()
                self.sent.append(cp)

    def order(self):
        n = self.p.hi_n
        return [d for pair in zip(reversed(range(n // 2, n)), range(n // 2)) for d in pair] if n > 1 else [0]

    def chip_sum(self, d):
        p = self.p
        here = self.blocks(self.acc, d)
        own = self.mine(self.blocks(self.src, d), p.core)
        if self.split:
            rcopy(here, here, self.s0.at[d], self.r0.at[d], p.on_seq(p.mate)).wait_recv()
            here[...] = (here[...].astype(f32) + own[...].astype(f32)).astype(bf16)
        else:
            here[...] = own[...]

    def chain(self, d, buf, send, recv, step):
        p = self.p
        first = 0 if step > 0 else p.hi_n - 1
        before = (p.hi < d) if step > 0 else (p.hi > d)
        here = buf.at[d]
        acc = self.blocks(self.acc, d)

        @pl.when(before & (p.hi == first))
        def _():
            rcopy(acc, here, send.at[d], recv.at[d], p.at_hi(p.hi + step)).start()

        @pl.when(before & (p.hi != first))
        def _():
            rcopy(here, here, send.at[d], recv.at[d], p.at_hi(p.hi + step)).wait_recv()
            here[...] = (here[...].astype(f32) + acc[...].astype(f32)).astype(bf16)
            rcopy(here, here, send.at[d], recv.at[d], p.at_hi(p.hi + step)).start()

    def chain_sent(self, d, buf, send, recv, step):
        p = self.p
        before = (p.hi < d) if step > 0 else (p.hi > d)

        @pl.when(before)
        def _():
            here = buf.at[d]
            rcopy(here, here, send.at[d], recv.at[d], p.at_hi(p.hi + step)).wait_send()

    def gather_hi(self):
        p = self.p
        here = self.acc.at[pl.ds(p.hi * p.lo_n, p.lo_n)]
        total = here[...].astype(f32)
        here[...] = here[...]

        @pl.when(p.hi > 0)
        def _():
            got = self.up.at[p.hi]
            rcopy(got, got, self.su.at[0], self.ru.at[p.hi], p.at_hi(p.hi)).wait_recv()
            here[...] = (here[...].astype(f32) + got[...].astype(f32)).astype(bf16)

        @pl.when(p.hi < p.hi_n - 1)
        def _():
            got = self.down.at[p.hi]
            rcopy(got, got, self.sd.at[0], self.rd.at[p.hi], p.at_hi(p.hi)).wait_recv()
            here[...] = (here[...].astype(f32) + got[...].astype(f32)).astype(bf16)

        for j in range(1, p.lo_n):
            lo = lax.rem(p.lo + j, p.lo_n)
            cp = rcopy(
                self.acc.at[p.hi * p.lo_n + lo], self.side.at[p.lo], self.sl.at[j], self.rl.at[p.lo], p.at_lo(lo)
            )
            cp.start()
            self.sent.append(cp)

    def gather_lo(self):
        p = self.p
        total = self.acc[p.i].astype(f32)
        for j in range(1, p.lo_n):
            lo = lax.rem(p.lo + j, p.lo_n)
            got = self.side.at[lo]
            rcopy(got, got, self.sl.at[0], self.rl.at[lo], p.at_lo(lo)).wait_recv()
            total = total + got[...].astype(f32)
        self.far[0] = total.astype(bf16)
        if self.split:
            cp = rcopy(self.far.at[0], self.far.at[1], self.sx.at[0], self.sx.at[1], p.on_seq(p.far))
            cp.start()
            self.sent.append(cp)
        else:
            for k in range(1, 4):
                to = lax.rem(p.s + k, 4)
                cp = rcopy(self.far.at[0], self.out.at[p.s], self.sx.at[k], self.sx.at[4 + p.s], p.on_seq(to))
                cp.start()
                self.sent.append(cp)
            self.out[p.s] = self.far[0]

    def gather_chips(self):
        p = self.p
        if self.split:
            got = self.far.at[1]
            rcopy(got, got, self.sx.at[0], self.sx.at[1], p.on_seq(p.far)).wait_recv()
            where = half(self.src.shape[-1], p.core)
            self.out[:, where] = (self.far[0].astype(f32) + self.far[1].astype(f32)).astype(bf16)
            cp = rcopy(self.out.at[:, where], self.out.at[:, where], self.sx.at[2], self.sx.at[3], p.on_seq(p.mate))
            cp.start()
            self.sent.append(cp)

    def finish(self):
        p = self.p
        if self.split:
            there = self.out.at[:, half(self.src.shape[-1], 1 - p.core)]
            rcopy(there, there, self.sx.at[2], self.sx.at[3], p.on_seq(p.mate)).wait_recv()
        else:
            for k in range(1, 4):
                frm = lax.rem(p.s + k, 4)
                there = self.out.at[frm]
                rcopy(there, there, self.sx.at[0], self.sx.at[4 + frm], p.on_seq(frm)).wait_recv()
        for cp in self.sent:
            cp.wait_send()
        for d in range(1, p.hi_n):
            self.chain_sent(d, self.up, self.su, self.ru, 1)
            self.chain_sent(d - 1, self.down, self.sd, self.rd, -1)

    def steps(self):
        n = self.p.hi_n
        for d in self.order():
            yield lambda d=d: self.chip_sum(d)
        for k in range(1, n):
            yield lambda k=k: self.chain(n - k, self.up, self.su, self.ru, 1)
            yield lambda k=k: self.chain(k - 1, self.down, self.sd, self.rd, -1)
        yield self.gather_hi
        yield self.gather_lo
        yield self.gather_chips


def reduce_peers(p):
    out = [p.at_hi(lax.rem(p.hi + k, p.hi_n)) for k in range(1, p.hi_n)]
    out += [p.at_lo(lax.rem(p.lo + j, p.lo_n)) for j in range(1, p.lo_n)]
    return out + [p.on_seq(lax.rem(p.s + k, 4)) for k in range(1, 4)]


def reduce_kernel(n, splits, *refs):
    count = len(splits)
    srcs, outs = refs[:count], refs[count : 2 * count]
    rest = refs[2 * count :]
    p = Place(n)
    meet(reduce_peers(p))
    reds = [Reduce(p, srcs[a], outs[a], rest[14 * a : 14 * a + 5], rest[14 * a + 5 : 14 * a + 14], splits[a]) for a in range(count)]
    for r in reds:
        r.start()
    for row in zip(*[list(r.steps()) for r in reds]):
        for step in row:
            step()
    for r in reds:
        r.finish()


def reduce_all(arrays, splits, n, cid):
    hi_n = 4 if n % 4 == 0 else 1
    vm = pl.BlockSpec(memory_space=pltpu.VMEM)
    scratch, outs = [], []
    for a, split in zip(arrays, splits):
        bufs, sems = Reduce.scratch(n, hi_n, a.shape[1], a.shape[2], split, not split)
        scratch += bufs + sems
        outs.append(jax.ShapeDtypeStruct(a.shape[1:] if split else (4,) + a.shape[1:], bf16))
    return pl.pallas_call(
        functools.partial(reduce_kernel, n, splits),
        out_shape=outs,
        in_specs=[vm] * len(arrays),
        out_specs=[vm] * len(arrays),
        scratch_shapes=scratch,
        compiler_params=pltpu.CompilerParams(collective_id=cid, has_side_effects=True, vmem_limit_bytes=VMEM_LIMIT),
    )(*arrays)


def finish_kernel(n, part_ref, resid_ref, vec_ref, out_ref, vout_ref, near, far, give, vin, vseq, sems, vs, vr, ws, wr):
    p = Place(n)
    seq_mates = [p.on_seq(lax.rem(p.s + k, 4)) for k in range(1, 4)]
    others = [(p.s, lax.rem(p.i + k, n)) for k in range(1, n)]
    meet(seq_mates + others)
    rows = part_ref.shape[0] // 4
    block = lambda s: part_ref.at[pl.ds(pl.multiple_of(s * rows, 16), rows)]
    sent = []
    beyond = lax.rem(p.mate + 2, 4)
    for slot, to in ((0, beyond), (1, p.mate)):
        cp = rcopy(block(to), near.at[slot], sems.at[slot], sems.at[2 + slot], p.on_seq(p.mate))
        cp.start()
        sent.append(cp)
    for k in range(1, n):
        to = lax.rem(p.i + k, n)
        cp = rcopy(vec_ref.at[to], vin.at[p.i], vs.at[k], vr.at[p.i], (p.s, to))
        cp.start()
        sent.append(cp)
    vin[p.i] = vec_ref[p.i]
    rcopy(near.at[0], near.at[0], sems.at[0], sems.at[2], p.on_seq(p.mate)).wait_recv()
    give[...] = (near[0].astype(f32) + block(p.far)[...].astype(f32)).astype(bf16)
    cp = rcopy(give, far, sems.at[4], sems.at[5], p.on_seq(p.far))
    cp.start()
    sent.append(cp)
    rcopy(near.at[1], near.at[1], sems.at[1], sems.at[3], p.on_seq(p.mate)).wait_recv()
    total = resid_ref[...] + near[1].astype(f32) + block(p.s)[...].astype(f32)
    for k in range(1, n):
        frm = lax.rem(p.i + k, n)
        there = vin.at[frm]
        rcopy(there, there, vs.at[0], vr.at[frm], (p.s, frm)).wait_recv()
    vseq[p.s] = jnp.sum(vin[...], axis=0)
    for k in range(1, 4):
        to = lax.rem(p.s + k, 4)
        cp = rcopy(vseq.at[p.s], vseq.at[p.s], ws.at[k], wr.at[p.s], p.on_seq(to))
        cp.start()
        sent.append(cp)
    rcopy(far, far, sems.at[4], sems.at[5], p.on_seq(p.far)).wait_recv()
    out_ref[...] = (total + far[...].astype(f32)).astype(bf16)
    for k in range(1, 4):
        frm = lax.rem(p.s + k, 4)
        there = vseq.at[frm]
        rcopy(there, there, ws.at[0], wr.at[frm], p.on_seq(frm)).wait_recv()
    vout_ref[...] = (vseq[0] + vseq[1]) + (vseq[2] + vseq[3])
    for cp in sent:
        cp.wait_send()


def finish(part, resid, vec, n, cid):
    rows, width = resid.shape
    vm = pl.BlockSpec(memory_space=pltpu.VMEM)
    dma = pltpu.SemaphoreType.DMA
    return pl.pallas_call(
        functools.partial(finish_kernel, n),
        out_shape=[jax.ShapeDtypeStruct((rows, width), bf16), jax.ShapeDtypeStruct(vec.shape[1:], f32)],
        in_specs=[vm] * 3,
        out_specs=[vm] * 2,
        scratch_shapes=[
            pltpu.VMEM((2, rows, width), bf16),
            pltpu.VMEM((rows, width), bf16),
            pltpu.VMEM((rows, width), bf16),
            pltpu.VMEM(vec.shape, f32),
            pltpu.VMEM((4,) + vec.shape[1:], f32),
            dma((6,)),
            dma((n,)),
            dma((n,)),
            dma((4,)),
            dma((4,)),
        ],
        compiler_params=pltpu.CompilerParams(collective_id=cid, has_side_effects=True, vmem_limit_bytes=VMEM_LIMIT),
    )(part, resid, vec)


def layer_norm(value, gain, shift):
    mean_val = jnp.mean(value, axis=-1, keepdims=True)
    centred = value - mean_val
    variance = jnp.mean(centred * centred, axis=-1, keepdims=True)
    return centred * lax.rsqrt(variance + epsilon) * gain + shift


def exact_gelu(value):
    return jax.nn.gelu(value, approximate=False)


def on_device(
    inputs, teacher, seq_lengths, w_qkv, q_bias, v_bias, w_out, out_bias, attn_gain, attn_shift, w_up, up_bias,
    w_down, down_bias, ffn_gain, ffn_shift,
):
    n = lax.axis_size("shard")
    s = lax.axis_index("seq")
    toks, width = inputs.shape[1:]
    group = 4 * toks
    hidden = w_up.shape[1]
    rows = w_qkv.shape[0]
    heads = HEADS // 4
    tokens = inputs[0]
    lens = seq_lengths[0]
    ends = [lens[0], lens[0] + lens[1], lens[0] + lens[1] + lens[2]]

    own_w = lax.dynamic_index_in_dim(w_qkv.reshape(rows, 3, 4, heads, HD), s, 2, keepdims=False)
    own_w = jnp.transpose(own_w, (0, 2, 1, 3)).reshape(rows, heads * 3 * HD)
    live = jnp.stack([ends[2] // 64, lax.rem(ends[2], 64)]).astype(bf16)
    small = jnp.concatenate(
        [q_bias[None], v_bias[None], out_bias[None], attn_gain[None], attn_shift[None], down_bias[None], ffn_gain[None],
         ffn_shift[None], up_bias.reshape(hidden // width, rows), jnp.broadcast_to(live[:, None], (2, rows))], axis=0
    )
    small = jnp.pad(small, ((0, 16 - small.shape[0]), (0, -rows % 128)))
    xg, wq_g, small_g, wo_g, up_g, down_g = gather_all(
        tokens, (own_w, small, w_out, w_up, w_down), (False, False, True, True, True), n, 1
    )
    x_all = xg.reshape(group, width)
    wq = wq_g.reshape(width, heads * 3 * HD)
    full_out = wo_g.reshape(width, width)
    full_up = up_g.reshape(width, hidden)
    full_down = down_g.reshape(hidden, width)
    vecs = jnp.transpose(small_g[:, :, :rows], (1, 0, 2)).astype(f32)
    rest = vecs[:8].reshape(8, width)
    b_q, b_v, b_out, g_attn, s_attn, b_down, g_ffn, s_ffn = [rest[k] for k in range(8)]
    b_up = jnp.transpose(vecs[8 : 8 + hidden // width], (1, 0, 2)).reshape(hidden)
    live_total = jnp.sum(vecs[8 + hidden // width, :, 0]) * 64.0 + jnp.sum(vecs[9 + hidden // width, :, 0])

    own_q = lax.dynamic_slice_in_dim(b_q, s * heads * HD, heads * HD).reshape(heads, 1, HD)
    own_v = lax.dynamic_slice_in_dim(b_v, s * heads * HD, heads * HD).reshape(heads, 1, HD)
    bias = jnp.concatenate([own_q, jnp.zeros_like(own_q), own_v], axis=1).reshape(heads, 3 * HD, 1)

    pos = lax.broadcasted_iota(jnp.int32, (16, group), 1)
    row = lax.broadcasted_iota(jnp.int32, (16, group), 0)
    seg = sum((pos >= e).astype(jnp.int32) for e in ends)
    augq = jnp.where((row < 4) & (seg != row), neg_large, 0.0).astype(bf16)
    augk = jnp.where((row < 4) & (seg == row) | (row >= 8) & (row < 11), 1.0, 0.0).astype(bf16)
    augv = jnp.where(row < 3, 1.0, 0.0).astype(bf16)

    w_t = jnp.transpose(wq).reshape(heads, 3 * HD, width)
    q, k, v, ctx, lse = attend(x_all, w_t, bias, augq, augk, augv)
    merged = exchange(ctx, False, 2)

    branch = mm(merged, full_out, TN) + b_out
    resid_one = tokens.astype(f32) + branch
    normed, norm_one_back = jax.vjp(layer_norm, resid_one, g_attn, s_attn)
    normed_low = normed.astype(bf16)
    pre_act = mm(normed_low, full_up) + b_up
    activated, gelu_back = jax.vjp(exact_gelu, pre_act)
    act_low = activated.astype(bf16)
    resid_two = normed + mm(act_low, full_down) + b_down
    result, norm_two_back = jax.vjp(layer_norm, resid_two, g_ffn, s_ffn)
    own_pos = s * toks + lax.iota(jnp.int32, toks)
    live_rows = (own_pos < ends[2]).astype(f32)
    loss_scale = float(group * n)
    grad_result = (result - teacher[0].astype(f32)) * live_rows[:, None] * (loss_scale / live_total)
    grad_resid_two, d_ffn_gain, d_ffn_shift = norm_two_back(grad_result)
    grad_ffn_low = grad_resid_two.astype(bf16)
    d_down = mm(act_low, grad_ffn_low, TN).astype(bf16)
    d_down_bias = jnp.sum(grad_ffn_low, axis=0, dtype=f32)
    (grad_pre_full,) = gelu_back(mm(grad_ffn_low, full_down, NT))
    grad_pre = grad_pre_full.astype(bf16)
    d_up = mm(normed_low, grad_pre, TN).astype(bf16)
    d_up_bias = jnp.sum(grad_pre, axis=0, dtype=f32)
    grad_normed = mm(grad_pre, full_up, NT) + grad_resid_two
    grad_resid_one, d_attn_gain, d_attn_shift = norm_one_back(grad_normed)
    grad_branch = grad_resid_one.astype(bf16)
    d_out = mm(merged, grad_branch).astype(bf16)
    d_out_bias = jnp.sum(grad_branch, axis=0, dtype=f32)
    grad_merged = mm(full_out, grad_branch, NT).astype(bf16)
    dctx = exchange(grad_merged, True, 3)

    d_up_r, d_down_r, d_out_r = reduce_all(
        (d_up.reshape(n, rows, hidden), d_down.reshape(n, hidden // n, width), d_out.reshape(n, rows, width)),
        (True, True, True), n, 4,
    )
    dqkv = attend_back(q, k, v, ctx, lse, dctx).reshape(heads * 3 * HD, group)
    d_qkv = lax.dot_general(x_all, dqkv, (((0,), (1,)), ((), ())), preferred_element_type=f32).astype(bf16)
    part = lax.dot_general(dqkv, wq, (((0,), (1,)), ((), ())), preferred_element_type=f32).astype(bf16)
    d_bias = jnp.sum(dqkv, axis=1, dtype=f32).reshape(heads, 3, HD)
    place = lambda v: lax.dynamic_update_slice_in_dim(jnp.zeros((width,), f32), v.reshape(-1), s * heads * HD, 0)
    flat = jnp.stack(
        [place(d_bias[:, 0]), place(d_bias[:, 2]), d_out_bias, d_attn_gain, d_attn_shift, d_down_bias, d_ffn_gain, d_ffn_shift]
    )
    vec = jnp.concatenate(
        [jnp.transpose(flat.reshape(8, n, rows), (1, 0, 2)), d_up_bias.reshape(n, hidden // width, rows)], axis=1
    )
    vec = jnp.pad(vec, ((0, 0), (0, 16 - vec.shape[1]), (0, -rows % 128)))
    (d_qkv_r,) = reduce_all((d_qkv.reshape(n, rows, heads * 3 * HD),), (False,), n, 5)
    grad_in, vsum = finish(part, grad_resid_one, vec, n, 6)

    d_qkv_out = jnp.transpose(d_qkv_r.reshape(4, rows, heads, 3, HD), (1, 3, 0, 2, 4)).reshape(rows, 3 * width)
    vsum = vsum[:, :rows]
    d_up_bias = vsum[8 : 8 + hidden // width].reshape(hidden // n)
    return (
        result.astype(bf16)[None], grad_in[None], d_qkv_out.astype(f32), vsum[0], vsum[1], d_out_r.astype(f32), vsum[2],
        vsum[3], vsum[4], d_up_r.astype(f32), d_up_bias, d_down_r.astype(f32), vsum[5], vsum[6], vsum[7],
    )


def solution(mesh):
    tokens, matrix, vector = P("shard", "seq", None), P("shard", None), P("shard")
    in_specs = (tokens, tokens, matrix, matrix, vector, vector, matrix, vector, vector, vector, matrix, vector, matrix,
                vector, vector, vector)
    out_specs = (tokens, tokens, matrix, vector, vector, matrix, vector, vector, vector, matrix, vector, matrix, vector,
                 vector, vector)
    return jax.shard_map(on_device, mesh=mesh, in_specs=in_specs, out_specs=out_specs, check_vma=False)
```

```python
import functools
import math

import jax
import jax.numpy as jnp
from jax import lax
from jax.experimental import pallas as pl
from jax.experimental.pallas import tpu as pltpu
from jax.sharding import PartitionSpec as P

HEADS = 12
HD = 64
ROWS = 80
MESH = pl.DeviceIdType.MESH
f32 = jnp.float32
bf16 = jnp.bfloat16
epsilon = 1e-12
neg_large = -1e30
LOG2E = math.log2(math.e)
LN2 = math.log(2.0)
VMEM_LIMIT = 60 << 20

NN = (((1,), (0,)), ((), ()))
NT = (((1,), (1,)), ((), ()))
TN = (((0,), (0,)), ((), ()))


def mm(left, right, dims=NN):
    return lax.dot_general(left, right, dims, preferred_element_type=f32)


class Place:
    def __init__(self, n):
        self.n = n
        self.hi_n = 4 if n % 4 == 0 else 1
        self.lo_n = n // self.hi_n
        self.s = lax.axis_index("seq")
        self.i = lax.axis_index("shard")
        self.core = lax.rem(self.s, 2)
        self.mate = self.s + 1 - 2 * self.core
        self.far = lax.rem(self.s + 2, 4)
        self.hi = self.i // self.lo_n
        self.lo = lax.rem(self.i, self.lo_n)

    def at_hi(self, hi):
        return (self.s, hi * self.lo_n + self.lo)

    def at_lo(self, lo):
        return (self.s, self.hi * self.lo_n + lo)

    def on_seq(self, s):
        return (s, self.i)


def meet(peers):
    bar = pltpu.get_barrier_semaphore()
    for peer in peers:
        pl.semaphore_signal(bar, inc=1, device_id=peer, device_id_type=MESH)
    pl.semaphore_wait(bar, len(peers))


def rcopy(src, dst, send, recv, peer):
    return pltpu.make_async_remote_copy(
        src_ref=src, dst_ref=dst, send_sem=send, recv_sem=recv, device_id=peer, device_id_type=MESH
    )


def half(cols, core):
    return pl.ds(pl.multiple_of(core * (cols // 2), 128), cols // 2)


def gather_sems(n, count):
    dma = pltpu.SemaphoreType.DMA
    return [dma((count, 2 * n)), dma((count, n)), dma((count, n)), dma((count, n)), dma((count, 3 * n)), dma((count, 3 * n)), dma((count,))]


class Gather:
    def __init__(self, place, idx, src, dst, mode, sems):
        self.p, self.a, self.src, self.dst, self.mode = place, idx, src, dst, mode
        self.s1, self.r1, self.s2, self.r2, self.s3, self.r3, self.own = sems

    def view(self, ref, core, chip=None):
        cols = ref.shape[-1]
        if self.mode == "whole":
            return ref
        if self.mode == "half" or chip is None:
            return ref.at[:, half(cols, core)]
        at = core * (cols // 2) + chip * (cols // 4)
        return ref.at[:, pl.ds(pl.multiple_of(at, 128), cols // 4)]

    def mine(self, ref):
        return self.view(ref, self.p.core, self.p.s // 2)

    def local(self):
        return pltpu.make_async_copy(self.src, self.dst.at[self.p.i], self.own.at[self.a])

    def along_hi(self, hi, step):
        p, a = self.p, self.a
        blk = hi * p.lo_n + p.lo
        there = self.mine(self.dst.at[blk])
        return lambda own: rcopy(
            self.mine(self.src) if own else there, there, self.s1.at[a, blk if step > 0 else p.n + blk], self.r1.at[a, blk],
            p.at_hi(p.hi + step),
        )

    def along_lo(self, hi, j, own=False):
        p, a = self.p, self.a
        blk = hi * p.lo_n + p.lo
        there = self.mine(self.dst.at[blk])
        return rcopy(
            self.mine(self.src) if own else there, there, self.s2.at[a, hi * p.lo_n + j], self.r2.at[a, blk],
            p.at_lo(lax.rem(p.lo + j, p.lo_n)),
        )

    def to_far(self, blk, chip):
        p, a = self.p, self.a
        here = self.view(self.dst.at[blk], p.core, chip)
        return rcopy(here, here, self.s3.at[a, 2 * p.n + blk], self.r3.at[a, 2 * p.n + blk], p.on_seq(p.far))

    def to_mate(self, blk, core, chip=None):
        p, a = self.p, self.a
        here = self.view(self.dst.at[blk], core, chip)
        at = blk if chip is None else chip * p.n + blk
        return rcopy(here, here, self.s3.at[a, at], self.r3.at[a, at], p.on_seq(p.mate))

    def here(self, blk):
        if self.mode == "half":
            self.to_mate(blk, self.p.core).start()
        if self.mode == "quarter":
            self.to_far(blk, self.p.s // 2).start()
            self.to_mate(blk, self.p.core, self.p.s // 2).start()

    def start(self):
        p = self.p
        self.local().start()
        for step in (1, -1):

            @pl.when((p.hi + step >= 0) & (p.hi + step < p.hi_n))
            def _(step=step):
                self.along_hi(p.hi, step)(True).start()

        for j in range(1, p.lo_n):
            self.along_lo(p.hi, j, True).start()

    def come(self, m, step):
        p = self.p
        hi = p.hi - step * m

        @pl.when((hi >= 0) & (hi < p.hi_n))
        def _():
            blk = hi * p.lo_n + p.lo
            there = self.mine(self.dst.at[blk])
            rcopy(there, there, self.s1.at[self.a, 0], self.r1.at[self.a, blk], p.at_hi(p.hi)).wait_recv()

            @pl.when((p.hi + step >= 0) & (p.hi + step < p.hi_n))
            def _():
                self.along_hi(hi, step)(False).start()

            for j in range(1, p.lo_n):
                self.along_lo(hi, j).start()
            self.here(blk)

    def pass_on(self, m):
        self.come(m, 1)
        self.come(m, -1)

    def both_ways(self, m, body):
        p = self.p
        if m == 0:
            body(p.hi)
            return
        for step in (1, -1):
            hi = p.hi - step * m
            pl.when((hi >= 0) & (hi < p.hi_n))(lambda hi=hi: body(hi))

    def take_lo(self, m):
        p, a = self.p, self.a

        def body(hi):
            for j in range(1, p.lo_n):
                lo = lax.rem(p.lo + j, p.lo_n)
                blk = hi * p.lo_n + lo
                there = self.mine(self.dst.at[blk])
                rcopy(there, there, self.s2.at[a, 0], self.r2.at[a, blk], p.at_lo(lo)).wait_recv()
                self.here(blk)

        self.both_ways(m, body)

    def take_far(self, m):
        p = self.p

        def body(hi):
            for j in range(p.lo_n):
                if m or j:
                    blk = hi * p.lo_n + lax.rem(p.lo + j, p.lo_n)
                    self.to_far(blk, 1 - p.s // 2).wait_recv()
                    self.to_mate(blk, p.core, 1 - p.s // 2).start()

        if self.mode == "quarter":
            self.both_ways(m, body)

    def finish(self):
        p = self.p
        for m in range(p.hi_n):
            hi = lax.rem(p.hi + m, p.hi_n)
            for j in range(p.lo_n):
                blk = hi * p.lo_n + lax.rem(p.lo + j, p.lo_n)
                if self.mode != "whole" and (m or j):
                    for chip in (None,) if self.mode == "half" else (0, 1):
                        self.to_mate(blk, 1 - p.core, chip).wait_recv()
                        self.to_mate(blk, p.core, chip).wait_send()
                    if self.mode == "quarter":
                        self.to_far(blk, p.s // 2).wait_send()
                if j:
                    self.along_lo(hi, j).wait_send()
        for step in (1, -1):
            for m in range(p.hi_n):
                hi = p.hi - step * m

                @pl.when((hi >= 0) & (hi < p.hi_n) & (p.hi + step >= 0) & (p.hi + step < p.hi_n))
                def _(hi=hi, step=step):
                    self.along_hi(hi, step)(False).wait_send()

        self.local().wait()

    def steps(self):
        for m in range(1, self.p.hi_n):
            yield lambda m=m: self.pass_on(m)
        for m in range(self.p.hi_n):
            yield lambda m=m: self.take_lo(m)
        if self.mode == "quarter":
            for m in range(self.p.hi_n):
                yield lambda m=m: self.take_far(m)


def peers_of(p, seq_mates):
    out = [p.at_hi(lax.rem(p.hi + k, p.hi_n)) for k in range(1, p.hi_n)]
    out += [p.at_lo(lax.rem(p.lo + j, p.lo_n)) for j in range(1, p.lo_n)]
    return out + [p.on_seq(s) for s in seq_mates]


def gather_kernel(n, splits, chunks, *refs):
    count = len(splits)
    x_ref, srcs = refs[0], refs[1 : 1 + count]
    xg_ref, dsts = refs[1 + count], refs[2 + count : 2 + 2 * count]
    sems = refs[2 + 2 * count : 9 + 2 * count]
    xsem, xs1, xr1, xs2, xr2, xown = refs[9 + 2 * count :]
    p = Place(n)
    meet(peers_of(p, (p.mate, p.far)))
    rows = x_ref.shape[0] // chunks
    part = lambda q: pl.ds(q * rows, rows)
    sent = []
    for q in range(chunks):
        cp = rcopy(x_ref.at[part(q)], xg_ref.at[p.s, part(q)], xs1.at[q], xr1.at[q], p.on_seq(p.far))
        cp.start()
        sent.append(cp)
    gathers = [Gather(p, a, srcs[a], dsts[a], splits[a], sems) for a in range(count)]
    for g in gathers:
        g.start()
    own = pltpu.make_async_copy(x_ref, xg_ref.at[p.s], xown)
    own.start()
    cp = rcopy(x_ref, xg_ref.at[p.s], xsem.at[0], xsem.at[1], p.on_seq(p.mate))
    cp.start()
    sent.append(cp)
    for m in range(1, p.hi_n):
        for g in gathers:
            g.pass_on(m)
    for m in range(p.hi_n):
        for g in gathers:
            g.take_lo(m)
    for q in range(chunks):
        here = xg_ref.at[p.far, part(q)]
        rcopy(here, here, xs1.at[q], xr1.at[q], p.on_seq(p.far)).wait_recv()
        cp = rcopy(here, here, xs2.at[q], xr2.at[q], p.on_seq(p.mate))
        cp.start()
        sent.append(cp)
    there = xg_ref.at[p.mate]
    rcopy(there, there, xsem.at[0], xsem.at[1], p.on_seq(p.mate)).wait_recv()
    for q in range(chunks):
        there = xg_ref.at[3 - p.s, part(q)]
        rcopy(there, there, xs2.at[q], xr2.at[q], p.on_seq(p.mate)).wait_recv()
    for g in gathers:
        g.finish()
    for cp in sent:
        cp.wait_send()
    own.wait()


def gather_all(x, arrays, splits, n, cid):
    hi_n = 4 if n % 4 == 0 else 1
    chunks = 4
    count = len(arrays)
    anywhere = pl.BlockSpec(memory_space=pl.ANY)
    return pl.pallas_call(
        functools.partial(gather_kernel, n, splits, chunks),
        out_shape=[jax.ShapeDtypeStruct((4,) + x.shape, x.dtype)]
        + [jax.ShapeDtypeStruct((n,) + a.shape, a.dtype) for a in arrays],
        in_specs=[anywhere] * (1 + count),
        out_specs=[anywhere] * (1 + count),
        scratch_shapes=gather_sems(n, count)
        + [
            pltpu.SemaphoreType.DMA((2,)),
            pltpu.SemaphoreType.DMA((chunks,)),
            pltpu.SemaphoreType.DMA((chunks,)),
            pltpu.SemaphoreType.DMA((chunks,)),
            pltpu.SemaphoreType.DMA((chunks,)),
            pltpu.SemaphoreType.DMA,
        ],
        compiler_params=pltpu.CompilerParams(collective_id=cid, has_side_effects=True),
    )(x, *arrays)


CHUNK = 512
STOPS = (0, 1, 2, 3, 4, 5)


OFFSETS = (2, 1, 3, 0)
WHEN_HALF = {"lo": (1, 3, 5, 7), "owner": 14, "meet": 17}
WHEN_QUARTER = {"far": (3.1, 5.1, 6.1, 8.1), "lo": (5.2, 7.2, 8.2, 10.2), "owner": 15, "meet": 17}
WHEN_GATHER = ((1, 2, 3, 4, 6, 8, 10, 8, 9, 12, 15), (4, 8, 12, 5, 10, 14, 16))


def forward_kernel(n, heads, splits, x_ref, w_ref, b_ref, augq_ref, augk_ref, augv_ref, *refs):
    count = len(splits)
    srcs = refs[:count]
    q_ref, k_ref, v_ref, ctx_ref, lse_ref, wt_ref, merged_ref = refs[count : count + 7]
    dsts = refs[count + 7 : 2 * count + 7]
    sems = refs[2 * count + 7 : 2 * count + 14]
    xsend, xrecv, xown = refs[2 * count + 14 :]
    p = Place(n)
    h = pl.program_id(0)
    toks = x_ref.shape[0]
    part_toks = toks // 4
    gathers = [Gather(p, a, srcs[a], dsts[a], splits[a], sems) for a in range(count)]

    @pl.when(h == 0)
    def _():
        meet(peers_of(p, [lax.rem(p.s + k, 4) for k in range(1, 4)]))
        for g in gathers:
            g.start()
        wt_ref[...] = w_ref[...].T

    plan = [[] for _ in range(heads * len(STOPS))]
    for a, g in enumerate(gathers):
        for slot, step in zip(WHEN_GATHER[a], g.steps()):
            plan[slot].append(step)
    proj = mm(wt_ref[pl.ds(pl.multiple_of(h * 3 * HD, 64), 3 * HD)], x_ref[...], NT) + b_ref[0]
    scale = LOG2E / math.sqrt(HD)
    q_ref[0, :HD] = (proj[:HD] * scale).astype(bf16)
    q_ref[0, HD:] = augq_ref[...]
    k_ref[0, :HD] = proj[HD : 2 * HD].astype(bf16)
    k_ref[0, HD:] = augk_ref[...]
    v_ref[0, :HD] = proj[2 * HD :].astype(bf16)
    v_ref[0, HD:] = augv_ref[...]
    q = q_ref[0]
    top = jnp.full((1, toks), -3e38, f32)
    acc = jnp.zeros((ROWS, toks), f32)
    for j in range(toks // CHUNK):
        part = pl.ds(j * CHUNK, CHUNK)
        s = mm(k_ref[0, :, part], q, TN)
        new = jnp.maximum(top, jnp.max(s, axis=0, keepdims=True))
        probs = jnp.exp2(s - new).astype(bf16)
        acc = acc * jnp.exp2(top - new) + mm(v_ref[0, :, part], probs)
        top = new
        if j in STOPS:
            for hh in range(heads):
                steps = plan[hh * len(STOPS) + STOPS.index(j)]
                if steps:

                    @pl.when(h == hh)
                    def _(steps=steps):
                        for step in steps:
                            step()

    z = acc[HD : HD + 1]
    mine = pl.ds(pl.multiple_of(h * HD, HD), HD)
    ctx_ref[mine] = (acc[:HD] / z).astype(bf16)
    lse_ref[0] = jnp.broadcast_to(top + jnp.log2(z), (8, toks))

    def there(hh, src):
        return merged_ref.at[pl.ds(pl.multiple_of(src * heads * HD + hh * HD, HD), HD)]

    def out(hh, k):
        to = lax.rem(p.s + k, 4)
        block = ctx_ref.at[
            pl.ds(pl.multiple_of(hh * HD, HD), HD), pl.ds(pl.multiple_of(to * part_toks, 128), part_toks)
        ]
        if k == 0:
            return pltpu.make_async_copy(block, there(hh, p.s), xown.at[hh])
        return rcopy(block, there(hh, p.s), xsend.at[hh * 4 + k], xrecv.at[hh * 4 + p.s], p.on_seq(to))

    for k in (2, 3, 1, 0):
        out(h, k).start()

    @pl.when(h == heads - 1)
    def _():
        for g in gathers:
            g.finish()
        for hh in range(heads):
            for k in range(1, 4):
                frm = lax.rem(p.s + k, 4)
                rcopy(there(hh, frm), there(hh, frm), xsend.at[0], xrecv.at[hh * 4 + frm], p.on_seq(frm)).wait_recv()
                out(hh, k).wait_send()
            out(hh, 0).wait()


def attend(x, w, bias, augq, augk, augv, arrays, splits, n, cid):
    toks, width = x.shape
    cols = w.shape[1]
    heads = cols // (3 * HD)
    hi_n = 4 if n % 4 == 0 else 1
    count = len(arrays)
    one = pl.Buffered(1)
    fixed = lambda shape: pl.BlockSpec(shape, lambda h: (0, 0), pipeline_mode=one)
    anywhere = pl.BlockSpec(memory_space=pl.ANY)
    aug = fixed((ROWS - HD, toks))
    head = pl.BlockSpec((1, ROWS, toks), lambda h: (h, 0, 0))
    dma = pltpu.SemaphoreType.DMA
    return pl.pallas_call(
        functools.partial(forward_kernel, n, heads, splits),
        grid=(heads,),
        in_specs=[
            fixed(x.shape),
            fixed(w.shape),
            pl.BlockSpec((1, 3 * HD, 1), lambda h: (h, 0, 0)),
            aug,
            aug,
            aug,
        ]
        + [anywhere] * count,
        out_specs=[
            head,
            head,
            head,
            fixed((heads * HD, toks)),
            pl.BlockSpec((1, 8, toks), lambda h: (h, 0, 0)),
            fixed((cols, width)),
            anywhere,
        ]
        + [anywhere] * count,
        out_shape=[jax.ShapeDtypeStruct((heads, ROWS, toks), bf16)] * 3
        + [
            jax.ShapeDtypeStruct((heads * HD, toks), bf16),
            jax.ShapeDtypeStruct((heads, 8, toks), f32),
            jax.ShapeDtypeStruct((cols, width), bf16),
            jax.ShapeDtypeStruct((width, toks // 4), bf16),
        ]
        + [jax.ShapeDtypeStruct((n,) + a.shape, a.dtype) for a in arrays],
        scratch_shapes=gather_sems(n, count) + [dma((4 * heads,)), dma((4 * heads,)), dma((heads,))],
        compiler_params=pltpu.CompilerParams(collective_id=cid, has_side_effects=True, vmem_limit_bytes=VMEM_LIMIT),
    )(x, w, bias, augq, augk, augv, *arrays)


def three_parts(row):
    first = row.astype(bf16)
    rest = row - first.astype(f32)
    second = rest.astype(bf16)
    third = (rest - second.astype(f32)).astype(bf16)
    rows = lax.broadcasted_iota(jnp.int32, (8, row.shape[1]), 0)
    pick = lambda k, v: jnp.where(rows == k, jnp.broadcast_to(v.astype(f32), rows.shape), 0.0)
    return pick(0, first) + pick(1, second) + pick(2, third)


class VectorSum:
    def __init__(self, p, src, inbox, seqbox, sems):
        self.p, self.src, self.inbox, self.seqbox = p, src, inbox, seqbox
        self.vs, self.vr, self.ws, self.wr = sems

    @staticmethod
    def scratch(n, shape):
        dma = pltpu.SemaphoreType.DMA
        return [pltpu.VMEM((n,) + shape, f32), pltpu.VMEM((4,) + shape, f32), dma((n,)), dma((n,)), dma((4,)), dma((4,))]

    def to_shard(self, k):
        p = self.p
        return rcopy(self.src, self.inbox.at[p.i], self.vs.at[k], self.vr.at[p.i], (p.s, lax.rem(p.i + k, p.n)))

    def to_seq(self, k):
        p = self.p
        here = self.seqbox.at[p.s]
        return rcopy(here, here, self.ws.at[k], self.wr.at[p.s], p.on_seq(lax.rem(p.s + k, 4)))

    def start(self):
        for k in range(1, self.p.n):
            self.to_shard(k).start()
        self.inbox[self.p.i] = self.src[...]

    def over_seq(self):
        p = self.p
        for k in range(1, p.n):
            frm = lax.rem(p.i + k, p.n)
            there = self.inbox.at[frm]
            rcopy(there, there, self.vs.at[0], self.vr.at[frm], (p.s, frm)).wait_recv()
        self.seqbox[p.s] = jnp.sum(self.inbox[...], axis=0)
        for k in range(1, 4):
            self.to_seq(k).start()

    def finish(self):
        p = self.p
        for k in range(1, 4):
            frm = lax.rem(p.s + k, 4)
            there = self.seqbox.at[frm]
            rcopy(there, there, self.ws.at[0], self.wr.at[frm], p.on_seq(frm)).wait_recv()
            self.to_seq(k).wait_send()
        for k in range(1, p.n):
            self.to_shard(k).wait_send()


class Reduce:
    BUFS, SEMS = 5, 8

    def __init__(self, p, src, bufs, mode):
        self.p, self.src, self.mode = p, src, mode
        self.acc, self.side, self.inbox, self.far, self.out = bufs[:5]
        self.so, self.sh, self.rh, self.sl, self.rl, self.sx, self.rx, self.sf = bufs[5:]
        self.pieces = p.hi_n

    @staticmethod
    def scratch(n, hi_n, rows, w, mode):
        lo_n = n // hi_n
        dma = pltpu.SemaphoreType.DMA
        return [
            pltpu.VMEM((n, rows, w), bf16),
            pltpu.VMEM((lo_n, hi_n, rows, w), bf16),
            pltpu.VMEM((hi_n, rows, w), bf16),
            pltpu.VMEM((n if mode == "quarter" else 2, rows, w), bf16),
            pltpu.VMEM((2 if mode == "half" else 4, rows, w), bf16),
            dma((hi_n,)), dma((hi_n,)), dma((hi_n,)), dma((lo_n * hi_n,)), dma((lo_n * hi_n,)), dma((4,)), dma((4,)),
            dma((2 * hi_n,)),
        ]

    def hi_of(self, k):
        n = self.p.hi_n
        return lax.rem(self.p.hi + (OFFSETS[k] if n == 4 else k + 1), n)

    def blocks(self, ref, k):
        return ref.at[pl.ds(self.hi_of(k) * self.p.lo_n, self.p.lo_n)]

    def part(self, chip):
        return self.src.at[chip] if self.mode == "quarter" else self.src

    def load(self, k):
        src = self.part(self.p.s // 2)
        return pltpu.make_async_copy(self.blocks(src, k), self.blocks(self.acc, k), self.so.at[k])

    def swap_chips(self, k):
        p = self.p
        return rcopy(
            self.blocks(self.part(1 - p.s // 2), k), self.blocks(self.far, k), self.sf.at[k], self.sf.at[p.hi_n + k],
            p.on_seq(p.far),
        )

    def along_lo(self, k, j):
        p, d = self.p, self.hi_of(k)
        lo = lax.rem(p.lo + j, p.lo_n)
        src = self.acc if self.mode == "quarter" else self.src
        return rcopy(
            src.at[d * p.lo_n + lo], self.side.at[p.lo, d], self.sl.at[k * p.lo_n + j], self.rl.at[k * p.lo_n + p.lo],
            p.at_lo(lo),
        )

    def to_owner(self, k):
        p, d = self.p, self.hi_of(k)
        return rcopy(self.acc.at[d * p.lo_n + p.lo], self.inbox.at[p.hi], self.sh.at[k], self.rh.at[p.hi], p.at_hi(d))

    def start(self, k):
        if self.mode == "quarter":
            self.swap_chips(k).start()
        else:
            for j in range(1, self.p.lo_n):
                self.along_lo(k, j).start()
        self.load(k).start()

    def far_sum(self, k):
        if self.mode == "quarter":
            self.load(k).wait()
            self.swap_chips(k).wait_recv()
            here = self.blocks(self.acc, k)
            here[...] = (here[...].astype(f32) + self.blocks(self.far, k)[...].astype(f32)).astype(bf16)
            for j in range(1, self.p.lo_n):
                self.along_lo(k, j).start()

    def lo_sum(self, k):
        p, d = self.p, self.hi_of(k)
        if self.mode != "quarter":
            self.load(k).wait()
        mine = self.acc.at[d * p.lo_n + p.lo]
        total = mine[...].astype(f32)
        for j in range(1, p.lo_n):
            lo = lax.rem(p.lo + j, p.lo_n)
            there = self.side.at[lo, d]
            rcopy(there, there, self.sl.at[0], self.rl.at[k * p.lo_n + lo], p.at_lo(lo)).wait_recv()
            total = total + self.side[lo, d].astype(f32)
        mine[...] = total.astype(bf16)
        if k < self.pieces - 1:
            self.to_owner(k).start()

    def owner_sum(self):
        p = self.p
        total = self.acc[p.i].astype(f32)
        for k in range(self.pieces - 1):
            frm = self.hi_of(k)
            got = self.inbox.at[frm]
            rcopy(got, got, self.sh.at[0], self.rh.at[frm], p.at_hi(frm)).wait_recv()
            total = total + self.inbox[frm].astype(f32)
        if self.mode == "half":
            self.far[0] = total.astype(bf16)
            self.to_far().start()
        else:
            self.out[p.s] = total.astype(bf16)
            for k in (2, 3, 1):
                self.to_seq(k).start()

    def to_far(self):
        return rcopy(self.far.at[0], self.far.at[1], self.sx.at[0], self.rx.at[0], self.p.on_seq(self.p.far))

    def to_seq(self, k):
        p = self.p
        here = self.out.at[p.s]
        return rcopy(here, here, self.sx.at[k], self.rx.at[p.s], p.on_seq(lax.rem(p.s + k, 4)))

    def to_mate(self, core):
        here = self.out.at[core]
        return rcopy(here, here, self.sx.at[1], self.rx.at[1], self.p.on_seq(self.p.mate))

    def meet_far(self):
        if self.mode == "half":
            self.to_far().wait_recv()
            self.out[self.p.core] = (self.far[0].astype(f32) + self.far[1].astype(f32)).astype(bf16)
            self.to_mate(self.p.core).start()

    def take_all(self):
        p = self.p
        if self.mode == "half":
            self.to_mate(1 - p.core).wait_recv()
        else:
            for k in range(1, 4):
                frm = lax.rem(p.s + k, 4)
                there = self.out.at[frm]
                rcopy(there, there, self.sx.at[0], self.rx.at[frm], p.on_seq(frm)).wait_recv()

    def store(self, ref):
        w = self.out.shape[2]
        if self.mode == "half":
            for core in range(2):
                ref[:, core * w : (core + 1) * w] = self.out[core].astype(f32)
        else:
            for s in range(4):
                for c in range(w // 128):
                    at = c * 512 + (s % 2) * 256 + (s // 2) * 128
                    ref[:, at : at + 128] = self.out[s, :, c * 128 : (c + 1) * 128].astype(f32)

    def drain(self):
        p = self.p
        if self.mode == "half":
            self.to_mate(p.core).wait_send()
            self.to_far().wait_send()
        else:
            for k in range(1, 4):
                self.to_seq(k).wait_send()
        for k in range(self.pieces):
            if self.mode == "quarter":
                self.swap_chips(k).wait_send()
            for j in range(1, p.lo_n):
                self.along_lo(k, j).wait_send()
            if k < self.pieces - 1:
                self.to_owner(k).wait_send()

    def timed(self, table):
        for k in range(self.pieces):
            if self.mode == "quarter":
                yield table["far"][k % 4], lambda k=k: self.far_sum(k)
            yield table["lo"][k % 4], lambda k=k: self.lo_sum(k)
        yield table["owner"], self.owner_sum
        yield table["meet"], self.meet_far


def backward_kernel(n, heads, modes, q_ref, k_ref, v_ref, ctx_ref, lse_ref, gm_ref, vec_ref, *refs):
    count = len(modes)
    srcs, refs = refs[:count], refs[count:]
    out_ref, vsum_ref, sums, refs = refs[0], refs[1], refs[2 : 2 + count], refs[2 + count :]
    qa, da, dq, dctx, xsend, xrecv, xown = refs[:7]
    vbufs, refs = refs[7:13], refs[13:]
    each = Reduce.BUFS + Reduce.SEMS
    p = Place(n)
    h = pl.program_id(0)
    toks = q_ref.shape[2]
    part_toks = toks // 4
    vec = VectorSum(p, vec_ref, vbufs[0], vbufs[1], vbufs[2:])
    reds = [Reduce(p, srcs[a], refs[a * each : (a + 1) * each], modes[a]) for a in range(count)]

    def landing(hh, src):
        return dctx.at[pl.ds(pl.multiple_of(hh * HD, HD), HD), pl.ds(pl.multiple_of(src * part_toks, 128), part_toks)]

    def give(hh, k):
        to = lax.rem(p.s + k, 4)
        block = gm_ref.at[pl.ds(pl.multiple_of(to * heads * HD + hh * HD, HD), HD)]
        if k == 0:
            return pltpu.make_async_copy(block, landing(hh, p.s), xown.at[hh])
        return rcopy(block, landing(hh, p.s), xsend.at[hh * 4 + k], xrecv.at[hh * 4 + p.s], p.on_seq(to))

    @pl.when(h == 0)
    def _():
        meet([(p.s, lax.rem(p.i + k, n)) for k in range(1, n)] + [p.on_seq(lax.rem(p.s + k, 4)) for k in range(1, 4)])
        for hh in range(heads):
            for k in (2, 3, 1, 0):
                give(hh, k).start()
        for k in range(p.hi_n):
            for r in reds:
                r.start(k)
        vec.start()

    for k in range(1, 4):
        frm = lax.rem(p.s + k, 4)
        rcopy(landing(h, frm), landing(h, frm), xsend.at[0], xrecv.at[h * 4 + frm], p.on_seq(frm)).wait_recv()
    give(h, 0).wait()

    slots = heads * len(STOPS)
    plan = [[] for _ in range(slots)]
    for r in reds:
        for slot, step in r.timed(WHEN_QUARTER if r.mode == "quarter" else WHEN_HALF):
            plan[min(int(slot), slots - 1)].append((slot, step))
    plan = [[step for _, step in sorted(todo, key=lambda x: x[0])] for todo in plan]
    plan[slots // 2].append(vec.over_seq)

    qa[:HD] = q_ref[h, :HD]
    mask = q_ref[h, HD : HD + 8].astype(f32)
    zero = jnp.zeros((8, toks), f32)
    qa[HD:] = jnp.concatenate([mask, three_parts(-lse_ref[h, :1])], axis=0).astype(bf16)
    grad = dctx[pl.ds(pl.multiple_of(h * HD, HD), HD)]
    delta = jnp.sum(grad.astype(f32) * ctx_ref[pl.ds(pl.multiple_of(h * HD, HD), HD)].astype(f32), axis=0, keepdims=True)
    da[:HD] = grad
    da[HD:] = jnp.concatenate([three_parts(-delta), zero], axis=0).astype(bf16)
    q, do = qa[...], da[...]
    for j in range(toks // CHUNK):
        part = pl.ds(j * CHUNK, CHUNK)
        k = k_ref[h, :, part]
        probs = jnp.exp2(mm(k, q, TN))
        gprobs = mm(v_ref[h, :, part], do, TN)
        ds = (probs * gprobs).astype(bf16)
        probs = probs.astype(bf16)
        out_ref[h, 2 * HD :, part] = mm(do[:HD], probs, NT).astype(bf16)
        out_ref[h, HD : 2 * HD, part] = (mm(q[:HD], ds, NT) * LN2).astype(bf16)
        dq_part = mm(k[:HD], ds)
        dq[...] = dq_part if j == 0 else dq[...] + dq_part
        if j in STOPS:
            for hh in range(heads):
                todo = plan[hh * len(STOPS) + STOPS.index(j)]
                if todo:

                    @pl.when(h == hh)
                    def _(todo=todo):
                        for step in todo:
                            step()

    out_ref[h, :HD] = (dq[...] * (1.0 / math.sqrt(HD))).astype(bf16)

    @pl.when(h == heads - 1)
    def _():
        vec.finish()
        vbox = vec.seqbox
        vsum_ref[...] = (vbox[0] + vbox[1]) + (vbox[2] + vbox[3])
        for a, r in enumerate(reds):
            r.take_all()
            r.store(sums[a])
        for r in reds:
            r.drain()
        for hh in range(heads):
            for k in range(1, 4):
                give(hh, k).wait_send()


def attend_back(q, k, v, ctx, lse, gm, vec, arrays, modes, n, cid):
    heads, _, toks = q.shape
    hi_n = 4 if n % 4 == 0 else 1
    count = len(arrays)
    one = pl.Buffered(1)
    fixed = lambda shape: pl.BlockSpec(shape, lambda h: (0,) * len(shape), pipeline_mode=one)
    anywhere = pl.BlockSpec(memory_space=pl.ANY)
    dma = pltpu.SemaphoreType.DMA
    sums = [(a.shape[-2], a.shape[-1] * (4 if mode == "quarter" else 2)) for a, mode in zip(arrays, modes)]
    scratch = [
        pltpu.VMEM((ROWS, toks), bf16),
        pltpu.VMEM((ROWS, toks), bf16),
        pltpu.VMEM((HD, toks), f32),
        pltpu.VMEM((heads * HD, toks), bf16),
        dma((4 * heads,)), dma((4 * heads,)), dma((heads,)),
    ] + VectorSum.scratch(n, vec.shape)
    for a, mode in zip(arrays, modes):
        scratch += Reduce.scratch(n, hi_n, a.shape[-2], a.shape[-1], mode)
    return pl.pallas_call(
        functools.partial(backward_kernel, n, heads, modes),
        grid=(heads,),
        in_specs=[
            fixed(q.shape),
            fixed(k.shape),
            fixed(v.shape),
            fixed(ctx.shape),
            fixed(lse.shape),
            anywhere,
            fixed(vec.shape),
        ]
        + [anywhere] * count,
        out_specs=[fixed((heads, 3 * HD, toks)), fixed(vec.shape)]
        + [fixed(s) for s in sums],
        out_shape=[jax.ShapeDtypeStruct((heads, 3 * HD, toks), bf16), jax.ShapeDtypeStruct(vec.shape, f32)]
        + [jax.ShapeDtypeStruct(s, f32) for s in sums],
        scratch_shapes=scratch,
        compiler_params=pltpu.CompilerParams(collective_id=cid, has_side_effects=True, vmem_limit_bytes=VMEM_LIMIT),
    )(q, k, v, ctx, lse, gm, vec, *arrays)


def finish_kernel(
    n, d_ref, x_ref, wt_ref, resid_ref, out_ref, dw_ref, brow_ref, part, near, give, far, dw, brow, sems, *refs
):
    p = Place(n)
    vec = VectorSum(p, brow, refs[0], refs[1], refs[2:6])
    rows, cols = dw_ref.shape[0], wt_ref.shape[0]
    red = Reduce(p, dw, refs[6:], "whole")
    meet([(p.s, lax.rem(p.i + k, n)) for k in range(1, n)] + [p.on_seq(lax.rem(p.s + k, 4)) for k in range(1, 4)])
    toks = resid_ref.shape[0]
    beyond = lax.rem(p.mate + 2, 4)

    def token_part(s):
        return mm(d_ref[:, pl.ds(pl.multiple_of(s * toks, 128), toks)], wt_ref[...], TN)

    def to_mate(slot):
        return rcopy(part.at[slot], near.at[slot], sems.at[slot], sems.at[2 + slot], p.on_seq(p.mate))

    def to_far():
        return rcopy(give, far, sems.at[4], sems.at[5], p.on_seq(p.far))

    part[0] = token_part(beyond).astype(bf16)
    to_mate(0).start()
    grad = mm(d_ref[...], x_ref[...]).T.astype(bf16)
    dw[...] = grad.reshape(dw.shape)
    for k in range(red.pieces):
        red.start(k)
    mine = token_part(p.far)
    to_mate(0).wait_recv()
    give[...] = (mine + near[0].astype(f32)).astype(bf16)
    to_far().start()
    part[1] = token_part(p.mate).astype(bf16)
    to_mate(1).start()
    brow[...] = mm(jnp.ones((8, d_ref.shape[1]), bf16), d_ref[...], NT)
    vec.start()
    total = resid_ref[...] + token_part(p.s)
    for k in range(red.pieces):
        red.lo_sum(k)
    red.owner_sum()
    to_mate(1).wait_recv()
    total = total + near[1].astype(f32)
    vec.over_seq()
    to_far().wait_recv()
    out_ref[...] = (total + far[...].astype(f32)).astype(bf16)
    red.take_all()
    heads = cols // (3 * HD)
    width = 4 * heads * HD
    for s in range(4):
        blk = red.out[s].astype(f32)
        for h in range(heads):
            for w in range(3):
                at = w * width + (s * heads + h) * HD
                dw_ref[:, at : at + HD] = blk[:, (3 * h + w) * HD : (3 * h + w + 1) * HD]
    vec.finish()
    brow_ref[...] = vec.seqbox[:, 0]
    red.drain()
    to_mate(0).wait_send()
    to_mate(1).wait_send()
    to_far().wait_send()


def finish(d, x, w_t, resid, n, cid):
    toks, width = resid.shape
    cols = w_t.shape[0]
    rows = width // n
    hi_n = 4 if n % 4 == 0 else 1
    vm = pl.BlockSpec(memory_space=pltpu.VMEM)
    dma = pltpu.SemaphoreType.DMA
    return pl.pallas_call(
        functools.partial(finish_kernel, n),
        out_shape=[
            jax.ShapeDtypeStruct((toks, width), bf16),
            jax.ShapeDtypeStruct((rows, 4 * cols), f32),
            jax.ShapeDtypeStruct((4, cols), f32),
        ],
        in_specs=[vm] * 4,
        out_specs=[vm] * 3,
        scratch_shapes=[
            pltpu.VMEM((2, toks, width), bf16),
            pltpu.VMEM((2, toks, width), bf16),
            pltpu.VMEM((toks, width), bf16),
            pltpu.VMEM((toks, width), bf16),
            pltpu.VMEM((n, rows, cols), bf16),
            pltpu.VMEM((8, cols), f32),
            dma((6,)),
        ]
        + VectorSum.scratch(n, (8, cols))
        + Reduce.scratch(n, hi_n, rows, cols, "whole"),
        compiler_params=pltpu.CompilerParams(collective_id=cid, has_side_effects=True, vmem_limit_bytes=VMEM_LIMIT),
    )(d, x, w_t, resid)


def norm_parts(value):
    centred = value - jnp.mean(value, axis=-1, keepdims=True)
    inv = lax.rsqrt(jnp.mean(centred * centred, axis=-1, keepdims=True) + epsilon)
    return centred * inv, inv


def norm_back(grad_hat, hat, inv):
    mean_grad = jnp.mean(grad_hat, axis=-1, keepdims=True)
    mean_both = jnp.mean(grad_hat * hat, axis=-1, keepdims=True)
    return inv * (grad_hat - mean_grad - hat * mean_both)


def ffn_kernel(
    n, chunks, scale_ref, merged_ref, tok_ref, teach_ref, live_ref, wo_ref, vec_ref, bup_ref, up0_ref, up1_ref, down_ref,
    result_ref, resid_ref, gm_ref, dout_ref, dup_ref, ddown_ref, dvec_ref, dbup_ref,
    low, hat, inv, acc, grad_low, act, slope, down_own, down_got, up_got, out_own, out_got, send, recv,
):
    i = pl.program_id(0)
    p = Place(n)
    row = lambda k: vec_ref[k : k + 1]
    col_sum = lambda v: jnp.sum(v, axis=0, keepdims=True)
    c = jnp.where(i < chunks, i, 2 * chunks - 1 - i)

    def swap(own, got, at):
        return rcopy(own.at[:, half(own.shape[1], 1 - p.core)], got, send.at[at], recv.at[at], p.on_seq(p.mate))

    def swap_down(k):
        return swap(down_own.at[k], down_got.at[k], k)

    def swap_up(k):
        return swap(act.at[k], up_got.at[k], chunks + k)

    def swap_out():
        return swap(out_own, out_got, 2 * chunks)

    def total(own, got):
        return own[:, half(own.shape[1], p.core)].astype(f32) + got[...].astype(f32)

    def settle(k):
        swap_down(k).wait_recv()
        rows = down_own.shape[1]
        ddown_ref[pl.ds(pl.multiple_of(k * rows, 16), rows)] = total(down_own.at[k], down_got.at[k]).astype(bf16)
        swap_up(k).wait_recv()
        both = total(act.at[k], up_got.at[k]).astype(bf16)
        cols = both.shape[1] // 2
        for chip in range(2):
            dup_ref[chip, :, pl.ds(pl.multiple_of(k * cols, 128), cols)] = both[:, chip * cols : (chip + 1) * cols]

    @pl.when(i == 0)
    def _():
        meet([p.on_seq(p.mate)])
        branch = mm(merged_ref[...], wo_ref[...], TN) + row(0)
        h, r = norm_parts(tok_ref[...].astype(f32) + branch)
        hat[...] = h
        inv[...] = r
        normed = h * row(1) + row(2)
        low[...] = normed.astype(bf16)
        acc[...] = normed + row(3)

    def forward(up_ref):
        pre = mm(low[...], up_ref[...]) + bup_ref[pl.ds(c, 1)]
        cdf = 0.5 + 0.5 * lax.erf(pre * math.sqrt(0.5))
        pdf = jnp.exp(-0.5 * pre * pre) * (1.0 / math.sqrt(2.0 * math.pi))
        a = (pre * cdf).astype(bf16)
        act[c] = a
        slope[c] = cdf + pre * pdf
        acc[...] += mm(a, down_ref[...])

    def choose(body):
        pl.when(c < chunks // 2)(lambda: body(up0_ref))
        pl.when(c >= chunks // 2)(lambda: body(up1_ref))

    @pl.when(i < chunks)
    def _():
        choose(forward)

    @pl.when(i == chunks - 1)
    def _():
        h, r = norm_parts(acc[...])
        result = h * row(4) + row(5)
        result_ref[...] = result.astype(bf16)
        grad = (result - teach_ref[...].astype(f32)) * (live_ref[...] * scale_ref[0])
        two = norm_back(grad * row(4), h, r)
        g = two.astype(bf16)
        grad_low[...] = g
        acc[...] = two
        dvec_ref[...] = jnp.zeros_like(dvec_ref)
        dvec_ref[3:4] = col_sum(g.astype(f32))
        dvec_ref[4:5] = col_sum(grad * h)
        dvec_ref[5:6] = col_sum(grad)

    def backward(up_ref):
        g = grad_low[...]
        grad_pre = (mm(g, down_ref[...], NT) * slope[c]).astype(bf16)
        dbup_ref[pl.ds(c, 1)] = col_sum(grad_pre.astype(f32))
        down_own[c] = mm(act[c], g, TN).astype(bf16)
        swap_down(c).start()
        act[c] = mm(low[...], grad_pre, TN).astype(bf16)
        swap_up(c).start()
        acc[...] += mm(grad_pre, up_ref[...], NT)

    @pl.when(i >= chunks)
    def _():
        choose(backward)

    @pl.when(i > chunks)
    def _():
        settle(c + 1)

    @pl.when(i == 2 * chunks - 1)
    def _():
        grad = acc[...]
        h = hat[...]
        one = norm_back(grad * row(1), h, inv[...])
        resid_ref[...] = one
        g = one.astype(bf16)
        out_own[...] = mm(merged_ref[...], g).astype(bf16)
        swap_out().start()
        dvec_ref[0:1] = col_sum(g.astype(f32))
        dvec_ref[1:2] = col_sum(grad * h)
        dvec_ref[2:3] = col_sum(grad)
        gm_ref[...] = mm(wo_ref[...], g, NT).astype(bf16)
        settle(0)
        swap_out().wait_recv()
        dout_ref[...] = total(out_own, out_got).astype(bf16)
        swap_out().wait_send()
        for k in range(chunks):
            swap_down(k).wait_send()
            swap_up(k).wait_send()


def feed_forward(scale, merged, tokens, teacher, live, w_out, vec, b_up, w_up0, w_up1, w_down, n, cid):
    toks, width = tokens.shape
    hidden = w_down.shape[0]
    size = 512
    chunks = hidden // size
    one = pl.Buffered(1)
    fixed = lambda shape: pl.BlockSpec(shape, lambda i: (0,) * len(shape), pipeline_mode=one)
    turn = lambda i: jnp.where(i < chunks, i, 2 * chunks - 1 - i)
    dma = pltpu.SemaphoreType.DMA
    outs = [
        jax.ShapeDtypeStruct((toks, width), bf16),
        jax.ShapeDtypeStruct((toks, width), f32),
        jax.ShapeDtypeStruct(merged.shape, bf16),
        jax.ShapeDtypeStruct((width, width // 2), bf16),
        jax.ShapeDtypeStruct((2, width, hidden // 4), bf16),
        jax.ShapeDtypeStruct((hidden, width // 2), bf16),
        jax.ShapeDtypeStruct((8, width), f32),
        jax.ShapeDtypeStruct((chunks, size), f32),
    ]
    return pl.pallas_call(
        functools.partial(ffn_kernel, n, chunks),
        grid=(2 * chunks,),
        in_specs=[
            pl.BlockSpec(memory_space=pltpu.SMEM),
            fixed(merged.shape), fixed(tokens.shape), fixed(teacher.shape), fixed(live.shape), fixed(w_out.shape),
            fixed(vec.shape), fixed(b_up.shape),
            pl.BlockSpec((width, size), lambda i: (0, jnp.minimum(turn(i), chunks // 2 - 1))),
            pl.BlockSpec((width, size), lambda i: (0, jnp.maximum(turn(i) - chunks // 2, 0))),
            pl.BlockSpec((size, width), lambda i: (turn(i), 0)),
        ],
        out_specs=[fixed(o.shape) for o in outs],
        out_shape=outs,
        scratch_shapes=[
            pltpu.VMEM((toks, width), bf16),
            pltpu.VMEM((toks, width), f32),
            pltpu.VMEM((toks, 1), f32),
            pltpu.VMEM((toks, width), f32),
            pltpu.VMEM((toks, width), bf16),
            pltpu.VMEM((chunks, toks, size), bf16),
            pltpu.VMEM((chunks, toks, size), f32),
            pltpu.VMEM((chunks, size, width), bf16),
            pltpu.VMEM((chunks, size, width // 2), bf16),
            pltpu.VMEM((chunks, width, size // 2), bf16),
            pltpu.VMEM((width, width), bf16),
            pltpu.VMEM((width, width // 2), bf16),
            dma((2 * chunks + 1,)),
            dma((2 * chunks + 1,)),
        ],
        compiler_params=pltpu.CompilerParams(collective_id=cid, has_side_effects=True, vmem_limit_bytes=VMEM_LIMIT),
    )(scale, merged, tokens, teacher, live, w_out, vec, b_up, w_up0, w_up1, w_down)


def on_device(
    inputs, teacher, seq_lengths, w_qkv, q_bias, v_bias, w_out, out_bias, attn_gain, attn_shift, w_up, up_bias,
    w_down, down_bias, ffn_gain, ffn_shift,
):
    n = lax.axis_size("shard")
    s = lax.axis_index("seq")
    i = lax.axis_index("shard")
    toks, width = inputs.shape[1:]
    group = 4 * toks
    hidden = w_up.shape[1]
    rows = w_qkv.shape[0]
    heads = HEADS // 4
    folds = hidden // width
    tokens = inputs[0]
    lens = seq_lengths[0]
    ends = [lens[0], lens[0] + lens[1], lens[0] + lens[1] + lens[2]]

    own_w = lax.dynamic_index_in_dim(w_qkv.reshape(rows, 3, 4, heads, HD), s, 2, keepdims=False)
    own_w = jnp.transpose(own_w, (0, 2, 1, 3)).reshape(rows, heads * 3 * HD)
    live = jnp.stack([ends[2] // 64, lax.rem(ends[2], 64)]).astype(bf16)
    small = jnp.concatenate(
        [out_bias[None], attn_gain[None], attn_shift[None], down_bias[None], ffn_gain[None], ffn_shift[None], q_bias[None],
         v_bias[None], up_bias.reshape(folds, rows), jnp.broadcast_to(live[:, None], (2, rows))], axis=0
    )
    small = jnp.pad(small, ((0, 16 - small.shape[0]), (0, -rows % 128)))
    cut = hidden // 2
    xg, wq_g, small_g, wo_g, up0_g = gather_all(
        tokens, (own_w, small, w_out, w_up[:, :cut]), ("whole", "whole", "half", "half"), n, 1
    )
    x_all = xg.reshape(group, width)
    wq = wq_g.reshape(width, heads * 3 * HD)
    vecs = jnp.transpose(small_g[:, :, :rows], (1, 0, 2)).astype(f32)
    eight = vecs[:8].reshape(8, width)
    b_up = jnp.transpose(vecs[8 : 8 + folds], (1, 0, 2)).reshape(hidden // 512, 512)
    live_total = jnp.sum(vecs[8 + folds, :, 0]) * 64.0 + jnp.sum(vecs[9 + folds, :, 0])

    own_q, own_v = [
        lax.dynamic_slice_in_dim(eight[r], s * heads * HD, heads * HD).reshape(heads, 1, HD) for r in (6, 7)
    ]
    bias = jnp.concatenate([own_q, jnp.zeros_like(own_q), own_v], axis=1).reshape(heads, 3 * HD, 1)

    pos = lax.broadcasted_iota(jnp.int32, (16, group), 1)
    row = lax.broadcasted_iota(jnp.int32, (16, group), 0)
    seg = sum((pos >= e).astype(jnp.int32) for e in ends)
    augq = jnp.where((row < 4) & (seg != row), neg_large, 0.0).astype(bf16)
    augk = jnp.where((row < 4) & (seg == row) | (row >= 8) & (row < 11), 1.0, 0.0).astype(bf16)
    augv = jnp.where(row < 3, 1.0, 0.0).astype(bf16)

    q, k, v, ctx, lse, w_t, merged, up1_g, down_g = attend(
        x_all, wq, bias, augq, augk, augv, (w_up[:, cut:], w_down), ("quarter", "half"), n, 2
    )
    own_pos = s * toks + lax.iota(jnp.int32, toks)
    live_rows = (own_pos < ends[2]).astype(f32)[:, None]
    scale = (float(group * n) / live_total).reshape(1)
    result, grad_resid_one, gm, d_out, d_up, d_down, dvec, d_bup = feed_forward(
        scale, merged, tokens, teacher[0], live_rows, wo_g.reshape(width, width), eight, b_up,
        up0_g.reshape(width, cut), up1_g.reshape(width, cut),        down_g.reshape(hidden, width), n, 5,
    )
    vec = jnp.concatenate([dvec, d_bup.reshape(folds, width), jnp.zeros((8 - folds, width), f32)], axis=0)
    dqkv, vsum, d_up_r, d_down_r, d_out_r = attend_back(
        q, k, v, ctx, lse, gm, vec,
        (d_up.reshape(2, n, rows, hidden // 4), d_down.reshape(n, hidden // n, width // 2), d_out.reshape(n, rows, width // 2)),
        ("quarter", "half", "half"), n, 3,
    )
    grad_in, d_qkv, brow = finish(dqkv.reshape(heads * 3 * HD, group), x_all, w_t, grad_resid_one, n, 4)

    brow = jnp.transpose(brow.reshape(4, heads, 3, HD), (2, 0, 1, 3)).reshape(3, width)
    take = lambda v: lax.dynamic_slice_in_dim(v, i * rows, rows)
    vs = [take(vsum[r]) for r in range(6)]
    d_bup = lax.dynamic_slice_in_dim(vsum[8 : 8 + folds].reshape(hidden), i * (hidden // n), hidden // n)
    return (
        result[None], grad_in[None], d_qkv, take(brow[0]), take(brow[2]), d_out_r, vs[0], vs[1], vs[2], d_up_r, d_bup,
        d_down_r, vs[3], vs[4], vs[5],
    )


def solution(mesh):
    tokens, matrix, vector = P("shard", "seq", None), P("shard", None), P("shard")
    in_specs = (tokens, tokens, matrix, matrix, vector, vector, matrix, vector, vector, vector, matrix, vector, matrix,
                vector, vector, vector)
    out_specs = (tokens, tokens, matrix, vector, vector, matrix, vector, vector, vector, matrix, vector, matrix, vector,
                 vector, vector)
    return jax.shard_map(on_device, mesh=mesh, in_specs=in_specs, out_specs=out_specs, check_vma=False)
```

```python
import functools
import math

import jax
import jax.numpy as jnp
from jax import lax
from jax.experimental import pallas as pl
from jax.experimental.pallas import tpu as pltpu
from jax.sharding import PartitionSpec as P

HEADS = 12
HD = 64
ROWS = 80
MESH = pl.DeviceIdType.MESH
f32 = jnp.float32
bf16 = jnp.bfloat16
epsilon = 1e-12
neg_large = -1e30
LOG2E = math.log2(math.e)
LN2 = math.log(2.0)
VMEM_LIMIT = 60 << 20

NN = (((1,), (0,)), ((), ()))
NT = (((1,), (1,)), ((), ()))
TN = (((0,), (0,)), ((), ()))


def mm(left, right, dims=NN):
    return lax.dot_general(left, right, dims, preferred_element_type=f32)


class Place:
    def __init__(self, n):
        self.n = n
        self.hi_n = 4 if n % 4 == 0 else 1
        self.lo_n = n // self.hi_n
        self.s = lax.axis_index("seq")
        self.i = lax.axis_index("shard")
        self.core = lax.rem(self.s, 2)
        self.mate = self.s + 1 - 2 * self.core
        self.far = lax.rem(self.s + 2, 4)
        self.hi = self.i // self.lo_n
        self.lo = lax.rem(self.i, self.lo_n)

    def at_hi(self, hi):
        return (self.s, hi * self.lo_n + self.lo)

    def at_lo(self, lo):
        return (self.s, self.hi * self.lo_n + lo)

    def on_seq(self, s):
        return (s, self.i)


def meet(peers):
    bar = pltpu.get_barrier_semaphore()
    for peer in peers:
        pl.semaphore_signal(bar, inc=1, device_id=peer, device_id_type=MESH)
    pl.semaphore_wait(bar, len(peers))


def rcopy(src, dst, send, recv, peer):
    return pltpu.make_async_remote_copy(
        src_ref=src, dst_ref=dst, send_sem=send, recv_sem=recv, device_id=peer, device_id_type=MESH
    )


def half(cols, core):
    return pl.ds(pl.multiple_of(core * (cols // 2), 128), cols // 2)


def gather_sems(n, count):
    dma = pltpu.SemaphoreType.DMA
    return [dma((count, 2 * n)), dma((count, n)), dma((count, n)), dma((count, n)), dma((count, 3 * n)), dma((count, 3 * n)), dma((count,))]


class Gather:
    def __init__(self, place, idx, src, dst, mode, sems):
        self.p, self.a, self.src, self.dst, self.mode = place, idx, src, dst, mode
        self.s1, self.r1, self.s2, self.r2, self.s3, self.r3, self.own = sems

    def view(self, ref, core, chip=None):
        cols = ref.shape[-1]
        if self.mode == "whole":
            return ref
        if self.mode == "half" or chip is None:
            return ref.at[:, half(cols, core)]
        at = core * (cols // 2) + chip * (cols // 4)
        return ref.at[:, pl.ds(pl.multiple_of(at, 128), cols // 4)]

    def mine(self, ref):
        return self.view(ref, self.p.core, self.p.s // 2)

    def local(self):
        return pltpu.make_async_copy(self.src, self.dst.at[self.p.i], self.own.at[self.a])

    def along_hi(self, hi, step):
        p, a = self.p, self.a
        blk = hi * p.lo_n + p.lo
        there = self.mine(self.dst.at[blk])
        return lambda own: rcopy(
            self.mine(self.src) if own else there, there, self.s1.at[a, blk if step > 0 else p.n + blk], self.r1.at[a, blk],
            p.at_hi(p.hi + step),
        )

    def along_lo(self, hi, j, own=False):
        p, a = self.p, self.a
        blk = hi * p.lo_n + p.lo
        there = self.mine(self.dst.at[blk])
        return rcopy(
            self.mine(self.src) if own else there, there, self.s2.at[a, hi * p.lo_n + j], self.r2.at[a, blk],
            p.at_lo(lax.rem(p.lo + j, p.lo_n)),
        )

    def to_far(self, blk, chip):
        p, a = self.p, self.a
        here = self.view(self.dst.at[blk], p.core, chip)
        return rcopy(here, here, self.s3.at[a, 2 * p.n + blk], self.r3.at[a, 2 * p.n + blk], p.on_seq(p.far))

    def to_mate(self, blk, core, chip=None):
        p, a = self.p, self.a
        here = self.view(self.dst.at[blk], core, chip)
        at = blk if chip is None else chip * p.n + blk
        return rcopy(here, here, self.s3.at[a, at], self.r3.at[a, at], p.on_seq(p.mate))

    def here(self, blk):
        if self.mode == "half":
            self.to_mate(blk, self.p.core).start()
        if self.mode == "quarter":
            self.to_far(blk, self.p.s // 2).start()
            self.to_mate(blk, self.p.core, self.p.s // 2).start()

    def start(self):
        p = self.p
        self.local().start()
        for step in (1, -1):

            @pl.when((p.hi + step >= 0) & (p.hi + step < p.hi_n))
            def _(step=step):
                self.along_hi(p.hi, step)(True).start()

        for j in range(1, p.lo_n):
            self.along_lo(p.hi, j, True).start()

    def come(self, m, step):
        p = self.p
        hi = p.hi - step * m

        @pl.when((hi >= 0) & (hi < p.hi_n))
        def _():
            blk = hi * p.lo_n + p.lo
            there = self.mine(self.dst.at[blk])
            rcopy(there, there, self.s1.at[self.a, 0], self.r1.at[self.a, blk], p.at_hi(p.hi)).wait_recv()

            @pl.when((p.hi + step >= 0) & (p.hi + step < p.hi_n))
            def _():
                self.along_hi(hi, step)(False).start()

            for j in range(1, p.lo_n):
                self.along_lo(hi, j).start()
            self.here(blk)

    def pass_on(self, m):
        self.come(m, 1)
        self.come(m, -1)

    def both_ways(self, m, body):
        p = self.p
        if m == 0:
            body(p.hi)
            return
        for step in (1, -1):
            hi = p.hi - step * m
            pl.when((hi >= 0) & (hi < p.hi_n))(lambda hi=hi: body(hi))

    def take_lo(self, m):
        p, a = self.p, self.a

        def body(hi):
            for j in range(1, p.lo_n):
                lo = lax.rem(p.lo + j, p.lo_n)
                blk = hi * p.lo_n + lo
                there = self.mine(self.dst.at[blk])
                rcopy(there, there, self.s2.at[a, 0], self.r2.at[a, blk], p.at_lo(lo)).wait_recv()
                self.here(blk)

        self.both_ways(m, body)

    def take_far(self, m):
        p = self.p

        def body(hi):
            for j in range(p.lo_n):
                if m or j:
                    blk = hi * p.lo_n + lax.rem(p.lo + j, p.lo_n)
                    self.to_far(blk, 1 - p.s // 2).wait_recv()
                    self.to_mate(blk, p.core, 1 - p.s // 2).start()

        if self.mode == "quarter":
            self.both_ways(m, body)

    def finish(self):
        p = self.p
        for m in range(p.hi_n):
            hi = lax.rem(p.hi + m, p.hi_n)
            for j in range(p.lo_n):
                blk = hi * p.lo_n + lax.rem(p.lo + j, p.lo_n)
                if self.mode != "whole" and (m or j):
                    for chip in (None,) if self.mode == "half" else (0, 1):
                        self.to_mate(blk, 1 - p.core, chip).wait_recv()
                        self.to_mate(blk, p.core, chip).wait_send()
                    if self.mode == "quarter":
                        self.to_far(blk, p.s // 2).wait_send()
                if j:
                    self.along_lo(hi, j).wait_send()
        for step in (1, -1):
            for m in range(p.hi_n):
                hi = p.hi - step * m

                @pl.when((hi >= 0) & (hi < p.hi_n) & (p.hi + step >= 0) & (p.hi + step < p.hi_n))
                def _(hi=hi, step=step):
                    self.along_hi(hi, step)(False).wait_send()

        self.local().wait()

    def steps(self):
        for m in range(1, self.p.hi_n):
            yield lambda m=m: self.pass_on(m)
        for m in range(self.p.hi_n):
            yield lambda m=m: self.take_lo(m)
        if self.mode == "quarter":
            for m in range(self.p.hi_n):
                yield lambda m=m: self.take_far(m)


def peers_of(p, seq_mates):
    out = [p.at_hi(lax.rem(p.hi + k, p.hi_n)) for k in range(1, p.hi_n)]
    out += [p.at_lo(lax.rem(p.lo + j, p.lo_n)) for j in range(1, p.lo_n)]
    return out + [p.on_seq(s) for s in seq_mates]


def gather_kernel(n, splits, chunks, *refs):
    count = len(splits)
    x_ref, srcs = refs[0], refs[1 : 1 + count]
    xg_ref, dsts = refs[1 + count], refs[2 + count : 2 + 2 * count]
    sems = refs[2 + 2 * count : 9 + 2 * count]
    xsem, xs1, xr1, xs2, xr2, xown = refs[9 + 2 * count :]
    p = Place(n)
    meet(peers_of(p, (p.mate, p.far)))
    rows = x_ref.shape[0] // chunks
    part = lambda q: pl.ds(q * rows, rows)
    sent = []
    for q in range(chunks):
        cp = rcopy(x_ref.at[part(q)], xg_ref.at[p.s, part(q)], xs1.at[q], xr1.at[q], p.on_seq(p.far))
        cp.start()
        sent.append(cp)
    gathers = [Gather(p, a, srcs[a], dsts[a], splits[a], sems) for a in range(count)]
    for g in gathers:
        g.start()
    own = pltpu.make_async_copy(x_ref, xg_ref.at[p.s], xown)
    own.start()
    cp = rcopy(x_ref, xg_ref.at[p.s], xsem.at[0], xsem.at[1], p.on_seq(p.mate))
    cp.start()
    sent.append(cp)
    for m in range(1, p.hi_n):
        for g in gathers:
            g.pass_on(m)
    for m in range(p.hi_n):
        for g in gathers:
            g.take_lo(m)
    for q in range(chunks):
        here = xg_ref.at[p.far, part(q)]
        rcopy(here, here, xs1.at[q], xr1.at[q], p.on_seq(p.far)).wait_recv()
        cp = rcopy(here, here, xs2.at[q], xr2.at[q], p.on_seq(p.mate))
        cp.start()
        sent.append(cp)
    there = xg_ref.at[p.mate]
    rcopy(there, there, xsem.at[0], xsem.at[1], p.on_seq(p.mate)).wait_recv()
    for q in range(chunks):
        there = xg_ref.at[3 - p.s, part(q)]
        rcopy(there, there, xs2.at[q], xr2.at[q], p.on_seq(p.mate)).wait_recv()
    for g in gathers:
        g.finish()
    for cp in sent:
        cp.wait_send()
    own.wait()


def gather_all(x, arrays, splits, n, cid):
    hi_n = 4 if n % 4 == 0 else 1
    chunks = 4
    count = len(arrays)
    anywhere = pl.BlockSpec(memory_space=pl.ANY)
    return pl.pallas_call(
        functools.partial(gather_kernel, n, splits, chunks),
        out_shape=[jax.ShapeDtypeStruct((4,) + x.shape, x.dtype)]
        + [jax.ShapeDtypeStruct((n,) + a.shape, a.dtype) for a in arrays],
        in_specs=[pl.BlockSpec(memory_space=pltpu.VMEM)] * (1 + count),
        out_specs=[anywhere] * (1 + count),
        scratch_shapes=gather_sems(n, count)
        + [
            pltpu.SemaphoreType.DMA((2,)),
            pltpu.SemaphoreType.DMA((chunks,)),
            pltpu.SemaphoreType.DMA((chunks,)),
            pltpu.SemaphoreType.DMA((chunks,)),
            pltpu.SemaphoreType.DMA((chunks,)),
            pltpu.SemaphoreType.DMA,
        ],
        compiler_params=pltpu.CompilerParams(collective_id=cid, has_side_effects=True),
    )(x, *arrays)


CHUNK = 512
BACK_CHUNK = 256
STOPS = (0, 1, 2, 3, 4, 5)


OFFSETS = (2, 1, 3, 0)
WHEN_HALF = {"lo": (1, 3, 5, 7), "owner": 14, "meet": 17}
WHEN_QUARTER = {"far": (3.1, 5.1, 6.1, 8.1), "lo": (5.2, 7.2, 8.2, 10.2), "owner": 15, "meet": 17}
WHEN_GATHER = (
    (1, 2, 4, 2, 3, 5, 7),
    (2, 6, 10, 4, 8, 12, 15),
    (3, 7, 11, 8, 10, 12, 14, 12, 14, 15, 17),
)


def forward_kernel(n, heads, splits, x_ref, w_ref, b_ref, augq_ref, augk_ref, augv_ref, *refs):
    count = len(splits)
    srcs = refs[:count]
    q_ref, k_ref, v_ref, ctx_ref, lse_ref, wt_ref, merged_ref = refs[count : count + 7]
    dsts = refs[count + 7 : 2 * count + 7]
    sems = refs[2 * count + 7 : 2 * count + 14]
    xsend, xrecv, xown = refs[2 * count + 14 :]
    p = Place(n)
    h = pl.program_id(0)
    toks = x_ref.shape[0]
    part_toks = toks // 4
    gathers = [Gather(p, a, srcs[a], dsts[a], splits[a], sems) for a in range(count)]

    @pl.when(h == 0)
    def _():
        meet(peers_of(p, [lax.rem(p.s + k, 4) for k in range(1, 4)]))
        for g in gathers:
            g.start()
        wt_ref[...] = w_ref[...].T

    plan = [[] for _ in range(heads * len(STOPS))]
    for a, g in enumerate(gathers):
        for slot, step in zip(WHEN_GATHER[a], g.steps()):
            plan[slot].append(step)
    proj = mm(wt_ref[pl.ds(pl.multiple_of(h * 3 * HD, 64), 3 * HD)], x_ref[...], NT) + b_ref[0]
    scale = LOG2E / math.sqrt(HD)
    q_ref[0, :HD] = (proj[:HD] * scale).astype(bf16)
    q_ref[0, HD:] = augq_ref[...]
    k_ref[0, :HD] = proj[HD : 2 * HD].astype(bf16)
    k_ref[0, HD:] = augk_ref[...]
    v_ref[0, :HD] = proj[2 * HD :].astype(bf16)
    v_ref[0, HD:] = augv_ref[...]
    q = q_ref[0]
    top = jnp.full((1, toks), -3e38, f32)
    acc = jnp.zeros((ROWS, toks), f32)
    for j in range(toks // CHUNK):
        part = pl.ds(j * CHUNK, CHUNK)
        s = mm(k_ref[0, :, part], q, TN)
        new = jnp.maximum(top, jnp.max(s, axis=0, keepdims=True))
        probs = jnp.exp2(s - new).astype(bf16)
        acc = acc * jnp.exp2(top - new) + mm(v_ref[0, :, part], probs)
        top = new
        if j in STOPS:
            for hh in range(heads):
                steps = plan[hh * len(STOPS) + STOPS.index(j)]
                if steps:

                    @pl.when(h == hh)
                    def _(steps=steps):
                        for step in steps:
                            step()

    z = acc[HD : HD + 1]
    mine = pl.ds(pl.multiple_of(h * HD, HD), HD)
    ctx_ref[mine] = (acc[:HD] / z).astype(bf16)
    lse_ref[0] = jnp.broadcast_to(top + jnp.log2(z), (8, toks))

    def there(hh, src):
        return merged_ref.at[pl.ds(pl.multiple_of(src * heads * HD + hh * HD, HD), HD)]

    def out(hh, k):
        to = lax.rem(p.s + k, 4)
        block = ctx_ref.at[
            pl.ds(pl.multiple_of(hh * HD, HD), HD), pl.ds(pl.multiple_of(to * part_toks, 128), part_toks)
        ]
        if k == 0:
            return pltpu.make_async_copy(block, there(hh, p.s), xown.at[hh])
        return rcopy(block, there(hh, p.s), xsend.at[hh * 4 + k], xrecv.at[hh * 4 + p.s], p.on_seq(to))

    for k in (2, 3, 1, 0):
        out(h, k).start()

    @pl.when(h == heads - 1)
    def _():
        for g in gathers:
            g.finish()
        for hh in range(heads):
            for k in range(1, 4):
                frm = lax.rem(p.s + k, 4)
                rcopy(there(hh, frm), there(hh, frm), xsend.at[0], xrecv.at[hh * 4 + frm], p.on_seq(frm)).wait_recv()
                out(hh, k).wait_send()
            out(hh, 0).wait()


def attend(x, w, bias, augq, augk, augv, arrays, splits, n, cid):
    toks, width = x.shape
    cols = w.shape[1]
    heads = cols // (3 * HD)
    hi_n = 4 if n % 4 == 0 else 1
    count = len(arrays)
    one = pl.Buffered(1)
    fixed = lambda shape: pl.BlockSpec(shape, lambda h: (0, 0), pipeline_mode=one)
    anywhere = pl.BlockSpec(memory_space=pl.ANY)
    aug = fixed((ROWS - HD, toks))
    head = pl.BlockSpec((1, ROWS, toks), lambda h: (h, 0, 0))
    dma = pltpu.SemaphoreType.DMA
    return pl.pallas_call(
        functools.partial(forward_kernel, n, heads, splits),
        grid=(heads,),
        in_specs=[
            fixed(x.shape),
            fixed(w.shape),
            pl.BlockSpec((1, 3 * HD, 1), lambda h: (h, 0, 0)),
            aug,
            aug,
            aug,
        ]
        + [fixed(a.shape) for a in arrays],
        out_specs=[
            head,
            head,
            head,
            fixed((heads * HD, toks)),
            pl.BlockSpec((1, 8, toks), lambda h: (h, 0, 0)),
            fixed((cols, width)),
            anywhere,
        ]
        + [anywhere] * count,
        out_shape=[jax.ShapeDtypeStruct((heads, ROWS, toks), bf16)] * 3
        + [
            jax.ShapeDtypeStruct((heads * HD, toks), bf16),
            jax.ShapeDtypeStruct((heads, 8, toks), f32),
            jax.ShapeDtypeStruct((cols, width), bf16),
            jax.ShapeDtypeStruct((width, toks // 4), bf16),
        ]
        + [jax.ShapeDtypeStruct((n,) + a.shape, a.dtype) for a in arrays],
        scratch_shapes=gather_sems(n, count) + [dma((4 * heads,)), dma((4 * heads,)), dma((heads,))],
        compiler_params=pltpu.CompilerParams(collective_id=cid, has_side_effects=True, vmem_limit_bytes=VMEM_LIMIT),
    )(x, w, bias, augq, augk, augv, *arrays)


def three_parts(row):
    first = row.astype(bf16)
    rest = row - first.astype(f32)
    second = rest.astype(bf16)
    third = (rest - second.astype(f32)).astype(bf16)
    rows = lax.broadcasted_iota(jnp.int32, (8, row.shape[1]), 0)
    pick = lambda k, v: jnp.where(rows == k, jnp.broadcast_to(v.astype(f32), rows.shape), 0.0)
    return pick(0, first) + pick(1, second) + pick(2, third)


class VectorSum:
    def __init__(self, p, src, inbox, seqbox, sems):
        self.p, self.src, self.inbox, self.seqbox = p, src, inbox, seqbox
        self.vs, self.vr, self.ws, self.wr = sems

    @staticmethod
    def scratch(n, shape):
        dma = pltpu.SemaphoreType.DMA
        return [pltpu.VMEM((n,) + shape, f32), pltpu.VMEM((4,) + shape, f32), dma((n,)), dma((n,)), dma((4,)), dma((4,))]

    def to_shard(self, k):
        p = self.p
        return rcopy(self.src, self.inbox.at[p.i], self.vs.at[k], self.vr.at[p.i], (p.s, lax.rem(p.i + k, p.n)))

    def to_seq(self, k):
        p = self.p
        here = self.seqbox.at[p.s]
        return rcopy(here, here, self.ws.at[k], self.wr.at[p.s], p.on_seq(lax.rem(p.s + k, 4)))

    def start(self):
        for k in range(1, self.p.n):
            self.to_shard(k).start()
        self.inbox[self.p.i] = self.src[...]

    def over_seq(self):
        p = self.p
        for k in range(1, p.n):
            frm = lax.rem(p.i + k, p.n)
            there = self.inbox.at[frm]
            rcopy(there, there, self.vs.at[0], self.vr.at[frm], (p.s, frm)).wait_recv()
        self.seqbox[p.s] = jnp.sum(self.inbox[...], axis=0)
        for k in range(1, 4):
            self.to_seq(k).start()

    def finish(self):
        p = self.p
        for k in range(1, 4):
            frm = lax.rem(p.s + k, 4)
            there = self.seqbox.at[frm]
            rcopy(there, there, self.ws.at[0], self.wr.at[frm], p.on_seq(frm)).wait_recv()
            self.to_seq(k).wait_send()
        for k in range(1, p.n):
            self.to_shard(k).wait_send()


class Reduce:
    BUFS, SEMS = 5, 8

    def __init__(self, p, src, bufs, mode):
        self.p, self.src, self.mode = p, src, mode
        self.acc, self.side, self.inbox, self.far, self.out = bufs[:5]
        self.so, self.sh, self.rh, self.sl, self.rl, self.sx, self.rx, self.sf = bufs[5:]
        self.pieces = p.hi_n

    @staticmethod
    def scratch(n, hi_n, rows, w, mode):
        lo_n = n // hi_n
        dma = pltpu.SemaphoreType.DMA
        return [
            pltpu.VMEM((n, rows, w), bf16),
            pltpu.VMEM((lo_n, hi_n, rows, w), bf16),
            pltpu.VMEM((hi_n, rows, w), bf16),
            pltpu.VMEM((n if mode == "quarter" else 2, rows, w), bf16),
            pltpu.VMEM((2 if mode == "half" else 4, rows, w), bf16),
            dma((hi_n,)), dma((hi_n,)), dma((hi_n,)), dma((lo_n * hi_n,)), dma((lo_n * hi_n,)), dma((4,)), dma((4,)),
            dma((2 * hi_n,)),
        ]

    def hi_of(self, k):
        n = self.p.hi_n
        return lax.rem(self.p.hi + (OFFSETS[k] if n == 4 else k + 1), n)

    def blocks(self, ref, k):
        return ref.at[pl.ds(self.hi_of(k) * self.p.lo_n, self.p.lo_n)]

    def part(self, chip):
        return self.src.at[chip] if self.mode == "quarter" else self.src

    def load(self, k):
        src = self.part(self.p.s // 2)
        return pltpu.make_async_copy(self.blocks(src, k), self.blocks(self.acc, k), self.so.at[k])

    def swap_chips(self, k):
        p = self.p
        return rcopy(
            self.blocks(self.part(1 - p.s // 2), k), self.blocks(self.far, k), self.sf.at[k], self.sf.at[p.hi_n + k],
            p.on_seq(p.far),
        )

    def along_lo(self, k, j):
        p, d = self.p, self.hi_of(k)
        lo = lax.rem(p.lo + j, p.lo_n)
        src = self.acc if self.mode == "quarter" else self.src
        return rcopy(
            src.at[d * p.lo_n + lo], self.side.at[p.lo, d], self.sl.at[k * p.lo_n + j], self.rl.at[k * p.lo_n + p.lo],
            p.at_lo(lo),
        )

    def to_owner(self, k):
        p, d = self.p, self.hi_of(k)
        return rcopy(self.acc.at[d * p.lo_n + p.lo], self.inbox.at[p.hi], self.sh.at[k], self.rh.at[p.hi], p.at_hi(d))

    def start(self, k):
        if self.mode == "quarter":
            self.swap_chips(k).start()
        else:
            for j in range(1, self.p.lo_n):
                self.along_lo(k, j).start()
        self.load(k).start()

    def far_sum(self, k):
        if self.mode == "quarter":
            self.load(k).wait()
            self.swap_chips(k).wait_recv()
            here = self.blocks(self.acc, k)
            here[...] = here[...] + self.blocks(self.far, k)[...]
            for j in range(1, self.p.lo_n):
                self.along_lo(k, j).start()

    def lo_sum(self, k):
        p, d = self.p, self.hi_of(k)
        if self.mode != "quarter":
            self.load(k).wait()
        mine = self.acc.at[d * p.lo_n + p.lo]
        total = mine[...].astype(f32)
        for j in range(1, p.lo_n):
            lo = lax.rem(p.lo + j, p.lo_n)
            there = self.side.at[lo, d]
            rcopy(there, there, self.sl.at[0], self.rl.at[k * p.lo_n + lo], p.at_lo(lo)).wait_recv()
            total = total + self.side[lo, d].astype(f32)
        mine[...] = total.astype(bf16)
        if k < self.pieces - 1:
            self.to_owner(k).start()

    def owner_sum(self):
        p = self.p
        total = self.acc[p.i].astype(f32)
        for k in range(self.pieces - 1):
            frm = self.hi_of(k)
            got = self.inbox.at[frm]
            rcopy(got, got, self.sh.at[0], self.rh.at[frm], p.at_hi(frm)).wait_recv()
            total = total + self.inbox[frm].astype(f32)
        if self.mode == "half":
            self.far[0] = total.astype(bf16)
            self.to_far().start()
        else:
            self.out[p.s] = total.astype(bf16)
            for k in (2, 3, 1):
                self.to_seq(k).start()

    def to_far(self):
        return rcopy(self.far.at[0], self.far.at[1], self.sx.at[0], self.rx.at[0], self.p.on_seq(self.p.far))

    def to_seq(self, k):
        p = self.p
        here = self.out.at[p.s]
        return rcopy(here, here, self.sx.at[k], self.rx.at[p.s], p.on_seq(lax.rem(p.s + k, 4)))

    def to_mate(self, core):
        here = self.out.at[core]
        return rcopy(here, here, self.sx.at[1], self.rx.at[1], self.p.on_seq(self.p.mate))

    def meet_far(self):
        if self.mode == "half":
            self.to_far().wait_recv()
            self.out[self.p.core] = self.far[0] + self.far[1]
            self.to_mate(self.p.core).start()

    def take_all(self):
        p = self.p
        if self.mode == "half":
            self.to_mate(1 - p.core).wait_recv()
        else:
            for k in range(1, 4):
                frm = lax.rem(p.s + k, 4)
                there = self.out.at[frm]
                rcopy(there, there, self.sx.at[0], self.rx.at[frm], p.on_seq(frm)).wait_recv()

    def store(self, ref):
        w = self.out.shape[2]
        if self.mode == "half":
            for core in range(2):
                ref[:, core * w : (core + 1) * w] = self.out[core].astype(f32)
        else:
            for s in range(4):
                for c in range(w // 128):
                    at = c * 512 + (s % 2) * 256 + (s // 2) * 128
                    ref[:, at : at + 128] = self.out[s, :, c * 128 : (c + 1) * 128].astype(f32)

    def drain(self):
        p = self.p
        if self.mode == "half":
            self.to_mate(p.core).wait_send()
            self.to_far().wait_send()
        else:
            for k in range(1, 4):
                self.to_seq(k).wait_send()
        for k in range(self.pieces):
            if self.mode == "quarter":
                self.swap_chips(k).wait_send()
            for j in range(1, p.lo_n):
                self.along_lo(k, j).wait_send()
            if k < self.pieces - 1:
                self.to_owner(k).wait_send()

    def timed(self, table):
        for k in range(self.pieces):
            if self.mode == "quarter":
                yield table["far"][k % 4], lambda k=k: self.far_sum(k)
            yield table["lo"][k % 4], lambda k=k: self.lo_sum(k)
        yield table["owner"], self.owner_sum
        yield table["meet"], self.meet_far


class Direct:
    REFS = 6

    def __init__(self, p, src, bufs):
        self.p, self.src = p, src
        self.inbox, self.out, self.vs, self.vr, self.ws, self.wr = bufs

    @staticmethod
    def scratch(n, rows, cols):
        dma = pltpu.SemaphoreType.DMA
        return [pltpu.VMEM((n, rows, cols), bf16), pltpu.VMEM((4, rows, cols), bf16), dma((n,)), dma((n,)), dma((4,)), dma((4,))]

    def to_shard(self, k):
        p = self.p
        to = lax.rem(p.i + k, p.n)
        return rcopy(self.src.at[to], self.inbox.at[p.i], self.vs.at[k], self.vr.at[p.i], (p.s, to))

    def to_seq(self, k):
        p = self.p
        here = self.out.at[p.s]
        return rcopy(here, here, self.ws.at[k], self.wr.at[p.s], p.on_seq(lax.rem(p.s + k, 4)))

    def start(self):
        for k in range(1, self.p.n):
            self.to_shard(k).start()

    def owner_sum(self):
        p = self.p
        total = self.src[p.i].astype(f32)
        for k in range(1, p.n):
            frm = lax.rem(p.i + k, p.n)
            there = self.inbox.at[frm]
            rcopy(there, there, self.vs.at[0], self.vr.at[frm], (p.s, frm)).wait_recv()
            total = total + self.inbox[frm].astype(f32)
        self.out[p.s] = total.astype(bf16)
        for k in (2, 3, 1):
            self.to_seq(k).start()

    def take_all(self):
        p = self.p
        for k in range(1, 4):
            frm = lax.rem(p.s + k, 4)
            there = self.out.at[frm]
            rcopy(there, there, self.ws.at[0], self.wr.at[frm], p.on_seq(frm)).wait_recv()

    def drain(self):
        for k in range(1, 4):
            self.to_seq(k).wait_send()
        for k in range(1, self.p.n):
            self.to_shard(k).wait_send()


def backward_kernel(
    n, heads, modes, q_ref, k_ref, v_ref, ctx_ref, lse_ref, gm_ref, x_hbm, wall_hbm, resid_ref, vec_ref, *refs
):
    count = len(modes)
    srcs, refs = refs[:count], refs[count:]
    grad_ref, dw_ref, brow_ref, vsum_ref, sums, refs = refs[0], refs[1], refs[2], refs[3], refs[4 : 4 + count], refs[4 + count :]
    qa, da, dq, dctx, dqkv, dw, got, total, x_ref, wall_ref, xsend, xrecv, xown, gsend, grecv, late_sem = refs[:16]
    vec_bufs, refs = refs[16:22], refs[22:]
    each = Reduce.BUFS + Reduce.SEMS
    p = Place(n)
    h = pl.program_id(0)
    toks = q_ref.shape[2]
    part_toks = toks // 4
    vec = VectorSum(p, vec_ref, vec_bufs[0], vec_bufs[1], vec_bufs[2:])
    reds = [Reduce(p, srcs[a], refs[a * each : (a + 1) * each], modes[a]) for a in range(count)]
    refs = refs[count * each :]
    heads_red = [Direct(p, dw.at[hh], refs[hh * Direct.REFS : (hh + 1) * Direct.REFS]) for hh in range(heads)]

    def tok_part(s):
        return pl.ds(pl.multiple_of(s * part_toks, 128), part_toks)

    def landing(hh, src):
        return dctx.at[pl.ds(pl.multiple_of(hh * HD, HD), HD), tok_part(src)]

    def give(hh, k):
        to = lax.rem(p.s + k, 4)
        block = gm_ref.at[pl.ds(pl.multiple_of(to * heads * HD + hh * HD, HD), HD)]
        if k == 0:
            return pltpu.make_async_copy(block, landing(hh, p.s), xown.at[hh])
        return rcopy(block, landing(hh, p.s), xsend.at[hh * 4 + k], xrecv.at[hh * 4 + p.s], p.on_seq(to))

    def give_keys(hh, to):
        return rcopy(
            dqkv.at[hh, HD:, tok_part(to)], got.at[hh, p.s, HD:], gsend.at[hh * 8 + to], grecv.at[hh * 8 + p.s], p.on_seq(to)
        )

    def give_queries(hh, k):
        to = lax.rem(p.s + k, 4)
        return rcopy(
            dqkv.at[hh, :HD, tok_part(to)], got.at[hh, p.s, :HD], gsend.at[hh * 8 + 4 + k], grecv.at[hh * 8 + 4 + p.s],
            p.on_seq(to),
        )

    def add_tokens(hh):
        for k in range(1, 4):
            frm = lax.rem(p.s + k, 4)
            for there, at in ((got.at[hh, frm, HD:], frm), (got.at[hh, frm, :HD], 4 + frm)):
                rcopy(there, there, gsend.at[0], grecv.at[hh * 8 + at], p.on_seq(frm)).wait_recv()
        flat = lambda v: v.reshape(4 * 3 * HD, v.shape[2])
        total[...] += mm(flat(got[hh]), flat(wall_ref[:, hh * 3 * HD : (hh + 1) * 3 * HD]), TN)

    late = [
        pltpu.make_async_copy(src, dst, late_sem.at[k])
        for k, (src, dst) in enumerate(((resid_ref, total), (x_hbm, x_ref), (wall_hbm, wall_ref)))
    ]

    @pl.when(h == 0)
    def _():
        meet([(p.s, lax.rem(p.i + k, n)) for k in range(1, n)] + [p.on_seq(lax.rem(p.s + k, 4)) for k in range(1, 4)])
        for hh in range(heads):
            for k in (2, 3, 1, 0):
                give(hh, k).start()
        for k in range(p.hi_n):
            for r in reds:
                r.start(k)
        vec.start()
        for cp in late:
            cp.start()

    for k in range(1, 4):
        frm = lax.rem(p.s + k, 4)
        rcopy(landing(h, frm), landing(h, frm), xsend.at[0], xrecv.at[h * 4 + frm], p.on_seq(frm)).wait_recv()
    give(h, 0).wait()

    per = len(STOPS)
    slots = heads * per
    plan = [[] for _ in range(slots)]
    for r in reds:
        for slot, step in r.timed(WHEN_QUARTER if r.mode == "quarter" else WHEN_HALF):
            plan[min(int(slot), slots - 1)].append((slot, step))
    for hh in range(heads - 1):
        plan[per * (hh + 1) + 3].append((per * (hh + 1) + 3.9, heads_red[hh].owner_sum))
        plan[per * (hh + 1) + 4].append((per * (hh + 1) + 4.9, lambda hh=hh: add_tokens(hh)))
    plan[1].extend((1.9, cp.wait) for cp in late)
    plan[slots // 2].append((slots // 2 + 0.8, vec.over_seq))
    plan = [[step for _, step in sorted(todo, key=lambda x: x[0])] for todo in plan]

    qa[:HD] = q_ref[h, :HD]
    mask = q_ref[h, HD : HD + 8].astype(f32)
    zero = jnp.zeros((8, toks), f32)
    qa[HD:] = jnp.concatenate([mask, three_parts(-lse_ref[h, :1])], axis=0).astype(bf16)
    mine = pl.ds(pl.multiple_of(h * HD, HD), HD)
    grad = dctx[mine]
    delta = jnp.sum(grad.astype(f32) * ctx_ref[mine].astype(f32), axis=0, keepdims=True)
    da[:HD] = grad
    da[HD:] = jnp.concatenate([three_parts(-delta), zero], axis=0).astype(bf16)
    q, do = qa[...], da[...]
    q_rows, do_rows = q.T, do.T
    for j in range(toks // BACK_CHUNK):
        part = pl.ds(j * BACK_CHUNK, BACK_CHUNK)
        k = k_ref[h, :, part]
        probs = jnp.exp2(mm(k, q, TN))
        gprobs = mm(v_ref[h, :, part], do, TN)
        ds = (probs * gprobs).astype(bf16)
        probs = probs.astype(bf16)
        dqkv[h, 2 * HD :, part] = mm(probs, do_rows).T[:HD].astype(bf16)
        dqkv[h, HD : 2 * HD, part] = (mm(ds, q_rows).T[:HD] * LN2).astype(bf16)
        dq_part = mm(k[:HD], ds)
        dq[...] = dq_part if j == 0 else dq[...] + dq_part
        ends = (j + 1) * BACK_CHUNK
        if ends % CHUNK == 0 and ends // CHUNK - 1 in STOPS:
            for hh in range(heads):
                todo = plan[hh * per + STOPS.index(ends // CHUNK - 1)]
                if todo:

                    @pl.when(h == hh)
                    def _(todo=todo):
                        for step in todo:
                            step()

        for to in range(4):
            if ends - BACK_CHUNK < (to + 1) * part_toks <= ends:

                @pl.when(p.s != to)
                def _(to=to):
                    give_keys(h, to).start()

    dqkv[h, :HD] = (dq[...] * (1.0 / math.sqrt(HD))).astype(bf16)
    for k in (2, 3, 1):
        give_queries(h, k).start()
    n_rows = dw_ref.shape[0]
    dw[h, :, :n_rows] = mm(dqkv[h], x_ref[...]).T.astype(bf16).reshape(n, n_rows, 3 * HD)
    sums_row = mm(jnp.ones((16, toks), bf16), dqkv[h], NT)
    first = sums_row.astype(bf16).astype(f32)
    pick = lax.broadcasted_iota(jnp.int32, sums_row.shape, 0)
    parts = jnp.where(pick == 0, first, jnp.where(pick == 1, sums_row - first, 0.0)).astype(bf16)
    dw[h, :, dw.shape[2] - 16 :] = jnp.broadcast_to(parts, (n, 16, 3 * HD))
    for hh in range(heads):

        @pl.when(h == hh)
        def _(hh=hh):
            heads_red[hh].start()

    got[h, p.s] = dqkv[h, :, tok_part(p.s)]

    @pl.when(h == heads - 1)
    def _():
        last = heads_red[heads - 1]
        vec.finish()
        vbox = vec.seqbox
        vsum_ref[...] = (vbox[0] + vbox[1]) + (vbox[2] + vbox[3])
        for a, r in enumerate(reds):
            r.take_all()
            r.store(sums[a])
        last.owner_sum()
        add_tokens(heads - 1)
        grad_ref[...] = total[...].astype(bf16)
        width = 4 * heads * HD
        for hh, r in enumerate(heads_red):
            r.take_all()
            for s in range(4):
                blk = r.out[s].astype(f32)
                top = blk.shape[0] - 16
                row = blk[top : top + 1] + blk[top + 1 : top + 2]
                for w in range(3):
                    at = (s * heads + hh) * HD
                    dw_ref[:, w * width + at : w * width + at + HD] = blk[:n_rows, w * HD : (w + 1) * HD]
                    brow_ref[w : w + 1, at : at + HD] = row[:, w * HD : (w + 1) * HD]
        for r in reds + heads_red:
            r.drain()
        for hh in range(heads):
            for k in range(1, 4):
                give(hh, k).wait_send()
                give_keys(hh, lax.rem(p.s + k, 4)).wait_send()
                give_queries(hh, k).wait_send()


def attend_back(q, k, v, ctx, lse, gm, x, wall, resid, vec, arrays, modes, n, cid):
    heads, _, toks = q.shape
    hi_n = 4 if n % 4 == 0 else 1
    count = len(arrays)
    one = pl.Buffered(1)
    fixed = lambda shape: pl.BlockSpec(shape, lambda h: (0,) * len(shape), pipeline_mode=one)
    anywhere = pl.BlockSpec(memory_space=pl.ANY)
    dma = pltpu.SemaphoreType.DMA
    sums = [(a.shape[-2], a.shape[-1] * (4 if mode == "quarter" else 2)) for a, mode in zip(arrays, modes)]
    part_toks, width = resid.shape
    cols = heads * 3 * HD
    rows = width // n
    high = -(-rows // 16) * 16 + 16
    scratch = [
        pltpu.VMEM((ROWS, toks), bf16),
        pltpu.VMEM((ROWS, toks), bf16),
        pltpu.VMEM((HD, toks), f32),
        pltpu.VMEM((heads * HD, toks), bf16),
        pltpu.VMEM((heads, 3 * HD, toks), bf16),
        pltpu.VMEM((heads, n, high, 3 * HD), bf16),
        pltpu.VMEM((heads, 4, 3 * HD, part_toks), bf16),
        pltpu.VMEM(resid.shape, f32),
        pltpu.VMEM(x.shape, bf16),
        pltpu.VMEM(wall.shape, bf16),
        dma((4 * heads,)), dma((4 * heads,)), dma((heads,)), dma((8 * heads,)), dma((8 * heads,)), dma((3,)),
    ] + VectorSum.scratch(n, vec.shape)
    for a, mode in zip(arrays, modes):
        scratch += Reduce.scratch(n, hi_n, a.shape[-2], a.shape[-1], mode)
    for _ in range(heads):
        scratch += Direct.scratch(n, high, 3 * HD)
    outs = [
        jax.ShapeDtypeStruct(resid.shape, bf16),
        jax.ShapeDtypeStruct((rows, 4 * cols), f32),
        jax.ShapeDtypeStruct((3, width), f32),
        jax.ShapeDtypeStruct(vec.shape, f32),
    ] + [jax.ShapeDtypeStruct(s, f32) for s in sums]
    return pl.pallas_call(
        functools.partial(backward_kernel, n, heads, modes),
        grid=(heads,),
        in_specs=[fixed(a.shape) for a in (q, k, v, ctx, lse)] + [anywhere] * 4 + [fixed(vec.shape)] + [anywhere] * count,
        out_specs=[fixed(o.shape) for o in outs],
        out_shape=outs,
        scratch_shapes=scratch,
        compiler_params=pltpu.CompilerParams(collective_id=cid, has_side_effects=True, vmem_limit_bytes=VMEM_LIMIT),
    )(q, k, v, ctx, lse, gm, x, wall, resid, vec, *arrays)


def norm_parts(value):
    centred = value - jnp.mean(value, axis=-1, keepdims=True)
    inv = lax.rsqrt(jnp.mean(centred * centred, axis=-1, keepdims=True) + epsilon)
    return centred * inv, inv


def norm_back(grad_hat, hat, inv):
    mean_grad = jnp.mean(grad_hat, axis=-1, keepdims=True)
    mean_both = jnp.mean(grad_hat * hat, axis=-1, keepdims=True)
    return inv * (grad_hat - mean_grad - hat * mean_both)


def ffn_kernel(
    n, chunks, scale_ref, merged_ref, tok_ref, teach_ref, live_ref, wo_ref, vec_ref, bup_ref, up_ref, down_ref,
    wt_ref, result_ref, resid_ref, gm_ref, dout_ref, dup_ref, ddown_ref, dvec_ref, dbup_ref, wall_ref,
    low, hat, inv, acc, grad_low, act, slope, down_own, down_got, up_got, out_own, out_got, send, recv, wsend, wrecv,
):
    i = pl.program_id(0)
    p = Place(n)
    row = lambda k: vec_ref[k : k + 1]
    col_sum = lambda v: jnp.sum(v, axis=0, keepdims=True)
    c = jnp.where(i < chunks, i, 2 * chunks - 1 - i)

    def swap(own, got, at):
        return rcopy(own.at[:, half(own.shape[1], 1 - p.core)], got, send.at[at], recv.at[at], p.on_seq(p.mate))

    def swap_down(k):
        return swap(down_own.at[k], down_got.at[k], k)

    def swap_up(k):
        return swap(act.at[k], up_got.at[k], chunks + k)

    def swap_out():
        return swap(out_own, out_got, 2 * chunks)

    def total(own, got):
        return own[:, half(own.shape[1], p.core)].astype(f32) + got[...].astype(f32)

    def settle(k):
        swap_down(k).wait_recv()
        rows = down_own.shape[1]
        ddown_ref[pl.ds(pl.multiple_of(k * rows, 16), rows)] = total(down_own.at[k], down_got.at[k]).astype(bf16)
        swap_up(k).wait_recv()
        both = total(act.at[k], up_got.at[k]).astype(bf16)
        cols = both.shape[1] // 2
        for chip in range(2):
            dup_ref[chip, :, pl.ds(pl.multiple_of(k * cols, 128), cols)] = both[:, chip * cols : (chip + 1) * cols]

    def share(k):
        if k == 0:
            return pltpu.make_async_copy(wt_ref, wall_ref.at[p.s], wsend.at[0])
        return rcopy(wt_ref, wall_ref.at[p.s], wsend.at[k], wrecv.at[p.s], p.on_seq(lax.rem(p.s + k, 4)))

    @pl.when(i == 0)
    def _():
        meet([p.on_seq(lax.rem(p.s + k, 4)) for k in range(1, 4)])
        for k in (2, 3, 1, 0):
            share(k).start()
        branch = mm(merged_ref[...], wo_ref[...], TN) + row(0)
        h, r = norm_parts(tok_ref[...].astype(f32) + branch)
        hat[...] = h
        inv[...] = r
        normed = h * row(1) + row(2)
        low[...] = normed.astype(bf16)
        acc[...] = normed + row(3)

    @pl.when(i < chunks)
    def _():
        pre = mm(low[...], up_ref[...]) + bup_ref[pl.ds(c, 1)]
        cdf = 0.5 + 0.5 * lax.erf(pre * math.sqrt(0.5))
        pdf = jnp.exp(-0.5 * pre * pre) * (1.0 / math.sqrt(2.0 * math.pi))
        a = (pre * cdf).astype(bf16)
        act[c] = a
        slope[c] = cdf + pre * pdf
        acc[...] += mm(a, down_ref[...])

    @pl.when(i == chunks - 1)
    def _():
        h, r = norm_parts(acc[...])
        result = h * row(4) + row(5)
        result_ref[...] = result.astype(bf16)
        grad = (result - teach_ref[...].astype(f32)) * (live_ref[...] * scale_ref[0])
        two = norm_back(grad * row(4), h, r)
        g = two.astype(bf16)
        grad_low[...] = g
        acc[...] = two
        dvec_ref[...] = jnp.zeros_like(dvec_ref)
        dvec_ref[3:4] = col_sum(g.astype(f32))
        dvec_ref[4:5] = col_sum(grad * h)
        dvec_ref[5:6] = col_sum(grad)

    @pl.when(i >= chunks)
    def _():
        g = grad_low[...]
        grad_pre = (mm(g, down_ref[...], NT) * slope[c]).astype(bf16)
        dbup_ref[pl.ds(c, 1)] = col_sum(grad_pre.astype(f32))
        down_own[c] = mm(act[c], g, TN).astype(bf16)
        swap_down(c).start()
        act[c] = mm(low[...], grad_pre, TN).astype(bf16)
        swap_up(c).start()
        acc[...] += mm(grad_pre, up_ref[...], NT)

    @pl.when(i > chunks)
    def _():
        settle(c + 1)

    @pl.when(i == 2 * chunks - 1)
    def _():
        grad = acc[...]
        h = hat[...]
        one = norm_back(grad * row(1), h, inv[...])
        resid_ref[...] = one
        g = one.astype(bf16)
        out_own[...] = mm(merged_ref[...], g).astype(bf16)
        swap_out().start()
        dvec_ref[0:1] = col_sum(g.astype(f32))
        dvec_ref[1:2] = col_sum(grad * h)
        dvec_ref[2:3] = col_sum(grad)
        gm_ref[...] = mm(wo_ref[...], g, NT).astype(bf16)
        settle(0)
        swap_out().wait_recv()
        dout_ref[...] = total(out_own, out_got).astype(bf16)
        swap_out().wait_send()
        for k in range(chunks):
            swap_down(k).wait_send()
            swap_up(k).wait_send()
        for k in range(1, 4):
            frm = lax.rem(p.s + k, 4)
            there = wall_ref.at[frm]
            rcopy(there, there, wsend.at[0], wrecv.at[frm], p.on_seq(frm)).wait_recv()
            share(k).wait_send()
        share(0).wait()


def feed_forward(scale, merged, tokens, teacher, live, w_out, vec, b_up, w_up, w_down, w_t, n, cid):
    toks, width = tokens.shape
    hidden = w_down.shape[0]
    size = 512
    chunks = hidden // size
    one = pl.Buffered(1)
    fixed = lambda shape: pl.BlockSpec(shape, lambda i: (0,) * len(shape), pipeline_mode=one)
    anywhere = pl.BlockSpec(memory_space=pl.ANY)
    turn = lambda i: jnp.where(i < chunks, i, 2 * chunks - 1 - i)
    dma = pltpu.SemaphoreType.DMA
    outs = [
        jax.ShapeDtypeStruct((toks, width), bf16),
        jax.ShapeDtypeStruct((toks, width), f32),
        jax.ShapeDtypeStruct(merged.shape, bf16),
        jax.ShapeDtypeStruct((width, width // 2), bf16),
        jax.ShapeDtypeStruct((2, width, hidden // 4), bf16),
        jax.ShapeDtypeStruct((hidden, width // 2), bf16),
        jax.ShapeDtypeStruct((8, width), f32),
        jax.ShapeDtypeStruct((chunks, size), f32),
    ]
    return pl.pallas_call(
        functools.partial(ffn_kernel, n, chunks),
        grid=(2 * chunks,),
        in_specs=[
            pl.BlockSpec(memory_space=pltpu.SMEM),
            fixed(merged.shape), fixed(tokens.shape), fixed(teacher.shape), fixed(live.shape), fixed(w_out.shape),
            fixed(vec.shape), fixed(b_up.shape),
            pl.BlockSpec((width, size), lambda i: (0, turn(i))),
            pl.BlockSpec((size, width), lambda i: (turn(i), 0)),
            anywhere,
        ],
        out_specs=[fixed(o.shape) for o in outs] + [anywhere],
        out_shape=outs + [jax.ShapeDtypeStruct((4,) + w_t.shape, bf16)],
        scratch_shapes=[
            pltpu.VMEM((toks, width), bf16),
            pltpu.VMEM((toks, width), f32),
            pltpu.VMEM((toks, 1), f32),
            pltpu.VMEM((toks, width), f32),
            pltpu.VMEM((toks, width), bf16),
            pltpu.VMEM((chunks, toks, size), bf16),
            pltpu.VMEM((chunks, toks, size), f32),
            pltpu.VMEM((chunks, size, width), bf16),
            pltpu.VMEM((chunks, size, width // 2), bf16),
            pltpu.VMEM((chunks, width, size // 2), bf16),
            pltpu.VMEM((width, width), bf16),
            pltpu.VMEM((width, width // 2), bf16),
            dma((2 * chunks + 1,)),
            dma((2 * chunks + 1,)),
            dma((4,)),
            dma((4,)),
        ],
        compiler_params=pltpu.CompilerParams(collective_id=cid, has_side_effects=True, vmem_limit_bytes=VMEM_LIMIT),
    )(scale, merged, tokens, teacher, live, w_out, vec, b_up, w_up, w_down, w_t)


def deliver_kernel(count, vsum_ref, brow_ref, *refs):
    srcs, outs, small, sem = refs[:count], refs[count : 2 * count], refs[2 * count : -1], refs[-1]
    copies = [pltpu.make_async_copy(a, b, sem.at[k]) for k, (a, b) in enumerate(zip(srcs, outs))]
    for cp in copies:
        cp.start()
    i = lax.axis_index("shard")
    width = vsum_ref.shape[1]

    def own(row, out):
        size = out.shape[1]
        shift = lax.rem(width - lax.rem(i * size, width), width)
        out[...] = pltpu.roll(jnp.broadcast_to(row, (8, width)), shift, 1)[:1, :size]

    own(brow_ref[0:1], small[0])
    own(brow_ref[2:3], small[1])
    for r in range(6):
        own(vsum_ref[r : r + 1], small[2 + r])
    row = 8 + (i * small[8].shape[1]) // width
    own(vsum_ref[pl.ds(row, 1)], small[8])
    for cp in copies:
        cp.wait()


def deliver(arrays, vsum, brow, rows, up_rows):
    count = len(arrays)
    vm = pl.BlockSpec(memory_space=pltpu.VMEM)
    anywhere = pl.BlockSpec(memory_space=pl.ANY)
    sizes = [rows] * 8 + [up_rows]
    got = pl.pallas_call(
        functools.partial(deliver_kernel, count),
        in_specs=[vm] * (2 + count),
        out_specs=[anywhere] * count + [vm] * len(sizes),
        out_shape=[jax.ShapeDtypeStruct(a.shape, a.dtype) for a in arrays] + [jax.ShapeDtypeStruct((1, s), f32) for s in sizes],
        scratch_shapes=[pltpu.SemaphoreType.DMA((count,))],
        compiler_params=pltpu.CompilerParams(vmem_limit_bytes=VMEM_LIMIT),
    )(vsum, brow, *arrays)
    return got[:count], [v.reshape(-1) for v in got[count:]]


def on_device(
    inputs, teacher, seq_lengths, w_qkv, q_bias, v_bias, w_out, out_bias, attn_gain, attn_shift, w_up, up_bias,
    w_down, down_bias, ffn_gain, ffn_shift,
):
    n = lax.axis_size("shard")
    s = lax.axis_index("seq")
    i = lax.axis_index("shard")
    toks, width = inputs.shape[1:]
    group = 4 * toks
    hidden = w_up.shape[1]
    rows = w_qkv.shape[0]
    heads = HEADS // 4
    folds = hidden // width
    tokens = inputs[0]
    lens = seq_lengths[0]
    ends = [lens[0], lens[0] + lens[1], lens[0] + lens[1] + lens[2]]

    own_w = lax.dynamic_index_in_dim(w_qkv.reshape(rows, 3, 4, heads, HD), s, 2, keepdims=False)
    own_w = jnp.transpose(own_w, (0, 2, 1, 3)).reshape(rows, heads * 3 * HD)
    live = jnp.stack([ends[2] // 64, lax.rem(ends[2], 64)]).astype(bf16)
    small = jnp.concatenate(
        [out_bias[None], attn_gain[None], attn_shift[None], down_bias[None], ffn_gain[None], ffn_shift[None], q_bias[None],
         v_bias[None], up_bias.reshape(folds, rows), jnp.broadcast_to(live[:, None], (2, rows))], axis=0
    )
    small = jnp.pad(small, ((0, 16 - small.shape[0]), (0, -rows % 128)))
    xg, wq_g, small_g = gather_all(tokens, (own_w, small), ("whole", "whole"), n, 1)
    x_all = xg.reshape(group, width)
    wq = wq_g.reshape(width, heads * 3 * HD)
    vecs = jnp.transpose(small_g[:, :, :rows], (1, 0, 2)).astype(f32)
    eight = vecs[:8].reshape(8, width)
    b_up = jnp.transpose(vecs[8 : 8 + folds], (1, 0, 2)).reshape(hidden // 512, 512)
    live_total = jnp.sum(vecs[8 + folds, :, 0]) * 64.0 + jnp.sum(vecs[9 + folds, :, 0])

    own_q, own_v = [
        lax.dynamic_slice_in_dim(eight[r], s * heads * HD, heads * HD).reshape(heads, 1, HD) for r in (6, 7)
    ]
    bias = jnp.concatenate([own_q, jnp.zeros_like(own_q), own_v], axis=1).reshape(heads, 3 * HD, 1)

    pos = lax.broadcasted_iota(jnp.int32, (16, group), 1)
    row = lax.broadcasted_iota(jnp.int32, (16, group), 0)
    seg = sum((pos >= e).astype(jnp.int32) for e in ends)
    augq = jnp.where((row < 4) & (seg != row), neg_large, 0.0).astype(bf16)
    augk = jnp.where((row < 4) & (seg == row) | (row >= 8) & (row < 11), 1.0, 0.0).astype(bf16)
    augv = jnp.where(row < 3, 1.0, 0.0).astype(bf16)

    q, k, v, ctx, lse, w_t, merged, wo_g, down_g, up_g = attend(
        x_all, wq, bias, augq, augk, augv, (w_out, w_down, w_up), ("half", "half", "quarter"), n, 2
    )
    own_pos = s * toks + lax.iota(jnp.int32, toks)
    live_rows = (own_pos < ends[2]).astype(f32)[:, None]
    scale = (float(group * n) / live_total).reshape(1)
    result, grad_resid_one, gm, d_out, d_up, d_down, dvec, d_bup, wall = feed_forward(
        scale, merged, tokens, teacher[0], live_rows, wo_g.reshape(width, width), eight, b_up,
        up_g.reshape(width, hidden),        down_g.reshape(hidden, width), w_t, n, 4,
    )
    vec = jnp.concatenate([dvec, d_bup.reshape(folds, width), jnp.zeros((8 - folds, width), f32)], axis=0)
    grad_in, d_qkv, brow, vsum, d_up_r, d_down_r, d_out_r = attend_back(
        q, k, v, ctx, lse, gm, x_all, wall, grad_resid_one, vec,
        (d_up.reshape(2, n, rows, hidden // 4), d_down.reshape(n, hidden // n, width // 2), d_out.reshape(n, rows, width // 2)),
        ("quarter", "half", "half"), n, 3,
    )

    big, small = deliver((result, grad_in, d_qkv, d_out_r, d_up_r, d_down_r), vsum, brow, rows, hidden // n)
    result, grad_in, d_qkv, d_out_r, d_up_r, d_down_r = big
    d_qb, d_vb, d_ob, d_ag, d_as, d_db, d_fg, d_fs, d_ub = small
    return (
        result[None], grad_in[None], d_qkv, d_qb, d_vb, d_out_r, d_ob, d_ag, d_as, d_up_r, d_ub, d_down_r, d_db, d_fg, d_fs,
    )


def solution(mesh):
    tokens, matrix, vector = P("shard", "seq", None), P("shard", None), P("shard")
    in_specs = (tokens, tokens, matrix, matrix, vector, vector, matrix, vector, vector, vector, matrix, vector, matrix,
                vector, vector, vector)
    out_specs = (tokens, tokens, matrix, vector, vector, matrix, vector, vector, vector, matrix, vector, matrix, vector,
                 vector, vector)
    return jax.shard_map(on_device, mesh=mesh, in_specs=in_specs, out_specs=out_specs, check_vma=False)
```

```python
import functools
import math

import jax
import jax.numpy as jnp
from jax import lax
from jax.experimental import pallas as pl
from jax.experimental.pallas import tpu as pltpu
from jax.sharding import PartitionSpec as P

HEADS = 12
HD = 64
ROWS = 80
MESH = pl.DeviceIdType.MESH
f32 = jnp.float32
bf16 = jnp.bfloat16
epsilon = 1e-12
neg_large = -1e30
LOG2E = math.log2(math.e)
LN2 = math.log(2.0)
VMEM_LIMIT = 60 << 20

NN = (((1,), (0,)), ((), ()))
NT = (((1,), (1,)), ((), ()))
TN = (((0,), (0,)), ((), ()))


def mm(left, right, dims=NN):
    return lax.dot_general(left, right, dims, preferred_element_type=f32)


class Place:
    def __init__(self, n):
        self.n = n
        self.hi_n = 4 if n % 4 == 0 else 1
        self.lo_n = n // self.hi_n
        self.s = lax.axis_index("seq")
        self.i = lax.axis_index("shard")
        self.core = lax.rem(self.s, 2)
        self.mate = self.s + 1 - 2 * self.core
        self.far = lax.rem(self.s + 2, 4)
        self.hi = self.i // self.lo_n
        self.lo = lax.rem(self.i, self.lo_n)

    def at_hi(self, hi):
        return (self.s, hi * self.lo_n + self.lo)

    def at_lo(self, lo):
        return (self.s, self.hi * self.lo_n + lo)

    def on_seq(self, s):
        return (s, self.i)


def meet(peers):
    bar = pltpu.get_barrier_semaphore()
    for peer in peers:
        pl.semaphore_signal(bar, inc=1, device_id=peer, device_id_type=MESH)
    pl.semaphore_wait(bar, len(peers))


def rcopy(src, dst, send, recv, peer):
    return pltpu.make_async_remote_copy(
        src_ref=src, dst_ref=dst, send_sem=send, recv_sem=recv, device_id=peer, device_id_type=MESH
    )


def half(cols, core):
    return pl.ds(pl.multiple_of(core * (cols // 2), 128), cols // 2)


def gather_sems(n, count):
    dma = pltpu.SemaphoreType.DMA
    return [dma((count, 2 * n)), dma((count, n)), dma((count, n)), dma((count, n)), dma((count, 3 * n)), dma((count, 3 * n)), dma((count,))]


class Gather:
    def __init__(self, place, idx, src, dst, mode, sems):
        self.p, self.a, self.src, self.dst, self.mode = place, idx, src, dst, mode
        self.s1, self.r1, self.s2, self.r2, self.s3, self.r3, self.own = sems

    def view(self, ref, core, chip=None):
        cols = ref.shape[-1]
        if self.mode == "whole":
            return ref
        if self.mode == "half" or chip is None:
            return ref.at[:, half(cols, core)]
        at = core * (cols // 2) + chip * (cols // 4)
        return ref.at[:, pl.ds(pl.multiple_of(at, 128), cols // 4)]

    def mine(self, ref):
        return self.view(ref, self.p.core, self.p.s // 2)

    def local(self):
        return pltpu.make_async_copy(self.src, self.dst.at[self.p.i], self.own.at[self.a])

    def along_hi(self, hi, step):
        p, a = self.p, self.a
        blk = hi * p.lo_n + p.lo
        there = self.mine(self.dst.at[blk])
        return lambda own: rcopy(
            self.mine(self.src) if own else there, there, self.s1.at[a, blk if step > 0 else p.n + blk], self.r1.at[a, blk],
            p.at_hi(p.hi + step),
        )

    def along_lo(self, hi, j, own=False):
        p, a = self.p, self.a
        blk = hi * p.lo_n + p.lo
        there = self.mine(self.dst.at[blk])
        return rcopy(
            self.mine(self.src) if own else there, there, self.s2.at[a, hi * p.lo_n + j], self.r2.at[a, blk],
            p.at_lo(lax.rem(p.lo + j, p.lo_n)),
        )

    def to_far(self, blk, chip):
        p, a = self.p, self.a
        here = self.view(self.dst.at[blk], p.core, chip)
        return rcopy(here, here, self.s3.at[a, 2 * p.n + blk], self.r3.at[a, 2 * p.n + blk], p.on_seq(p.far))

    def to_mate(self, blk, core, chip=None):
        p, a = self.p, self.a
        here = self.view(self.dst.at[blk], core, chip)
        at = blk if chip is None else chip * p.n + blk
        return rcopy(here, here, self.s3.at[a, at], self.r3.at[a, at], p.on_seq(p.mate))

    def here(self, blk):
        if self.mode == "half":
            self.to_mate(blk, self.p.core).start()
        if self.mode == "quarter":
            self.to_far(blk, self.p.s // 2).start()
            self.to_mate(blk, self.p.core, self.p.s // 2).start()

    def start(self):
        p = self.p
        self.local().start()
        for step in (1, -1):

            @pl.when((p.hi + step >= 0) & (p.hi + step < p.hi_n))
            def _(step=step):
                self.along_hi(p.hi, step)(True).start()

        for j in range(1, p.lo_n):
            self.along_lo(p.hi, j, True).start()

    def come(self, m, step):
        p = self.p
        hi = p.hi - step * m

        @pl.when((hi >= 0) & (hi < p.hi_n))
        def _():
            blk = hi * p.lo_n + p.lo
            there = self.mine(self.dst.at[blk])
            rcopy(there, there, self.s1.at[self.a, 0], self.r1.at[self.a, blk], p.at_hi(p.hi)).wait_recv()

            @pl.when((p.hi + step >= 0) & (p.hi + step < p.hi_n))
            def _():
                self.along_hi(hi, step)(False).start()

            for j in range(1, p.lo_n):
                self.along_lo(hi, j).start()
            self.here(blk)

    def pass_on(self, m):
        self.come(m, 1)
        self.come(m, -1)

    def both_ways(self, m, body):
        p = self.p
        if m == 0:
            body(p.hi)
            return
        for step in (1, -1):
            hi = p.hi - step * m
            pl.when((hi >= 0) & (hi < p.hi_n))(lambda hi=hi: body(hi))

    def take_lo(self, m):
        p, a = self.p, self.a

        def body(hi):
            for j in range(1, p.lo_n):
                lo = lax.rem(p.lo + j, p.lo_n)
                blk = hi * p.lo_n + lo
                there = self.mine(self.dst.at[blk])
                rcopy(there, there, self.s2.at[a, 0], self.r2.at[a, blk], p.at_lo(lo)).wait_recv()
                self.here(blk)

        self.both_ways(m, body)

    def take_far(self, m):
        p = self.p

        def body(hi):
            for j in range(p.lo_n):
                if m or j:
                    blk = hi * p.lo_n + lax.rem(p.lo + j, p.lo_n)
                    self.to_far(blk, 1 - p.s // 2).wait_recv()
                    self.to_mate(blk, p.core, 1 - p.s // 2).start()

        if self.mode == "quarter":
            self.both_ways(m, body)

    def finish(self):
        p = self.p
        for m in range(p.hi_n):
            hi = lax.rem(p.hi + m, p.hi_n)
            for j in range(p.lo_n):
                blk = hi * p.lo_n + lax.rem(p.lo + j, p.lo_n)
                if self.mode != "whole" and (m or j):
                    for chip in (None,) if self.mode == "half" else (0, 1):
                        self.to_mate(blk, 1 - p.core, chip).wait_recv()
                        self.to_mate(blk, p.core, chip).wait_send()
                    if self.mode == "quarter":
                        self.to_far(blk, p.s // 2).wait_send()
                if j:
                    self.along_lo(hi, j).wait_send()
        for step in (1, -1):
            for m in range(p.hi_n):
                hi = p.hi - step * m

                @pl.when((hi >= 0) & (hi < p.hi_n) & (p.hi + step >= 0) & (p.hi + step < p.hi_n))
                def _(hi=hi, step=step):
                    self.along_hi(hi, step)(False).wait_send()

        self.local().wait()

    def steps(self):
        for m in range(1, self.p.hi_n):
            yield lambda m=m: self.pass_on(m)
        for m in range(self.p.hi_n):
            yield lambda m=m: self.take_lo(m)
        if self.mode == "quarter":
            for m in range(self.p.hi_n):
                yield lambda m=m: self.take_far(m)


def peers_of(p, seq_mates):
    out = [p.at_hi(lax.rem(p.hi + k, p.hi_n)) for k in range(1, p.hi_n)]
    out += [p.at_lo(lax.rem(p.lo + j, p.lo_n)) for j in range(1, p.lo_n)]
    return out + [p.on_seq(s) for s in seq_mates]


def gather_kernel(n, splits, chunks, *refs):
    count = len(splits)
    x_ref, srcs = refs[0], refs[1 : 1 + count]
    xg_ref, dsts = refs[1 + count], refs[2 + count : 2 + 2 * count]
    sems = refs[2 + 2 * count : 9 + 2 * count]
    xsem, xs1, xr1, xs2, xr2, xown = refs[9 + 2 * count :]
    p = Place(n)
    meet(peers_of(p, (p.mate, p.far)))
    rows = x_ref.shape[0] // chunks
    part = lambda q: pl.ds(q * rows, rows)
    sent = []
    for q in range(chunks):
        cp = rcopy(x_ref.at[part(q)], xg_ref.at[p.s, part(q)], xs1.at[q], xr1.at[q], p.on_seq(p.far))
        cp.start()
        sent.append(cp)
    gathers = [Gather(p, a, srcs[a], dsts[a], splits[a], sems) for a in range(count)]
    for g in gathers:
        g.start()
    own = pltpu.make_async_copy(x_ref, xg_ref.at[p.s], xown)
    own.start()
    cp = rcopy(x_ref, xg_ref.at[p.s], xsem.at[0], xsem.at[1], p.on_seq(p.mate))
    cp.start()
    sent.append(cp)
    for m in range(1, p.hi_n):
        for g in gathers:
            g.pass_on(m)
    for m in range(p.hi_n):
        for g in gathers:
            g.take_lo(m)
    for q in range(chunks):
        here = xg_ref.at[p.far, part(q)]
        rcopy(here, here, xs1.at[q], xr1.at[q], p.on_seq(p.far)).wait_recv()
        cp = rcopy(here, here, xs2.at[q], xr2.at[q], p.on_seq(p.mate))
        cp.start()
        sent.append(cp)
    there = xg_ref.at[p.mate]
    rcopy(there, there, xsem.at[0], xsem.at[1], p.on_seq(p.mate)).wait_recv()
    for q in range(chunks):
        there = xg_ref.at[3 - p.s, part(q)]
        rcopy(there, there, xs2.at[q], xr2.at[q], p.on_seq(p.mate)).wait_recv()
    for g in gathers:
        g.finish()
    for cp in sent:
        cp.wait_send()
    own.wait()


def gather_all(x, arrays, splits, n, cid):
    hi_n = 4 if n % 4 == 0 else 1
    chunks = 4
    count = len(arrays)
    anywhere = pl.BlockSpec(memory_space=pl.ANY)
    return pl.pallas_call(
        functools.partial(gather_kernel, n, splits, chunks),
        out_shape=[jax.ShapeDtypeStruct((4,) + x.shape, x.dtype)]
        + [jax.ShapeDtypeStruct((n,) + a.shape, a.dtype) for a in arrays],
        in_specs=[pl.BlockSpec(memory_space=pltpu.VMEM)] * (1 + count),
        out_specs=[anywhere] * (1 + count),
        scratch_shapes=gather_sems(n, count)
        + [
            pltpu.SemaphoreType.DMA((2,)),
            pltpu.SemaphoreType.DMA((chunks,)),
            pltpu.SemaphoreType.DMA((chunks,)),
            pltpu.SemaphoreType.DMA((chunks,)),
            pltpu.SemaphoreType.DMA((chunks,)),
            pltpu.SemaphoreType.DMA,
        ],
        compiler_params=pltpu.CompilerParams(collective_id=cid, has_side_effects=True),
    )(x, *arrays)


CHUNK = 512
BACK_CHUNK = 256
STOPS = (0, 1, 2, 3, 4, 5)


OFFSETS = (2, 1, 3, 0)
WHEN_HALF = {"lo": (3, 5, 7, 9), "owner": 15, "meet": 17}
WHEN_QUARTER = {"far": (6, 7, 8, 9), "lo": (8, 9.5, 11, 12), "owner": 17, "meet": 17}
WHEN_HEAD = ((17, 16), (17, 17))
WHEN_GATHER = (
    (2, 4, 7, 6, 8, 10, 12),
    (3, 8, 12, 9, 12, 15, 17),
    (4, 9, 13, 10, 12, 14, 16, 15, 16, 17, 17),
)


def forward_kernel(n, heads, splits, x_ref, w_ref, b_ref, augq_ref, augk_ref, augv_ref, *refs):
    count = len(splits)
    srcs = refs[:count]
    q_ref, k_ref, v_ref, ctx_ref, lse_ref, wt_ref, merged_ref = refs[count : count + 7]
    dsts = refs[count + 7 : 2 * count + 7]
    sems = refs[2 * count + 7 : 2 * count + 14]
    xsend, xrecv, xown = refs[2 * count + 14 :]
    p = Place(n)
    h = pl.program_id(0)
    toks = x_ref.shape[0]
    part_toks = toks // 4
    gathers = [Gather(p, a, srcs[a], dsts[a], splits[a], sems) for a in range(count)]

    @pl.when(h == 0)
    def _():
        meet(peers_of(p, [lax.rem(p.s + k, 4) for k in range(1, 4)]))
        for g in gathers:
            g.start()
        wt_ref[...] = w_ref[...].T

    plan = [[] for _ in range(heads * len(STOPS))]
    for a, g in enumerate(gathers):
        for slot, step in zip(WHEN_GATHER[a], g.steps()):
            plan[slot].append(step)
    proj = mm(wt_ref[pl.ds(pl.multiple_of(h * 3 * HD, 64), 3 * HD)], x_ref[...], NT) + b_ref[0]
    scale = LOG2E / math.sqrt(HD)
    q_ref[0, :HD] = (proj[:HD] * scale).astype(bf16)
    q_ref[0, HD:] = augq_ref[...]
    k_ref[0, :HD] = proj[HD : 2 * HD].astype(bf16)
    k_ref[0, HD:] = augk_ref[...]
    v_ref[0, :HD] = proj[2 * HD :].astype(bf16)
    v_ref[0, HD:] = augv_ref[...]
    q = q_ref[0]
    top = jnp.full((1, toks), -3e38, f32)
    acc = jnp.zeros((ROWS, toks), f32)
    for j in range(toks // CHUNK):
        part = pl.ds(j * CHUNK, CHUNK)
        s = mm(k_ref[0, :, part], q, TN)
        new = jnp.maximum(top, jnp.max(s, axis=0, keepdims=True))
        probs = jnp.exp2(s - new).astype(bf16)
        acc = acc * jnp.exp2(top - new) + mm(v_ref[0, :, part], probs)
        top = new
        if j in STOPS:
            for hh in range(heads):
                steps = plan[hh * len(STOPS) + STOPS.index(j)]
                if steps:

                    @pl.when(h == hh)
                    def _(steps=steps):
                        for step in steps:
                            step()

    z = acc[HD : HD + 1]
    mine = pl.ds(pl.multiple_of(h * HD, HD), HD)
    ctx_ref[mine] = (acc[:HD] / z).astype(bf16)
    lse_ref[0] = jnp.broadcast_to(top + jnp.log2(z), (8, toks))

    def there(hh, src):
        return merged_ref.at[pl.ds(pl.multiple_of(src * heads * HD + hh * HD, HD), HD)]

    def out(hh, k):
        to = lax.rem(p.s + k, 4)
        block = ctx_ref.at[
            pl.ds(pl.multiple_of(hh * HD, HD), HD), pl.ds(pl.multiple_of(to * part_toks, 128), part_toks)
        ]
        if k == 0:
            return pltpu.make_async_copy(block, there(hh, p.s), xown.at[hh])
        return rcopy(block, there(hh, p.s), xsend.at[hh * 4 + k], xrecv.at[hh * 4 + p.s], p.on_seq(to))

    for k in (2, 3, 1, 0):
        out(h, k).start()

    @pl.when(h == heads - 1)
    def _():
        for g in gathers:
            g.finish()
        for hh in range(heads):
            for k in range(1, 4):
                frm = lax.rem(p.s + k, 4)
                rcopy(there(hh, frm), there(hh, frm), xsend.at[0], xrecv.at[hh * 4 + frm], p.on_seq(frm)).wait_recv()
                out(hh, k).wait_send()
            out(hh, 0).wait()


def attend(x, w, bias, augq, augk, augv, arrays, splits, n, cid):
    toks, width = x.shape
    cols = w.shape[1]
    heads = cols // (3 * HD)
    hi_n = 4 if n % 4 == 0 else 1
    count = len(arrays)
    one = pl.Buffered(1)
    fixed = lambda shape: pl.BlockSpec(shape, lambda h: (0, 0), pipeline_mode=one)
    anywhere = pl.BlockSpec(memory_space=pl.ANY)
    aug = fixed((ROWS - HD, toks))
    head = pl.BlockSpec((1, ROWS, toks), lambda h: (h, 0, 0))
    dma = pltpu.SemaphoreType.DMA
    return pl.pallas_call(
        functools.partial(forward_kernel, n, heads, splits),
        grid=(heads,),
        in_specs=[
            fixed(x.shape),
            fixed(w.shape),
            pl.BlockSpec((1, 3 * HD, 1), lambda h: (h, 0, 0)),
            aug,
            aug,
            aug,
        ]
        + [fixed(a.shape) for a in arrays],
        out_specs=[
            head,
            head,
            head,
            fixed((heads * HD, toks)),
            pl.BlockSpec((1, 8, toks), lambda h: (h, 0, 0)),
            fixed((cols, width)),
            anywhere,
        ]
        + [anywhere] * count,
        out_shape=[jax.ShapeDtypeStruct((heads, ROWS, toks), bf16)] * 3
        + [
            jax.ShapeDtypeStruct((heads * HD, toks), bf16),
            jax.ShapeDtypeStruct((heads, 8, toks), f32),
            jax.ShapeDtypeStruct((cols, width), bf16),
            jax.ShapeDtypeStruct((width, toks // 4), bf16),
        ]
        + [jax.ShapeDtypeStruct((n,) + a.shape, a.dtype) for a in arrays],
        scratch_shapes=gather_sems(n, count) + [dma((4 * heads,)), dma((4 * heads,)), dma((heads,))],
        compiler_params=pltpu.CompilerParams(collective_id=cid, has_side_effects=True, vmem_limit_bytes=VMEM_LIMIT),
    )(x, w, bias, augq, augk, augv, *arrays)


def three_parts(row):
    first = row.astype(bf16)
    rest = row - first.astype(f32)
    second = rest.astype(bf16)
    third = (rest - second.astype(f32)).astype(bf16)
    rows = lax.broadcasted_iota(jnp.int32, (8, row.shape[1]), 0)
    pick = lambda k, v: jnp.where(rows == k, jnp.broadcast_to(v.astype(f32), rows.shape), 0.0)
    return pick(0, first) + pick(1, second) + pick(2, third)


class VectorSum:
    def __init__(self, p, src, inbox, seqbox, sems):
        self.p, self.src, self.inbox, self.seqbox = p, src, inbox, seqbox
        self.vs, self.vr, self.ws, self.wr = sems

    @staticmethod
    def scratch(n, shape):
        dma = pltpu.SemaphoreType.DMA
        return [pltpu.VMEM((n,) + shape, f32), pltpu.VMEM((4,) + shape, f32), dma((n,)), dma((n,)), dma((4,)), dma((4,))]

    def to_shard(self, k):
        p = self.p
        return rcopy(self.src, self.inbox.at[p.i], self.vs.at[k], self.vr.at[p.i], (p.s, lax.rem(p.i + k, p.n)))

    def to_seq(self, k):
        p = self.p
        here = self.seqbox.at[p.s]
        return rcopy(here, here, self.ws.at[k], self.wr.at[p.s], p.on_seq(lax.rem(p.s + k, 4)))

    def start(self):
        for k in range(1, self.p.n):
            self.to_shard(k).start()
        self.inbox[self.p.i] = self.src[...]

    def over_seq(self):
        p = self.p
        for k in range(1, p.n):
            frm = lax.rem(p.i + k, p.n)
            there = self.inbox.at[frm]
            rcopy(there, there, self.vs.at[0], self.vr.at[frm], (p.s, frm)).wait_recv()
        self.seqbox[p.s] = jnp.sum(self.inbox[...], axis=0)
        for k in range(1, 4):
            self.to_seq(k).start()

    def finish(self):
        p = self.p
        for k in range(1, 4):
            frm = lax.rem(p.s + k, 4)
            there = self.seqbox.at[frm]
            rcopy(there, there, self.ws.at[0], self.wr.at[frm], p.on_seq(frm)).wait_recv()
            self.to_seq(k).wait_send()
        for k in range(1, p.n):
            self.to_shard(k).wait_send()


class Reduce:
    BUFS, SEMS = 5, 8

    def __init__(self, p, src, bufs, mode):
        self.p, self.src, self.mode = p, src, mode
        self.acc, self.side, self.inbox, self.far, self.out = bufs[:5]
        self.so, self.sh, self.rh, self.sl, self.rl, self.sx, self.rx, self.sf = bufs[5:]
        self.pieces = p.hi_n

    @staticmethod
    def scratch(n, hi_n, rows, w, mode):
        lo_n = n // hi_n
        dma = pltpu.SemaphoreType.DMA
        return [
            pltpu.VMEM((n, rows, w), bf16),
            pltpu.VMEM((lo_n, hi_n, rows, w), bf16),
            pltpu.VMEM((hi_n, rows, w), bf16),
            pltpu.VMEM((n if mode == "quarter" else 2, rows, w), bf16),
            pltpu.VMEM((2 if mode == "half" else 4, rows, w), bf16),
            dma((hi_n,)), dma((hi_n,)), dma((hi_n,)), dma((lo_n * hi_n,)), dma((lo_n * hi_n,)), dma((4,)), dma((4,)),
            dma((2 * hi_n,)),
        ]

    def hi_of(self, k):
        n = self.p.hi_n
        return lax.rem(self.p.hi + (OFFSETS[k] if n == 4 else k + 1), n)

    def blocks(self, ref, k):
        return ref.at[pl.ds(self.hi_of(k) * self.p.lo_n, self.p.lo_n)]

    def part(self, chip):
        return self.src.at[chip] if self.mode == "quarter" else self.src

    def load(self, k):
        src = self.part(self.p.s // 2)
        return pltpu.make_async_copy(self.blocks(src, k), self.blocks(self.acc, k), self.so.at[k])

    def swap_chips(self, k):
        p = self.p
        return rcopy(
            self.blocks(self.part(1 - p.s // 2), k), self.blocks(self.far, k), self.sf.at[k], self.sf.at[p.hi_n + k],
            p.on_seq(p.far),
        )

    def along_lo(self, k, j):
        p, d = self.p, self.hi_of(k)
        lo = lax.rem(p.lo + j, p.lo_n)
        src = self.acc if self.mode == "quarter" else self.src
        return rcopy(
            src.at[d * p.lo_n + lo], self.side.at[p.lo, d], self.sl.at[k * p.lo_n + j], self.rl.at[k * p.lo_n + p.lo],
            p.at_lo(lo),
        )

    def to_owner(self, k):
        p, d = self.p, self.hi_of(k)
        return rcopy(self.acc.at[d * p.lo_n + p.lo], self.inbox.at[p.hi], self.sh.at[k], self.rh.at[p.hi], p.at_hi(d))

    def start(self, k):
        if self.mode == "quarter":
            self.swap_chips(k).start()
        else:
            for j in range(1, self.p.lo_n):
                self.along_lo(k, j).start()
        self.load(k).start()

    def far_sum(self, k):
        if self.mode == "quarter":
            self.load(k).wait()
            self.swap_chips(k).wait_recv()
            here = self.blocks(self.acc, k)
            here[...] = here[...] + self.blocks(self.far, k)[...]
            for j in range(1, self.p.lo_n):
                self.along_lo(k, j).start()

    def lo_sum(self, k):
        p, d = self.p, self.hi_of(k)
        if self.mode != "quarter":
            self.load(k).wait()
        mine = self.acc.at[d * p.lo_n + p.lo]
        total = mine[...].astype(f32)
        for j in range(1, p.lo_n):
            lo = lax.rem(p.lo + j, p.lo_n)
            there = self.side.at[lo, d]
            rcopy(there, there, self.sl.at[0], self.rl.at[k * p.lo_n + lo], p.at_lo(lo)).wait_recv()
            total = total + self.side[lo, d].astype(f32)
        mine[...] = total.astype(bf16)
        if k < self.pieces - 1:
            self.to_owner(k).start()

    def owner_sum(self):
        p = self.p
        total = self.acc[p.i].astype(f32)
        for k in range(self.pieces - 1):
            frm = self.hi_of(k)
            got = self.inbox.at[frm]
            rcopy(got, got, self.sh.at[0], self.rh.at[frm], p.at_hi(frm)).wait_recv()
            total = total + self.inbox[frm].astype(f32)
        if self.mode == "half":
            self.far[0] = total.astype(bf16)
            self.to_far().start()
        else:
            self.out[p.s] = total.astype(bf16)
            for k in (2, 3, 1):
                self.to_seq(k).start()

    def to_far(self):
        return rcopy(self.far.at[0], self.far.at[1], self.sx.at[0], self.rx.at[0], self.p.on_seq(self.p.far))

    def to_seq(self, k):
        p = self.p
        here = self.out.at[p.s]
        return rcopy(here, here, self.sx.at[k], self.rx.at[p.s], p.on_seq(lax.rem(p.s + k, 4)))

    def to_mate(self, core):
        here = self.out.at[core]
        return rcopy(here, here, self.sx.at[1], self.rx.at[1], self.p.on_seq(self.p.mate))

    def meet_far(self):
        if self.mode == "half":
            self.to_far().wait_recv()
            self.out[self.p.core] = self.far[0] + self.far[1]
            self.to_mate(self.p.core).start()

    def take_all(self):
        p = self.p
        if self.mode == "half":
            self.to_mate(1 - p.core).wait_recv()
        else:
            for k in range(1, 4):
                frm = lax.rem(p.s + k, 4)
                there = self.out.at[frm]
                rcopy(there, there, self.sx.at[0], self.rx.at[frm], p.on_seq(frm)).wait_recv()

    def store(self, ref):
        w = self.out.shape[2]
        if self.mode == "half":
            for core in range(2):
                ref[:, core * w : (core + 1) * w] = self.out[core].astype(f32)
        else:
            for s in range(4):
                for c in range(w // 128):
                    at = c * 512 + (s % 2) * 256 + (s // 2) * 128
                    ref[:, at : at + 128] = self.out[s, :, c * 128 : (c + 1) * 128].astype(f32)

    def drain(self):
        p = self.p
        if self.mode == "half":
            self.to_mate(p.core).wait_send()
            self.to_far().wait_send()
        else:
            for k in range(1, 4):
                self.to_seq(k).wait_send()
        for k in range(self.pieces):
            if self.mode == "quarter":
                self.swap_chips(k).wait_send()
            for j in range(1, p.lo_n):
                self.along_lo(k, j).wait_send()
            if k < self.pieces - 1:
                self.to_owner(k).wait_send()

    def timed(self, table):
        for k in range(self.pieces):
            if self.mode == "quarter":
                yield table["far"][k % 4], lambda k=k: self.far_sum(k)
            yield table["lo"][k % 4], lambda k=k: self.lo_sum(k)
        yield table["owner"], self.owner_sum
        yield table["meet"], self.meet_far


class Direct:
    REFS = 6

    def __init__(self, p, src, bufs):
        self.p, self.src = p, src
        self.inbox, self.out, self.vs, self.vr, self.ws, self.wr = bufs

    @staticmethod
    def scratch(n, rows, cols):
        dma = pltpu.SemaphoreType.DMA
        return [pltpu.VMEM((n, rows, cols), bf16), pltpu.VMEM((4, rows, cols), bf16), dma((n,)), dma((n,)), dma((4,)), dma((4,))]

    def to_shard(self, k):
        p = self.p
        to = lax.rem(p.i + k, p.n)
        return rcopy(self.src.at[to], self.inbox.at[p.i], self.vs.at[k], self.vr.at[p.i], (p.s, to))

    def to_seq(self, k):
        p = self.p
        here = self.out.at[p.s]
        return rcopy(here, here, self.ws.at[k], self.wr.at[p.s], p.on_seq(lax.rem(p.s + k, 4)))

    def start(self):
        for k in range(1, self.p.n):
            self.to_shard(k).start()

    def owner_sum(self):
        p = self.p
        total = self.src[p.i].astype(f32)
        for k in range(1, p.n):
            frm = lax.rem(p.i + k, p.n)
            there = self.inbox.at[frm]
            rcopy(there, there, self.vs.at[0], self.vr.at[frm], (p.s, frm)).wait_recv()
            total = total + self.inbox[frm].astype(f32)
        self.out[p.s] = total.astype(bf16)
        for k in (2, 3, 1):
            self.to_seq(k).start()

    def take_all(self):
        p = self.p
        for k in range(1, 4):
            frm = lax.rem(p.s + k, 4)
            there = self.out.at[frm]
            rcopy(there, there, self.ws.at[0], self.wr.at[frm], p.on_seq(frm)).wait_recv()

    def drain(self):
        for k in range(1, 4):
            self.to_seq(k).wait_send()
        for k in range(1, self.p.n):
            self.to_shard(k).wait_send()


def backward_kernel(
    n, heads, modes, q_ref, k_ref, v_ref, ctx_ref, lse_ref, gm_ref, x_hbm, wall_hbm, resid_ref, vec_ref, *refs
):
    count = len(modes)
    srcs, refs = refs[:count], refs[count:]
    grad_ref, dw_ref, brow_ref, vsum_ref, sums, refs = refs[0], refs[1], refs[2], refs[3], refs[4 : 4 + count], refs[4 + count :]
    qa, da, dq, dctx, dqkv, dw, got, total, x_ref, wall_ref, xsend, xrecv, xown, gsend, grecv, late_sem = refs[:16]
    vec_bufs, refs = refs[16:22], refs[22:]
    each = Reduce.BUFS + Reduce.SEMS
    p = Place(n)
    h = pl.program_id(0)
    toks = q_ref.shape[2]
    part_toks = toks // 4
    vec = VectorSum(p, vec_ref, vec_bufs[0], vec_bufs[1], vec_bufs[2:])
    reds = [Reduce(p, srcs[a], refs[a * each : (a + 1) * each], modes[a]) for a in range(count)]
    refs = refs[count * each :]
    heads_red = [Direct(p, dw.at[hh], refs[hh * Direct.REFS : (hh + 1) * Direct.REFS]) for hh in range(heads)]

    def tok_part(s):
        return pl.ds(pl.multiple_of(s * part_toks, 128), part_toks)

    def landing(hh, src):
        return dctx.at[pl.ds(pl.multiple_of(hh * HD, HD), HD), tok_part(src)]

    def give(hh, k):
        to = lax.rem(p.s + k, 4)
        block = gm_ref.at[pl.ds(pl.multiple_of(to * heads * HD + hh * HD, HD), HD)]
        if k == 0:
            return pltpu.make_async_copy(block, landing(hh, p.s), xown.at[hh])
        return rcopy(block, landing(hh, p.s), xsend.at[hh * 4 + k], xrecv.at[hh * 4 + p.s], p.on_seq(to))

    def give_keys(hh, to):
        return rcopy(
            dqkv.at[hh, HD:, tok_part(to)], got.at[hh, p.s, HD:], gsend.at[hh * 8 + to], grecv.at[hh * 8 + p.s], p.on_seq(to)
        )

    def give_queries(hh, k):
        to = lax.rem(p.s + k, 4)
        return rcopy(
            dqkv.at[hh, :HD, tok_part(to)], got.at[hh, p.s, :HD], gsend.at[hh * 8 + 4 + k], grecv.at[hh * 8 + 4 + p.s],
            p.on_seq(to),
        )

    def add_tokens(hh):
        for k in range(1, 4):
            frm = lax.rem(p.s + k, 4)
            for there, at in ((got.at[hh, frm, HD:], frm), (got.at[hh, frm, :HD], 4 + frm)):
                rcopy(there, there, gsend.at[0], grecv.at[hh * 8 + at], p.on_seq(frm)).wait_recv()
        flat = lambda v: v.reshape(4 * 3 * HD, v.shape[2])
        total[...] += mm(flat(got[hh]), flat(wall_ref[:, hh * 3 * HD : (hh + 1) * 3 * HD]), TN)

    late = [
        pltpu.make_async_copy(src, dst, late_sem.at[k])
        for k, (src, dst) in enumerate(((resid_ref, total), (x_hbm, x_ref), (wall_hbm, wall_ref)))
    ]

    @pl.when(h == 0)
    def _():
        meet([(p.s, lax.rem(p.i + k, n)) for k in range(1, n)] + [p.on_seq(lax.rem(p.s + k, 4)) for k in range(1, 4)])
        for hh in range(heads):
            for k in (2, 3, 1, 0):
                give(hh, k).start()
        for k in range(p.hi_n):
            for r in reds:
                r.start(k)
        vec.start()
        for cp in late:
            cp.start()

    for k in range(1, 4):
        frm = lax.rem(p.s + k, 4)
        rcopy(landing(h, frm), landing(h, frm), xsend.at[0], xrecv.at[h * 4 + frm], p.on_seq(frm)).wait_recv()
    give(h, 0).wait()

    per = len(STOPS)
    slots = heads * per
    plan, tail = [[] for _ in range(slots)], []
    for r in reds:
        for slot, step in r.timed(WHEN_QUARTER if r.mode == "quarter" else WHEN_HALF):
            plan[min(int(slot), slots - 1)].append((slot, step))
    for hh in range(heads - 1):
        for slot, step in zip(WHEN_HEAD[hh], (heads_red[hh].owner_sum, lambda hh=hh: add_tokens(hh))):
            if slot < slots:
                plan[slot].append((slot + 0.9, step))
            else:
                tail.append(step)
    plan[1].extend((1.9, cp.wait) for cp in late)
    plan[slots // 2].append((slots // 2 + 0.8, vec.over_seq))
    plan = [[step for _, step in sorted(todo, key=lambda x: x[0])] for todo in plan]

    qa[:HD] = q_ref[h, :HD]
    mask = q_ref[h, HD : HD + 8].astype(f32)
    zero = jnp.zeros((8, toks), f32)
    qa[HD:] = jnp.concatenate([mask, three_parts(-lse_ref[h, :1])], axis=0).astype(bf16)
    mine = pl.ds(pl.multiple_of(h * HD, HD), HD)
    grad = dctx[mine]
    delta = jnp.sum(grad.astype(f32) * ctx_ref[mine].astype(f32), axis=0, keepdims=True)
    da[:HD] = grad
    da[HD:] = jnp.concatenate([three_parts(-delta), zero], axis=0).astype(bf16)
    q, do = qa[...], da[...]
    q_rows, do_rows = q.T, do.T
    for j in range(toks // BACK_CHUNK):
        part = pl.ds(j * BACK_CHUNK, BACK_CHUNK)
        k = k_ref[h, :, part]
        probs = jnp.exp2(mm(k, q, TN))
        gprobs = mm(v_ref[h, :, part], do, TN)
        ds = (probs * gprobs).astype(bf16)
        probs = probs.astype(bf16)
        dqkv[h, 2 * HD :, part] = mm(probs, do_rows).T[:HD].astype(bf16)
        dqkv[h, HD : 2 * HD, part] = (mm(ds, q_rows).T[:HD] * LN2).astype(bf16)
        dq_part = mm(k[:HD], ds)
        dq[...] = dq_part if j == 0 else dq[...] + dq_part
        ends = (j + 1) * BACK_CHUNK
        if ends % CHUNK == 0 and ends // CHUNK - 1 in STOPS:
            for hh in range(heads):
                todo = plan[hh * per + STOPS.index(ends // CHUNK - 1)]
                if todo:

                    @pl.when(h == hh)
                    def _(todo=todo):
                        for step in todo:
                            step()

        for to in range(4):
            if ends - BACK_CHUNK < (to + 1) * part_toks <= ends:

                @pl.when(p.s != to)
                def _(to=to):
                    give_keys(h, to).start()

    dqkv[h, :HD] = (dq[...] * (1.0 / math.sqrt(HD))).astype(bf16)
    for k in (2, 3, 1):
        give_queries(h, k).start()
    n_rows = dw_ref.shape[0]
    dw[h, :, :n_rows] = mm(dqkv[h], x_ref[...]).T.astype(bf16).reshape(n, n_rows, 3 * HD)
    sums_row = mm(jnp.ones((16, toks), bf16), dqkv[h], NT)
    first = sums_row.astype(bf16).astype(f32)
    pick = lax.broadcasted_iota(jnp.int32, sums_row.shape, 0)
    parts = jnp.where(pick == 0, first, jnp.where(pick == 1, sums_row - first, 0.0)).astype(bf16)
    dw[h, :, dw.shape[2] - 16 :] = jnp.broadcast_to(parts, (n, 16, 3 * HD))
    for hh in range(heads):

        @pl.when(h == hh)
        def _(hh=hh):
            heads_red[hh].start()

    got[h, p.s] = dqkv[h, :, tok_part(p.s)]

    @pl.when(h == heads - 1)
    def _():
        last = heads_red[heads - 1]
        vec.finish()
        vbox = vec.seqbox
        vsum_ref[...] = (vbox[0] + vbox[1]) + (vbox[2] + vbox[3])
        for a, r in enumerate(reds):
            r.take_all()
            r.store(sums[a])
        for step in tail:
            step()
        last.owner_sum()
        add_tokens(heads - 1)
        grad_ref[...] = total[...].astype(bf16)
        width = 4 * heads * HD
        for hh, r in enumerate(heads_red):
            r.take_all()
            for s in range(4):
                blk = r.out[s].astype(f32)
                top = blk.shape[0] - 16
                row = blk[top : top + 1] + blk[top + 1 : top + 2]
                for w in range(3):
                    at = (s * heads + hh) * HD
                    dw_ref[:, w * width + at : w * width + at + HD] = blk[:n_rows, w * HD : (w + 1) * HD]
                    brow_ref[w : w + 1, at : at + HD] = row[:, w * HD : (w + 1) * HD]
        for r in reds + heads_red:
            r.drain()
        for hh in range(heads):
            for k in range(1, 4):
                give(hh, k).wait_send()
                give_keys(hh, lax.rem(p.s + k, 4)).wait_send()
                give_queries(hh, k).wait_send()


def attend_back(q, k, v, ctx, lse, gm, x, wall, resid, vec, arrays, modes, n, cid):
    heads, _, toks = q.shape
    hi_n = 4 if n % 4 == 0 else 1
    count = len(arrays)
    one = pl.Buffered(1)
    fixed = lambda shape: pl.BlockSpec(shape, lambda h: (0,) * len(shape), pipeline_mode=one)
    anywhere = pl.BlockSpec(memory_space=pl.ANY)
    dma = pltpu.SemaphoreType.DMA
    sums = [(a.shape[-2], a.shape[-1] * (4 if mode == "quarter" else 2)) for a, mode in zip(arrays, modes)]
    part_toks, width = resid.shape
    cols = heads * 3 * HD
    rows = width // n
    high = -(-rows // 16) * 16 + 16
    scratch = [
        pltpu.VMEM((ROWS, toks), bf16),
        pltpu.VMEM((ROWS, toks), bf16),
        pltpu.VMEM((HD, toks), f32),
        pltpu.VMEM((heads * HD, toks), bf16),
        pltpu.VMEM((heads, 3 * HD, toks), bf16),
        pltpu.VMEM((heads, n, high, 3 * HD), bf16),
        pltpu.VMEM((heads, 4, 3 * HD, part_toks), bf16),
        pltpu.VMEM(resid.shape, f32),
        pltpu.VMEM(x.shape, bf16),
        pltpu.VMEM(wall.shape, bf16),
        dma((4 * heads,)), dma((4 * heads,)), dma((heads,)), dma((8 * heads,)), dma((8 * heads,)), dma((3,)),
    ] + VectorSum.scratch(n, vec.shape)
    for a, mode in zip(arrays, modes):
        scratch += Reduce.scratch(n, hi_n, a.shape[-2], a.shape[-1], mode)
    for _ in range(heads):
        scratch += Direct.scratch(n, high, 3 * HD)
    outs = [
        jax.ShapeDtypeStruct(resid.shape, bf16),
        jax.ShapeDtypeStruct((rows, 4 * cols), f32),
        jax.ShapeDtypeStruct((3, width), f32),
        jax.ShapeDtypeStruct(vec.shape, f32),
    ] + [jax.ShapeDtypeStruct(s, f32) for s in sums]
    return pl.pallas_call(
        functools.partial(backward_kernel, n, heads, modes),
        grid=(heads,),
        in_specs=[fixed(a.shape) for a in (q, k, v, ctx, lse)] + [anywhere] * 4 + [fixed(vec.shape)] + [anywhere] * count,
        out_specs=[fixed(o.shape) for o in outs],
        out_shape=outs,
        scratch_shapes=scratch,
        compiler_params=pltpu.CompilerParams(collective_id=cid, has_side_effects=True, vmem_limit_bytes=VMEM_LIMIT),
    )(q, k, v, ctx, lse, gm, x, wall, resid, vec, *arrays)


def norm_parts(value):
    centred = value - jnp.mean(value, axis=-1, keepdims=True)
    inv = lax.rsqrt(jnp.mean(centred * centred, axis=-1, keepdims=True) + epsilon)
    return centred * inv, inv


def norm_back(grad_hat, hat, inv):
    mean_grad = jnp.mean(grad_hat, axis=-1, keepdims=True)
    mean_both = jnp.mean(grad_hat * hat, axis=-1, keepdims=True)
    return inv * (grad_hat - mean_grad - hat * mean_both)


def ffn_kernel(
    n, chunks, scale_ref, merged_ref, tok_ref, teach_ref, live_ref, wo_ref, vec_ref, bup_ref, up_ref, down_ref,
    wt_ref, result_ref, resid_ref, gm_ref, dout_ref, dup_ref, ddown_ref, dvec_ref, dbup_ref, wall_ref,
    low, hat, inv, acc, grad_low, act, slope, down_own, down_got, up_got, out_own, out_got, send, recv, wsend, wrecv,
):
    i = pl.program_id(0)
    p = Place(n)
    row = lambda k: vec_ref[k : k + 1]
    col_sum = lambda v: jnp.sum(v, axis=0, keepdims=True)
    c = jnp.where(i < chunks, i, 2 * chunks - 1 - i)

    def swap(own, got, at):
        return rcopy(own.at[:, half(own.shape[1], 1 - p.core)], got, send.at[at], recv.at[at], p.on_seq(p.mate))

    def swap_down(k):
        return swap(down_own.at[k], down_got.at[k], k)

    def swap_up(k):
        return swap(act.at[k], up_got.at[k], chunks + k)

    def swap_out():
        return swap(out_own, out_got, 2 * chunks)

    def total(own, got):
        return own[:, half(own.shape[1], p.core)].astype(f32) + got[...].astype(f32)

    def settle(k):
        swap_down(k).wait_recv()
        rows = down_own.shape[1]
        ddown_ref[pl.ds(pl.multiple_of(k * rows, 16), rows)] = total(down_own.at[k], down_got.at[k]).astype(bf16)
        swap_up(k).wait_recv()
        both = total(act.at[k], up_got.at[k]).astype(bf16)
        cols = both.shape[1] // 2
        for chip in range(2):
            dup_ref[chip, :, pl.ds(pl.multiple_of(k * cols, 128), cols)] = both[:, chip * cols : (chip + 1) * cols]

    def share(k):
        if k == 0:
            return pltpu.make_async_copy(wt_ref, wall_ref.at[p.s], wsend.at[0])
        return rcopy(wt_ref, wall_ref.at[p.s], wsend.at[k], wrecv.at[p.s], p.on_seq(lax.rem(p.s + k, 4)))

    @pl.when(i == 0)
    def _():
        meet([p.on_seq(lax.rem(p.s + k, 4)) for k in range(1, 4)])
        for k in (2, 3, 1, 0):
            share(k).start()
        branch = mm(merged_ref[...], wo_ref[...], TN) + row(0)
        h, r = norm_parts(tok_ref[...].astype(f32) + branch)
        hat[...] = h
        inv[...] = r
        normed = h * row(1) + row(2)
        low[...] = normed.astype(bf16)
        acc[...] = normed + row(3)

    @pl.when(i < chunks)
    def _():
        pre = mm(low[...], up_ref[...]) + bup_ref[pl.ds(c, 1)]
        cdf = 0.5 + 0.5 * lax.erf(pre * math.sqrt(0.5))
        pdf = jnp.exp(-0.5 * pre * pre) * (1.0 / math.sqrt(2.0 * math.pi))
        a = (pre * cdf).astype(bf16)
        act[c] = a
        slope[c] = cdf + pre * pdf
        acc[...] += mm(a, down_ref[...])

    @pl.when(i == chunks - 1)
    def _():
        h, r = norm_parts(acc[...])
        result = h * row(4) + row(5)
        result_ref[...] = result.astype(bf16)
        grad = (result - teach_ref[...].astype(f32)) * (live_ref[...] * scale_ref[0])
        two = norm_back(grad * row(4), h, r)
        g = two.astype(bf16)
        grad_low[...] = g
        acc[...] = two
        dvec_ref[...] = jnp.zeros_like(dvec_ref)
        dvec_ref[3:4] = col_sum(g.astype(f32))
        dvec_ref[4:5] = col_sum(grad * h)
        dvec_ref[5:6] = col_sum(grad)

    @pl.when(i >= chunks)
    def _():
        g = grad_low[...]
        grad_pre = (mm(g, down_ref[...], NT) * slope[c]).astype(bf16)
        dbup_ref[pl.ds(c, 1)] = col_sum(grad_pre.astype(f32))
        down_own[c] = mm(act[c], g, TN).astype(bf16)
        swap_down(c).start()
        act[c] = mm(low[...], grad_pre, TN).astype(bf16)
        swap_up(c).start()
        acc[...] += mm(grad_pre, up_ref[...], NT)

    @pl.when(i > chunks)
    def _():
        settle(c + 1)

    @pl.when(i == 2 * chunks - 1)
    def _():
        grad = acc[...]
        h = hat[...]
        one = norm_back(grad * row(1), h, inv[...])
        resid_ref[...] = one
        g = one.astype(bf16)
        out_own[...] = mm(merged_ref[...], g).astype(bf16)
        swap_out().start()
        dvec_ref[0:1] = col_sum(g.astype(f32))
        dvec_ref[1:2] = col_sum(grad * h)
        dvec_ref[2:3] = col_sum(grad)
        gm_ref[...] = mm(wo_ref[...], g, NT).astype(bf16)
        settle(0)
        swap_out().wait_recv()
        dout_ref[...] = total(out_own, out_got).astype(bf16)
        swap_out().wait_send()
        for k in range(chunks):
            swap_down(k).wait_send()
            swap_up(k).wait_send()
        for k in range(1, 4):
            frm = lax.rem(p.s + k, 4)
            there = wall_ref.at[frm]
            rcopy(there, there, wsend.at[0], wrecv.at[frm], p.on_seq(frm)).wait_recv()
            share(k).wait_send()
        share(0).wait()


def feed_forward(scale, merged, tokens, teacher, live, w_out, vec, b_up, w_up, w_down, w_t, n, cid):
    toks, width = tokens.shape
    hidden = w_down.shape[0]
    size = 512
    chunks = hidden // size
    one = pl.Buffered(1)
    fixed = lambda shape: pl.BlockSpec(shape, lambda i: (0,) * len(shape), pipeline_mode=one)
    anywhere = pl.BlockSpec(memory_space=pl.ANY)
    turn = lambda i: jnp.where(i < chunks, i, 2 * chunks - 1 - i)
    dma = pltpu.SemaphoreType.DMA
    outs = [
        jax.ShapeDtypeStruct((toks, width), bf16),
        jax.ShapeDtypeStruct((toks, width), f32),
        jax.ShapeDtypeStruct(merged.shape, bf16),
        jax.ShapeDtypeStruct((width, width // 2), bf16),
        jax.ShapeDtypeStruct((2, width, hidden // 4), bf16),
        jax.ShapeDtypeStruct((hidden, width // 2), bf16),
        jax.ShapeDtypeStruct((8, width), f32),
        jax.ShapeDtypeStruct((chunks, size), f32),
    ]
    return pl.pallas_call(
        functools.partial(ffn_kernel, n, chunks),
        grid=(2 * chunks,),
        in_specs=[
            pl.BlockSpec(memory_space=pltpu.SMEM),
            fixed(merged.shape), fixed(tokens.shape), fixed(teacher.shape), fixed(live.shape), fixed(w_out.shape),
            fixed(vec.shape), fixed(b_up.shape),
            pl.BlockSpec((width, size), lambda i: (0, turn(i))),
            pl.BlockSpec((size, width), lambda i: (turn(i), 0)),
            anywhere,
        ],
        out_specs=[fixed(o.shape) for o in outs] + [anywhere],
        out_shape=outs + [jax.ShapeDtypeStruct((4,) + w_t.shape, bf16)],
        scratch_shapes=[
            pltpu.VMEM((toks, width), bf16),
            pltpu.VMEM((toks, width), f32),
            pltpu.VMEM((toks, 1), f32),
            pltpu.VMEM((toks, width), f32),
            pltpu.VMEM((toks, width), bf16),
            pltpu.VMEM((chunks, toks, size), bf16),
            pltpu.VMEM((chunks, toks, size), f32),
            pltpu.VMEM((chunks, size, width), bf16),
            pltpu.VMEM((chunks, size, width // 2), bf16),
            pltpu.VMEM((chunks, width, size // 2), bf16),
            pltpu.VMEM((width, width), bf16),
            pltpu.VMEM((width, width // 2), bf16),
            dma((2 * chunks + 1,)),
            dma((2 * chunks + 1,)),
            dma((4,)),
            dma((4,)),
        ],
        compiler_params=pltpu.CompilerParams(collective_id=cid, has_side_effects=True, vmem_limit_bytes=VMEM_LIMIT),
    )(scale, merged, tokens, teacher, live, w_out, vec, b_up, w_up, w_down, w_t)


def deliver_kernel(count, vsum_ref, brow_ref, *refs):
    srcs, outs, small, sem = refs[:count], refs[count : 2 * count], refs[2 * count : -1], refs[-1]
    copies = [pltpu.make_async_copy(a, b, sem.at[k]) for k, (a, b) in enumerate(zip(srcs, outs))]
    for cp in copies:
        cp.start()
    i = lax.axis_index("shard")
    width = vsum_ref.shape[1]

    def own(row, out):
        size = out.shape[1]
        shift = lax.rem(width - lax.rem(i * size, width), width)
        out[...] = pltpu.roll(jnp.broadcast_to(row, (8, width)), shift, 1)[:1, :size]

    own(brow_ref[0:1], small[0])
    own(brow_ref[2:3], small[1])
    for r in range(6):
        own(vsum_ref[r : r + 1], small[2 + r])
    row = 8 + (i * small[8].shape[1]) // width
    own(vsum_ref[pl.ds(row, 1)], small[8])
    for cp in copies:
        cp.wait()


def deliver(arrays, vsum, brow, rows, up_rows):
    count = len(arrays)
    vm = pl.BlockSpec(memory_space=pltpu.VMEM)
    anywhere = pl.BlockSpec(memory_space=pl.ANY)
    sizes = [rows] * 8 + [up_rows]
    got = pl.pallas_call(
        functools.partial(deliver_kernel, count),
        in_specs=[vm] * (2 + count),
        out_specs=[anywhere] * count + [vm] * len(sizes),
        out_shape=[jax.ShapeDtypeStruct(a.shape, a.dtype) for a in arrays] + [jax.ShapeDtypeStruct((1, s), f32) for s in sizes],
        scratch_shapes=[pltpu.SemaphoreType.DMA((count,))],
        compiler_params=pltpu.CompilerParams(vmem_limit_bytes=VMEM_LIMIT),
    )(vsum, brow, *arrays)
    return got[:count], [v.reshape(-1) for v in got[count:]]


def on_device(
    inputs, teacher, seq_lengths, w_qkv, q_bias, v_bias, w_out, out_bias, attn_gain, attn_shift, w_up, up_bias,
    w_down, down_bias, ffn_gain, ffn_shift,
):
    n = lax.axis_size("shard")
    s = lax.axis_index("seq")
    i = lax.axis_index("shard")
    toks, width = inputs.shape[1:]
    group = 4 * toks
    hidden = w_up.shape[1]
    rows = w_qkv.shape[0]
    heads = HEADS // 4
    folds = hidden // width
    tokens = inputs[0]
    lens = seq_lengths[0]
    ends = [lens[0], lens[0] + lens[1], lens[0] + lens[1] + lens[2]]

    own_w = lax.dynamic_index_in_dim(w_qkv.reshape(rows, 3, 4, heads, HD), s, 2, keepdims=False)
    own_w = jnp.transpose(own_w, (0, 2, 1, 3)).reshape(rows, heads * 3 * HD)
    live = jnp.stack([ends[2] // 64, lax.rem(ends[2], 64)]).astype(bf16)
    small = jnp.concatenate(
        [out_bias[None], attn_gain[None], attn_shift[None], down_bias[None], ffn_gain[None], ffn_shift[None], q_bias[None],
         v_bias[None], up_bias.reshape(folds, rows), jnp.broadcast_to(live[:, None], (2, rows))], axis=0
    )
    small = jnp.pad(small, ((0, 16 - small.shape[0]), (0, -rows % 128)))
    xg, wq_g, small_g = gather_all(tokens, (own_w, small), ("whole", "whole"), n, 1)
    x_all = xg.reshape(group, width)
    wq = wq_g.reshape(width, heads * 3 * HD)
    vecs = jnp.transpose(small_g[:, :, :rows], (1, 0, 2)).astype(f32)
    eight = vecs[:8].reshape(8, width)
    b_up = jnp.transpose(vecs[8 : 8 + folds], (1, 0, 2)).reshape(hidden // 512, 512)
    live_total = jnp.sum(vecs[8 + folds, :, 0]) * 64.0 + jnp.sum(vecs[9 + folds, :, 0])

    own_q, own_v = [
        lax.dynamic_slice_in_dim(eight[r], s * heads * HD, heads * HD).reshape(heads, 1, HD) for r in (6, 7)
    ]
    bias = jnp.concatenate([own_q, jnp.zeros_like(own_q), own_v], axis=1).reshape(heads, 3 * HD, 1)

    pos = lax.broadcasted_iota(jnp.int32, (16, group), 1)
    row = lax.broadcasted_iota(jnp.int32, (16, group), 0)
    seg = sum((pos >= e).astype(jnp.int32) for e in ends)
    augq = jnp.where((row < 4) & (seg != row), neg_large, 0.0).astype(bf16)
    augk = jnp.where((row < 4) & (seg == row) | (row >= 8) & (row < 11), 1.0, 0.0).astype(bf16)
    augv = jnp.where(row < 3, 1.0, 0.0).astype(bf16)

    q, k, v, ctx, lse, w_t, merged, wo_g, down_g, up_g = attend(
        x_all, wq, bias, augq, augk, augv, (w_out, w_down, w_up), ("half", "half", "quarter"), n, 2
    )
    own_pos = s * toks + lax.iota(jnp.int32, toks)
    live_rows = (own_pos < ends[2]).astype(f32)[:, None]
    scale = (float(group * n) / live_total).reshape(1)
    result, grad_resid_one, gm, d_out, d_up, d_down, dvec, d_bup, wall = feed_forward(
        scale, merged, tokens, teacher[0], live_rows, wo_g.reshape(width, width), eight, b_up,
        up_g.reshape(width, hidden),        down_g.reshape(hidden, width), w_t, n, 4,
    )
    vec = jnp.concatenate([dvec, d_bup.reshape(folds, width), jnp.zeros((8 - folds, width), f32)], axis=0)
    grad_in, d_qkv, brow, vsum, d_up_r, d_down_r, d_out_r = attend_back(
        q, k, v, ctx, lse, gm, x_all, wall, grad_resid_one, vec,
        (d_up.reshape(2, n, rows, hidden // 4), d_down.reshape(n, hidden // n, width // 2), d_out.reshape(n, rows, width // 2)),
        ("quarter", "half", "half"), n, 3,
    )

    big, small = deliver((result, grad_in, d_qkv, d_out_r, d_up_r, d_down_r), vsum, brow, rows, hidden // n)
    result, grad_in, d_qkv, d_out_r, d_up_r, d_down_r = big
    d_qb, d_vb, d_ob, d_ag, d_as, d_db, d_fg, d_fs, d_ub = small
    return (
        result[None], grad_in[None], d_qkv, d_qb, d_vb, d_out_r, d_ob, d_ag, d_as, d_up_r, d_ub, d_down_r, d_db, d_fg, d_fs,
    )


def solution(mesh):
    tokens, matrix, vector = P("shard", "seq", None), P("shard", None), P("shard")
    in_specs = (tokens, tokens, matrix, matrix, vector, vector, matrix, vector, vector, vector, matrix, vector, matrix,
                vector, vector, vector)
    out_specs = (tokens, tokens, matrix, vector, vector, matrix, vector, vector, vector, matrix, vector, matrix, vector,
                 vector, vector)
    return jax.shard_map(on_device, mesh=mesh, in_specs=in_specs, out_specs=out_specs, check_vma=False)
```

```python
import functools
import math

import jax
import jax.numpy as jnp
from jax import lax
from jax.experimental import pallas as pl
from jax.experimental.pallas import tpu as pltpu
from jax.sharding import PartitionSpec as P

HEADS = 12
HD = 64
ROWS = 80
MESH = pl.DeviceIdType.MESH
f32 = jnp.float32
bf16 = jnp.bfloat16
epsilon = 1e-12
neg_large = -1e30
LOG2E = math.log2(math.e)
LN2 = math.log(2.0)
VMEM_LIMIT = 60 << 20

NN = (((1,), (0,)), ((), ()))
NT = (((1,), (1,)), ((), ()))
TN = (((0,), (0,)), ((), ()))


def mm(left, right, dims=NN):
    return lax.dot_general(left, right, dims, preferred_element_type=f32)


class Place:
    def __init__(self, n):
        self.n = n
        self.hi_n = 4 if n % 4 == 0 else 1
        self.lo_n = n // self.hi_n
        self.s = lax.axis_index("seq")
        self.i = lax.axis_index("shard")
        self.core = lax.rem(self.s, 2)
        self.mate = self.s + 1 - 2 * self.core
        self.far = lax.rem(self.s + 2, 4)
        self.hi = self.i // self.lo_n
        self.lo = lax.rem(self.i, self.lo_n)

    def at_hi(self, hi):
        return (self.s, hi * self.lo_n + self.lo)

    def at_lo(self, lo):
        return (self.s, self.hi * self.lo_n + lo)

    def on_seq(self, s):
        return (s, self.i)


def meet(peers):
    bar = pltpu.get_barrier_semaphore()
    for peer in peers:
        pl.semaphore_signal(bar, inc=1, device_id=peer, device_id_type=MESH)
    pl.semaphore_wait(bar, len(peers))


def rcopy(src, dst, send, recv, peer):
    return pltpu.make_async_remote_copy(
        src_ref=src, dst_ref=dst, send_sem=send, recv_sem=recv, device_id=peer, device_id_type=MESH
    )


def half(cols, core):
    return pl.ds(pl.multiple_of(core * (cols // 2), 128), cols // 2)


def gather_sems(n, count):
    dma = pltpu.SemaphoreType.DMA
    return [dma((count, 2 * n)), dma((count, n)), dma((count, n)), dma((count, n)), dma((count, 3 * n)), dma((count, 3 * n)), dma((count,))]


class Gather:
    def __init__(self, place, idx, src, dst, mode, sems):
        self.p, self.a, self.src, self.dst, self.mode = place, idx, src, dst, mode
        self.s1, self.r1, self.s2, self.r2, self.s3, self.r3, self.own = sems

    def view(self, ref, core, chip=None):
        cols = ref.shape[-1]
        if self.mode == "whole":
            return ref
        if self.mode == "half" or chip is None:
            return ref.at[:, half(cols, core)]
        at = core * (cols // 2) + chip * (cols // 4)
        return ref.at[:, pl.ds(pl.multiple_of(at, 128), cols // 4)]

    def mine(self, ref):
        return self.view(ref, self.p.core, self.p.s // 2)

    def local(self):
        return pltpu.make_async_copy(self.src, self.dst.at[self.p.i], self.own.at[self.a])

    def along_hi(self, hi, step):
        p, a = self.p, self.a
        blk = hi * p.lo_n + p.lo
        there = self.mine(self.dst.at[blk])
        return lambda own: rcopy(
            self.mine(self.src) if own else there, there, self.s1.at[a, blk if step > 0 else p.n + blk], self.r1.at[a, blk],
            p.at_hi(p.hi + step),
        )

    def along_lo(self, hi, j, own=False):
        p, a = self.p, self.a
        blk = hi * p.lo_n + p.lo
        there = self.mine(self.dst.at[blk])
        return rcopy(
            self.mine(self.src) if own else there, there, self.s2.at[a, hi * p.lo_n + j], self.r2.at[a, blk],
            p.at_lo(lax.rem(p.lo + j, p.lo_n)),
        )

    def to_far(self, blk, chip):
        p, a = self.p, self.a
        here = self.view(self.dst.at[blk], p.core, chip)
        return rcopy(here, here, self.s3.at[a, 2 * p.n + blk], self.r3.at[a, 2 * p.n + blk], p.on_seq(p.far))

    def to_mate(self, blk, core, chip=None):
        p, a = self.p, self.a
        here = self.view(self.dst.at[blk], core, chip)
        at = blk if chip is None else chip * p.n + blk
        return rcopy(here, here, self.s3.at[a, at], self.r3.at[a, at], p.on_seq(p.mate))

    def here(self, blk):
        if self.mode == "half":
            self.to_mate(blk, self.p.core).start()
        if self.mode == "quarter":
            self.to_far(blk, self.p.s // 2).start()
            self.to_mate(blk, self.p.core, self.p.s // 2).start()

    def start(self):
        p = self.p
        self.local().start()
        for step in (1, -1):

            @pl.when((p.hi + step >= 0) & (p.hi + step < p.hi_n))
            def _(step=step):
                self.along_hi(p.hi, step)(True).start()

        for j in range(1, p.lo_n):
            self.along_lo(p.hi, j, True).start()

    def come(self, m, step):
        p = self.p
        hi = p.hi - step * m

        @pl.when((hi >= 0) & (hi < p.hi_n))
        def _():
            blk = hi * p.lo_n + p.lo
            there = self.mine(self.dst.at[blk])
            rcopy(there, there, self.s1.at[self.a, 0], self.r1.at[self.a, blk], p.at_hi(p.hi)).wait_recv()

            @pl.when((p.hi + step >= 0) & (p.hi + step < p.hi_n))
            def _():
                self.along_hi(hi, step)(False).start()

            for j in range(1, p.lo_n):
                self.along_lo(hi, j).start()
            self.here(blk)

    def pass_on(self, m):
        self.come(m, 1)
        self.come(m, -1)

    def both_ways(self, m, body):
        p = self.p
        if m == 0:
            body(p.hi)
            return
        for step in (1, -1):
            hi = p.hi - step * m
            pl.when((hi >= 0) & (hi < p.hi_n))(lambda hi=hi: body(hi))

    def take_lo(self, m):
        p, a = self.p, self.a

        def body(hi):
            for j in range(1, p.lo_n):
                lo = lax.rem(p.lo + j, p.lo_n)
                blk = hi * p.lo_n + lo
                there = self.mine(self.dst.at[blk])
                rcopy(there, there, self.s2.at[a, 0], self.r2.at[a, blk], p.at_lo(lo)).wait_recv()
                self.here(blk)

        self.both_ways(m, body)

    def take_far(self, m):
        p = self.p

        def body(hi):
            for j in range(p.lo_n):
                if m or j:
                    blk = hi * p.lo_n + lax.rem(p.lo + j, p.lo_n)
                    self.to_far(blk, 1 - p.s // 2).wait_recv()
                    self.to_mate(blk, p.core, 1 - p.s // 2).start()

        if self.mode == "quarter":
            self.both_ways(m, body)

    def finish(self):
        p = self.p
        for m in range(p.hi_n):
            hi = lax.rem(p.hi + m, p.hi_n)
            for j in range(p.lo_n):
                blk = hi * p.lo_n + lax.rem(p.lo + j, p.lo_n)
                if self.mode != "whole" and (m or j):
                    for chip in (None,) if self.mode == "half" else (0, 1):
                        self.to_mate(blk, 1 - p.core, chip).wait_recv()
                        self.to_mate(blk, p.core, chip).wait_send()
                    if self.mode == "quarter":
                        self.to_far(blk, p.s // 2).wait_send()
                if j:
                    self.along_lo(hi, j).wait_send()
        for step in (1, -1):
            for m in range(p.hi_n):
                hi = p.hi - step * m

                @pl.when((hi >= 0) & (hi < p.hi_n) & (p.hi + step >= 0) & (p.hi + step < p.hi_n))
                def _(hi=hi, step=step):
                    self.along_hi(hi, step)(False).wait_send()

        self.local().wait()

    def steps(self):
        for m in range(1, self.p.hi_n):
            yield lambda m=m: self.pass_on(m)
        for m in range(self.p.hi_n):
            yield lambda m=m: self.take_lo(m)
        if self.mode == "quarter":
            for m in range(self.p.hi_n):
                yield lambda m=m: self.take_far(m)


def peers_of(p, seq_mates):
    out = [p.at_hi(lax.rem(p.hi + k, p.hi_n)) for k in range(1, p.hi_n)]
    out += [p.at_lo(lax.rem(p.lo + j, p.lo_n)) for j in range(1, p.lo_n)]
    return out + [p.on_seq(s) for s in seq_mates]


def gather_kernel(n, splits, chunks, *refs):
    count = len(splits)
    x_ref, srcs = refs[0], refs[1 : 1 + count]
    xg_ref, dsts = refs[1 + count], refs[2 + count : 2 + 2 * count]
    sems = refs[2 + 2 * count : 9 + 2 * count]
    xsem, xs1, xr1, xs2, xr2, xown = refs[9 + 2 * count :]
    p = Place(n)
    meet(peers_of(p, (p.mate, p.far)))
    rows = x_ref.shape[0] // chunks
    part = lambda q: pl.ds(q * rows, rows)
    sent = []
    for q in range(chunks):
        cp = rcopy(x_ref.at[part(q)], xg_ref.at[p.s, part(q)], xs1.at[q], xr1.at[q], p.on_seq(p.far))
        cp.start()
        sent.append(cp)
    gathers = [Gather(p, a, srcs[a], dsts[a], splits[a], sems) for a in range(count)]
    for g in gathers:
        g.start()
    own = pltpu.make_async_copy(x_ref, xg_ref.at[p.s], xown)
    own.start()
    cp = rcopy(x_ref, xg_ref.at[p.s], xsem.at[0], xsem.at[1], p.on_seq(p.mate))
    cp.start()
    sent.append(cp)
    for m in range(1, p.hi_n):
        for g in gathers:
            g.pass_on(m)
    for m in range(p.hi_n):
        for g in gathers:
            g.take_lo(m)
    for q in range(chunks):
        here = xg_ref.at[p.far, part(q)]
        rcopy(here, here, xs1.at[q], xr1.at[q], p.on_seq(p.far)).wait_recv()
        cp = rcopy(here, here, xs2.at[q], xr2.at[q], p.on_seq(p.mate))
        cp.start()
        sent.append(cp)
    there = xg_ref.at[p.mate]
    rcopy(there, there, xsem.at[0], xsem.at[1], p.on_seq(p.mate)).wait_recv()
    for q in range(chunks):
        there = xg_ref.at[3 - p.s, part(q)]
        rcopy(there, there, xs2.at[q], xr2.at[q], p.on_seq(p.mate)).wait_recv()
    for g in gathers:
        g.finish()
    for cp in sent:
        cp.wait_send()
    own.wait()


def gather_all(x, arrays, splits, n, cid):
    hi_n = 4 if n % 4 == 0 else 1
    chunks = 4
    count = len(arrays)
    anywhere = pl.BlockSpec(memory_space=pl.ANY)
    return pl.pallas_call(
        functools.partial(gather_kernel, n, splits, chunks),
        out_shape=[jax.ShapeDtypeStruct((4,) + x.shape, x.dtype)]
        + [jax.ShapeDtypeStruct((n,) + a.shape, a.dtype) for a in arrays],
        in_specs=[pl.BlockSpec(memory_space=pltpu.VMEM)] * (1 + count),
        out_specs=[anywhere] * (1 + count),
        scratch_shapes=gather_sems(n, count)
        + [
            pltpu.SemaphoreType.DMA((2,)),
            pltpu.SemaphoreType.DMA((chunks,)),
            pltpu.SemaphoreType.DMA((chunks,)),
            pltpu.SemaphoreType.DMA((chunks,)),
            pltpu.SemaphoreType.DMA((chunks,)),
            pltpu.SemaphoreType.DMA,
        ],
        compiler_params=pltpu.CompilerParams(collective_id=cid, has_side_effects=True),
    )(x, *arrays)


CHUNK = 512
BACK_CHUNK = 256
STOPS = (0, 1, 2, 3, 4, 5)


OFFSETS = (2, 1, 3, 0)
WHEN_HALF = {"lo": (3, 5, 7, 9), "owner": 15, "meet": 17}
WHEN_QUARTER = {"far": (6, 7, 8, 9), "lo": (8, 9.5, 11, 12), "owner": 17, "meet": 17}
WHEN_HEAD = ((17, 16), (17, 17))
WHEN_GATHER = (
    (2, 4, 7, 6, 8, 10, 12),
    (3, 8, 12, 9, 12, 15, 17),
    (4, 9, 13, 10, 12, 14, 16, 15, 16, 17, 17),
)


def forward_kernel(n, heads, splits, x_ref, w_ref, b_ref, ends_ref, *refs):
    count = len(splits)
    srcs = refs[:count]
    q_ref, k_ref, v_ref, ctx_ref, lse_ref, wt_ref, merged_ref = refs[count : count + 7]
    dsts = refs[count + 7 : 2 * count + 7]
    sems = refs[2 * count + 7 : 2 * count + 14]
    xsend, xrecv, xown = refs[2 * count + 14 :]
    p = Place(n)
    h = pl.program_id(0)
    toks = x_ref.shape[0]
    part_toks = toks // 4
    gathers = [Gather(p, a, srcs[a], dsts[a], splits[a], sems) for a in range(count)]

    @pl.when(h == 0)
    def _():
        meet(peers_of(p, [lax.rem(p.s + k, 4) for k in range(1, 4)]))
        for g in gathers:
            g.start()
        wt_ref[...] = w_ref[...].T

    plan = [[] for _ in range(heads * len(STOPS))]
    for a, g in enumerate(gathers):
        for slot, step in zip(WHEN_GATHER[a], g.steps()):
            plan[slot].append(step)
    proj = mm(wt_ref[pl.ds(pl.multiple_of(h * 3 * HD, 64), 3 * HD)], x_ref[...], NT) + b_ref[0]
    pos = lax.broadcasted_iota(jnp.int32, (ROWS - HD, toks), 1)
    row = lax.broadcasted_iota(jnp.int32, (ROWS - HD, toks), 0)
    seg = sum((pos >= ends_ref[e]).astype(jnp.int32) for e in range(3))
    scale = LOG2E / math.sqrt(HD)
    q_ref[0, :HD] = (proj[:HD] * scale).astype(bf16)
    q_ref[0, HD:] = jnp.where((row < 4) & (seg != row), neg_large, 0.0).astype(bf16)
    k_ref[0, :HD] = proj[HD : 2 * HD].astype(bf16)
    k_ref[0, HD:] = jnp.where((row < 4) & (seg == row) | (row >= 8) & (row < 11), 1.0, 0.0).astype(bf16)
    v_ref[0, :HD] = proj[2 * HD :].astype(bf16)
    v_ref[0, HD:] = jnp.where(row < 3, 1.0, 0.0).astype(bf16)
    q = q_ref[0]
    top = jnp.full((1, toks), -3e38, f32)
    acc = jnp.zeros((ROWS, toks), f32)
    for j in range(toks // CHUNK):
        part = pl.ds(j * CHUNK, CHUNK)
        s = mm(k_ref[0, :, part], q, TN)
        new = jnp.maximum(top, jnp.max(s, axis=0, keepdims=True))
        probs = jnp.exp2(s - new).astype(bf16)
        acc = acc * jnp.exp2(top - new) + mm(v_ref[0, :, part], probs)
        top = new
        if j in STOPS:
            for hh in range(heads):
                steps = plan[hh * len(STOPS) + STOPS.index(j)]
                if steps:

                    @pl.when(h == hh)
                    def _(steps=steps):
                        for step in steps:
                            step()

    z = acc[HD : HD + 1]
    mine = pl.ds(pl.multiple_of(h * HD, HD), HD)
    ctx_ref[mine] = (acc[:HD] / z).astype(bf16)
    lse_ref[0] = jnp.broadcast_to(top + jnp.log2(z), (8, toks))

    def there(hh, src):
        return merged_ref.at[pl.ds(pl.multiple_of(src * heads * HD + hh * HD, HD), HD)]

    def out(hh, k):
        to = lax.rem(p.s + k, 4)
        block = ctx_ref.at[
            pl.ds(pl.multiple_of(hh * HD, HD), HD), pl.ds(pl.multiple_of(to * part_toks, 128), part_toks)
        ]
        if k == 0:
            return pltpu.make_async_copy(block, there(hh, p.s), xown.at[hh])
        return rcopy(block, there(hh, p.s), xsend.at[hh * 4 + k], xrecv.at[hh * 4 + p.s], p.on_seq(to))

    for k in (2, 3, 1, 0):
        out(h, k).start()

    @pl.when(h == heads - 1)
    def _():
        for g in gathers:
            g.finish()
        for hh in range(heads):
            for k in range(1, 4):
                frm = lax.rem(p.s + k, 4)
                rcopy(there(hh, frm), there(hh, frm), xsend.at[0], xrecv.at[hh * 4 + frm], p.on_seq(frm)).wait_recv()
                out(hh, k).wait_send()
            out(hh, 0).wait()


def attend(x, w, bias, ends, arrays, splits, n, cid):
    toks, width = x.shape
    cols = w.shape[1]
    heads = cols // (3 * HD)
    hi_n = 4 if n % 4 == 0 else 1
    count = len(arrays)
    one = pl.Buffered(1)
    fixed = lambda shape: pl.BlockSpec(shape, lambda h: (0, 0), pipeline_mode=one)
    anywhere = pl.BlockSpec(memory_space=pl.ANY)
    head = pl.BlockSpec((1, ROWS, toks), lambda h: (h, 0, 0))
    dma = pltpu.SemaphoreType.DMA
    return pl.pallas_call(
        functools.partial(forward_kernel, n, heads, splits),
        grid=(heads,),
        in_specs=[
            fixed(x.shape),
            fixed(w.shape),
            pl.BlockSpec((1, 3 * HD, 1), lambda h: (h, 0, 0)),
            pl.BlockSpec(memory_space=pltpu.SMEM),
        ]
        + [fixed(a.shape) for a in arrays],
        out_specs=[
            head,
            head,
            head,
            fixed((heads * HD, toks)),
            pl.BlockSpec((1, 8, toks), lambda h: (h, 0, 0)),
            fixed((cols, width)),
            anywhere,
        ]
        + [anywhere] * count,
        out_shape=[jax.ShapeDtypeStruct((heads, ROWS, toks), bf16)] * 3
        + [
            jax.ShapeDtypeStruct((heads * HD, toks), bf16),
            jax.ShapeDtypeStruct((heads, 8, toks), f32),
            jax.ShapeDtypeStruct((cols, width), bf16),
            jax.ShapeDtypeStruct((width, toks // 4), bf16),
        ]
        + [jax.ShapeDtypeStruct((n,) + a.shape, a.dtype) for a in arrays],
        scratch_shapes=gather_sems(n, count) + [dma((4 * heads,)), dma((4 * heads,)), dma((heads,))],
        compiler_params=pltpu.CompilerParams(collective_id=cid, has_side_effects=True, vmem_limit_bytes=VMEM_LIMIT),
    )(x, w, bias, ends, *arrays)


def three_parts(row):
    first = row.astype(bf16)
    rest = row - first.astype(f32)
    second = rest.astype(bf16)
    third = (rest - second.astype(f32)).astype(bf16)
    rows = lax.broadcasted_iota(jnp.int32, (8, row.shape[1]), 0)
    pick = lambda k, v: jnp.where(rows == k, jnp.broadcast_to(v.astype(f32), rows.shape), 0.0)
    return pick(0, first) + pick(1, second) + pick(2, third)


class VectorSum:
    def __init__(self, p, src, inbox, seqbox, sems):
        self.p, self.src, self.inbox, self.seqbox = p, src, inbox, seqbox
        self.vs, self.vr, self.ws, self.wr = sems

    @staticmethod
    def scratch(n, shape):
        dma = pltpu.SemaphoreType.DMA
        return [pltpu.VMEM((n,) + shape, f32), pltpu.VMEM((4,) + shape, f32), dma((n,)), dma((n,)), dma((4,)), dma((4,))]

    def to_shard(self, k):
        p = self.p
        return rcopy(self.src, self.inbox.at[p.i], self.vs.at[k], self.vr.at[p.i], (p.s, lax.rem(p.i + k, p.n)))

    def to_seq(self, k):
        p = self.p
        here = self.seqbox.at[p.s]
        return rcopy(here, here, self.ws.at[k], self.wr.at[p.s], p.on_seq(lax.rem(p.s + k, 4)))

    def start(self):
        for k in range(1, self.p.n):
            self.to_shard(k).start()
        self.inbox[self.p.i] = self.src[...]

    def over_seq(self):
        p = self.p
        for k in range(1, p.n):
            frm = lax.rem(p.i + k, p.n)
            there = self.inbox.at[frm]
            rcopy(there, there, self.vs.at[0], self.vr.at[frm], (p.s, frm)).wait_recv()
        self.seqbox[p.s] = jnp.sum(self.inbox[...], axis=0)
        for k in range(1, 4):
            self.to_seq(k).start()

    def finish(self):
        p = self.p
        for k in range(1, 4):
            frm = lax.rem(p.s + k, 4)
            there = self.seqbox.at[frm]
            rcopy(there, there, self.ws.at[0], self.wr.at[frm], p.on_seq(frm)).wait_recv()
            self.to_seq(k).wait_send()
        for k in range(1, p.n):
            self.to_shard(k).wait_send()


class Reduce:
    BUFS, SEMS = 5, 8

    def __init__(self, p, src, bufs, mode):
        self.p, self.src, self.mode = p, src, mode
        self.acc, self.side, self.inbox, self.far, self.out = bufs[:5]
        self.so, self.sh, self.rh, self.sl, self.rl, self.sx, self.rx, self.sf = bufs[5:]
        self.pieces = p.hi_n

    @staticmethod
    def scratch(n, hi_n, rows, w, mode):
        lo_n = n // hi_n
        dma = pltpu.SemaphoreType.DMA
        return [
            pltpu.VMEM((n, rows, w), bf16),
            pltpu.VMEM((lo_n, hi_n, rows, w), bf16),
            pltpu.VMEM((hi_n, rows, w), bf16),
            pltpu.VMEM((n if mode == "quarter" else 2, rows, w), bf16),
            pltpu.VMEM((2 if mode == "half" else 4, rows, w), bf16),
            dma((hi_n,)), dma((hi_n,)), dma((hi_n,)), dma((lo_n * hi_n,)), dma((lo_n * hi_n,)), dma((4,)), dma((4,)),
            dma((2 * hi_n,)),
        ]

    def hi_of(self, k):
        n = self.p.hi_n
        return lax.rem(self.p.hi + (OFFSETS[k] if n == 4 else k + 1), n)

    def blocks(self, ref, k):
        return ref.at[pl.ds(self.hi_of(k) * self.p.lo_n, self.p.lo_n)]

    def part(self, chip):
        return self.src.at[chip] if self.mode == "quarter" else self.src

    def load(self, k):
        src = self.part(self.p.s // 2)
        return pltpu.make_async_copy(self.blocks(src, k), self.blocks(self.acc, k), self.so.at[k])

    def swap_chips(self, k):
        p = self.p
        return rcopy(
            self.blocks(self.part(1 - p.s // 2), k), self.blocks(self.far, k), self.sf.at[k], self.sf.at[p.hi_n + k],
            p.on_seq(p.far),
        )

    def along_lo(self, k, j):
        p, d = self.p, self.hi_of(k)
        lo = lax.rem(p.lo + j, p.lo_n)
        src = self.acc if self.mode == "quarter" else self.src
        return rcopy(
            src.at[d * p.lo_n + lo], self.side.at[p.lo, d], self.sl.at[k * p.lo_n + j], self.rl.at[k * p.lo_n + p.lo],
            p.at_lo(lo),
        )

    def to_owner(self, k):
        p, d = self.p, self.hi_of(k)
        return rcopy(self.acc.at[d * p.lo_n + p.lo], self.inbox.at[p.hi], self.sh.at[k], self.rh.at[p.hi], p.at_hi(d))

    def start(self, k):
        if self.mode == "quarter":
            self.swap_chips(k).start()
        else:
            for j in range(1, self.p.lo_n):
                self.along_lo(k, j).start()
        self.load(k).start()

    def far_sum(self, k):
        if self.mode == "quarter":
            self.load(k).wait()
            self.swap_chips(k).wait_recv()
            here = self.blocks(self.acc, k)
            here[...] = here[...] + self.blocks(self.far, k)[...]
            for j in range(1, self.p.lo_n):
                self.along_lo(k, j).start()

    def lo_sum(self, k):
        p, d = self.p, self.hi_of(k)
        if self.mode != "quarter":
            self.load(k).wait()
        mine = self.acc.at[d * p.lo_n + p.lo]
        total = mine[...].astype(f32)
        for j in range(1, p.lo_n):
            lo = lax.rem(p.lo + j, p.lo_n)
            there = self.side.at[lo, d]
            rcopy(there, there, self.sl.at[0], self.rl.at[k * p.lo_n + lo], p.at_lo(lo)).wait_recv()
            total = total + self.side[lo, d].astype(f32)
        mine[...] = total.astype(bf16)
        if k < self.pieces - 1:
            self.to_owner(k).start()

    def owner_sum(self):
        p = self.p
        total = self.acc[p.i].astype(f32)
        for k in range(self.pieces - 1):
            frm = self.hi_of(k)
            got = self.inbox.at[frm]
            rcopy(got, got, self.sh.at[0], self.rh.at[frm], p.at_hi(frm)).wait_recv()
            total = total + self.inbox[frm].astype(f32)
        if self.mode == "half":
            self.far[0] = total.astype(bf16)
            self.to_far().start()
        else:
            self.out[p.s] = total.astype(bf16)
            for k in (2, 3, 1):
                self.to_seq(k).start()

    def to_far(self):
        return rcopy(self.far.at[0], self.far.at[1], self.sx.at[0], self.rx.at[0], self.p.on_seq(self.p.far))

    def to_seq(self, k):
        p = self.p
        here = self.out.at[p.s]
        return rcopy(here, here, self.sx.at[k], self.rx.at[p.s], p.on_seq(lax.rem(p.s + k, 4)))

    def to_mate(self, core):
        here = self.out.at[core]
        return rcopy(here, here, self.sx.at[1], self.rx.at[1], self.p.on_seq(self.p.mate))

    def meet_far(self):
        if self.mode == "half":
            self.to_far().wait_recv()
            self.out[self.p.core] = self.far[0] + self.far[1]
            self.to_mate(self.p.core).start()

    def take_all(self):
        p = self.p
        if self.mode == "half":
            self.to_mate(1 - p.core).wait_recv()
        else:
            for k in range(1, 4):
                frm = lax.rem(p.s + k, 4)
                there = self.out.at[frm]
                rcopy(there, there, self.sx.at[0], self.rx.at[frm], p.on_seq(frm)).wait_recv()

    def store(self, ref):
        w = self.out.shape[2]
        if self.mode == "half":
            for core in range(2):
                ref[:, core * w : (core + 1) * w] = self.out[core].astype(f32)
        else:
            for s in range(4):
                for c in range(w // 128):
                    at = c * 512 + (s % 2) * 256 + (s // 2) * 128
                    ref[:, at : at + 128] = self.out[s, :, c * 128 : (c + 1) * 128].astype(f32)

    def drain(self):
        p = self.p
        if self.mode == "half":
            self.to_mate(p.core).wait_send()
            self.to_far().wait_send()
        else:
            for k in range(1, 4):
                self.to_seq(k).wait_send()
        for k in range(self.pieces):
            if self.mode == "quarter":
                self.swap_chips(k).wait_send()
            for j in range(1, p.lo_n):
                self.along_lo(k, j).wait_send()
            if k < self.pieces - 1:
                self.to_owner(k).wait_send()

    def timed(self, table):
        for k in range(self.pieces):
            if self.mode == "quarter":
                yield table["far"][k % 4], lambda k=k: self.far_sum(k)
            yield table["lo"][k % 4], lambda k=k: self.lo_sum(k)
        yield table["owner"], self.owner_sum
        yield table["meet"], self.meet_far


class Direct:
    REFS = 6

    def __init__(self, p, src, bufs):
        self.p, self.src = p, src
        self.inbox, self.out, self.vs, self.vr, self.ws, self.wr = bufs

    @staticmethod
    def scratch(n, rows, cols):
        dma = pltpu.SemaphoreType.DMA
        return [pltpu.VMEM((n, rows, cols), bf16), pltpu.VMEM((4, rows, cols), bf16), dma((n,)), dma((n,)), dma((4,)), dma((4,))]

    def to_shard(self, k):
        p = self.p
        to = lax.rem(p.i + k, p.n)
        return rcopy(self.src.at[to], self.inbox.at[p.i], self.vs.at[k], self.vr.at[p.i], (p.s, to))

    def to_seq(self, k):
        p = self.p
        here = self.out.at[p.s]
        return rcopy(here, here, self.ws.at[k], self.wr.at[p.s], p.on_seq(lax.rem(p.s + k, 4)))

    def start(self):
        for k in range(1, self.p.n):
            self.to_shard(k).start()

    def owner_sum(self):
        p = self.p
        total = self.src[p.i].astype(f32)
        for k in range(1, p.n):
            frm = lax.rem(p.i + k, p.n)
            there = self.inbox.at[frm]
            rcopy(there, there, self.vs.at[0], self.vr.at[frm], (p.s, frm)).wait_recv()
            total = total + self.inbox[frm].astype(f32)
        self.out[p.s] = total.astype(bf16)
        for k in (2, 3, 1):
            self.to_seq(k).start()

    def take_all(self):
        p = self.p
        for k in range(1, 4):
            frm = lax.rem(p.s + k, 4)
            there = self.out.at[frm]
            rcopy(there, there, self.ws.at[0], self.wr.at[frm], p.on_seq(frm)).wait_recv()

    def drain(self):
        for k in range(1, 4):
            self.to_seq(k).wait_send()
        for k in range(1, self.p.n):
            self.to_shard(k).wait_send()


def backward_kernel(
    n, heads, modes, q_ref, k_ref, v_ref, ctx_ref, lse_ref, gm_ref, x_hbm, wall_hbm, resid_ref, vec_ref, *refs
):
    count = len(modes)
    srcs, refs = refs[:count], refs[count:]
    grad_ref, dw_ref, brow_ref, vsum_ref, sums, refs = refs[0], refs[1], refs[2], refs[3], refs[4 : 4 + count], refs[4 + count :]
    qa, da, dq, dctx, dqkv, dw, got, total, x_ref, wall_ref, xsend, xrecv, xown, gsend, grecv, late_sem = refs[:16]
    vec_bufs, refs = refs[16:22], refs[22:]
    each = Reduce.BUFS + Reduce.SEMS
    p = Place(n)
    h = pl.program_id(0)
    toks = q_ref.shape[2]
    part_toks = toks // 4
    vec = VectorSum(p, vec_ref, vec_bufs[0], vec_bufs[1], vec_bufs[2:])
    reds = [Reduce(p, srcs[a], refs[a * each : (a + 1) * each], modes[a]) for a in range(count)]
    refs = refs[count * each :]
    heads_red = [Direct(p, dw.at[hh], refs[hh * Direct.REFS : (hh + 1) * Direct.REFS]) for hh in range(heads)]

    def tok_part(s):
        return pl.ds(pl.multiple_of(s * part_toks, 128), part_toks)

    def landing(hh, src):
        return dctx.at[pl.ds(pl.multiple_of(hh * HD, HD), HD), tok_part(src)]

    def give(hh, k):
        to = lax.rem(p.s + k, 4)
        block = gm_ref.at[pl.ds(pl.multiple_of(to * heads * HD + hh * HD, HD), HD)]
        if k == 0:
            return pltpu.make_async_copy(block, landing(hh, p.s), xown.at[hh])
        return rcopy(block, landing(hh, p.s), xsend.at[hh * 4 + k], xrecv.at[hh * 4 + p.s], p.on_seq(to))

    def give_keys(hh, to):
        return rcopy(
            dqkv.at[hh, HD:, tok_part(to)], got.at[hh, p.s, HD:], gsend.at[hh * 8 + to], grecv.at[hh * 8 + p.s], p.on_seq(to)
        )

    def give_queries(hh, k):
        to = lax.rem(p.s + k, 4)
        return rcopy(
            dqkv.at[hh, :HD, tok_part(to)], got.at[hh, p.s, :HD], gsend.at[hh * 8 + 4 + k], grecv.at[hh * 8 + 4 + p.s],
            p.on_seq(to),
        )

    def add_tokens(hh):
        for k in range(1, 4):
            frm = lax.rem(p.s + k, 4)
            for there, at in ((got.at[hh, frm, HD:], frm), (got.at[hh, frm, :HD], 4 + frm)):
                rcopy(there, there, gsend.at[0], grecv.at[hh * 8 + at], p.on_seq(frm)).wait_recv()
        flat = lambda v: v.reshape(4 * 3 * HD, v.shape[2])
        total[...] += mm(flat(got[hh]), flat(wall_ref[:, hh * 3 * HD : (hh + 1) * 3 * HD]), TN)

    late = [
        pltpu.make_async_copy(src, dst, late_sem.at[k])
        for k, (src, dst) in enumerate(((resid_ref, total), (x_hbm, x_ref), (wall_hbm, wall_ref)))
    ]

    @pl.when(h == 0)
    def _():
        meet([(p.s, lax.rem(p.i + k, n)) for k in range(1, n)] + [p.on_seq(lax.rem(p.s + k, 4)) for k in range(1, 4)])
        for hh in range(heads):
            for k in (2, 3, 1, 0):
                give(hh, k).start()
        for k in range(p.hi_n):
            for r in reds:
                r.start(k)
        vec.start()
        for cp in late:
            cp.start()

    for k in range(1, 4):
        frm = lax.rem(p.s + k, 4)
        rcopy(landing(h, frm), landing(h, frm), xsend.at[0], xrecv.at[h * 4 + frm], p.on_seq(frm)).wait_recv()
    give(h, 0).wait()

    per = len(STOPS)
    slots = heads * per
    plan, tail = [[] for _ in range(slots)], []
    for r in reds:
        for slot, step in r.timed(WHEN_QUARTER if r.mode == "quarter" else WHEN_HALF):
            plan[min(int(slot), slots - 1)].append((slot, step))
    for hh in range(heads - 1):
        for slot, step in zip(WHEN_HEAD[hh], (heads_red[hh].owner_sum, lambda hh=hh: add_tokens(hh))):
            if slot < slots:
                plan[slot].append((slot + 0.9, step))
            else:
                tail.append(step)
    plan[1].extend((1.9, cp.wait) for cp in late)
    plan[slots // 2].append((slots // 2 + 0.8, vec.over_seq))
    plan = [[step for _, step in sorted(todo, key=lambda x: x[0])] for todo in plan]

    qa[:HD] = q_ref[h, :HD]
    mask = q_ref[h, HD : HD + 8].astype(f32)
    zero = jnp.zeros((8, toks), f32)
    qa[HD:] = jnp.concatenate([mask, three_parts(-lse_ref[h, :1])], axis=0).astype(bf16)
    mine = pl.ds(pl.multiple_of(h * HD, HD), HD)
    grad = dctx[mine]
    delta = jnp.sum(grad.astype(f32) * ctx_ref[mine].astype(f32), axis=0, keepdims=True)
    da[:HD] = grad
    da[HD:] = jnp.concatenate([three_parts(-delta), zero], axis=0).astype(bf16)
    q, do = qa[...], da[...]
    q_rows, do_rows = q.T, do.T
    for j in range(toks // BACK_CHUNK):
        part = pl.ds(j * BACK_CHUNK, BACK_CHUNK)
        k = k_ref[h, :, part]
        probs = jnp.exp2(mm(k, q, TN))
        gprobs = mm(v_ref[h, :, part], do, TN)
        ds = (probs * gprobs).astype(bf16)
        probs = probs.astype(bf16)
        dqkv[h, 2 * HD :, part] = mm(probs, do_rows).T[:HD].astype(bf16)
        dqkv[h, HD : 2 * HD, part] = (mm(ds, q_rows).T[:HD] * LN2).astype(bf16)
        dq_part = mm(k[:HD], ds)
        dq[...] = dq_part if j == 0 else dq[...] + dq_part
        ends = (j + 1) * BACK_CHUNK
        if ends % CHUNK == 0 and ends // CHUNK - 1 in STOPS:
            for hh in range(heads):
                todo = plan[hh * per + STOPS.index(ends // CHUNK - 1)]
                if todo:

                    @pl.when(h == hh)
                    def _(todo=todo):
                        for step in todo:
                            step()

        for to in range(4):
            if ends - BACK_CHUNK < (to + 1) * part_toks <= ends:

                @pl.when(p.s != to)
                def _(to=to):
                    give_keys(h, to).start()

    dqkv[h, :HD] = (dq[...] * (1.0 / math.sqrt(HD))).astype(bf16)
    for k in (2, 3, 1):
        give_queries(h, k).start()
    n_rows = dw_ref.shape[0]
    dw[h, :, :n_rows] = mm(dqkv[h], x_ref[...]).T.astype(bf16).reshape(n, n_rows, 3 * HD)
    sums_row = mm(jnp.ones((16, toks), bf16), dqkv[h], NT)
    first = sums_row.astype(bf16).astype(f32)
    pick = lax.broadcasted_iota(jnp.int32, sums_row.shape, 0)
    parts = jnp.where(pick == 0, first, jnp.where(pick == 1, sums_row - first, 0.0)).astype(bf16)
    dw[h, :, dw.shape[2] - 16 :] = jnp.broadcast_to(parts, (n, 16, 3 * HD))
    for hh in range(heads):

        @pl.when(h == hh)
        def _(hh=hh):
            heads_red[hh].start()

    got[h, p.s] = dqkv[h, :, tok_part(p.s)]

    @pl.when(h == heads - 1)
    def _():
        last = heads_red[heads - 1]
        vec.finish()
        vbox = vec.seqbox
        vsum_ref[...] = (vbox[0] + vbox[1]) + (vbox[2] + vbox[3])
        for a, r in enumerate(reds):
            r.take_all()
            r.store(sums[a])
        for step in tail:
            step()
        last.owner_sum()
        add_tokens(heads - 1)
        grad_ref[...] = total[...].astype(bf16)
        width = 4 * heads * HD
        for hh, r in enumerate(heads_red):
            r.take_all()
            for s in range(4):
                blk = r.out[s].astype(f32)
                top = blk.shape[0] - 16
                row = blk[top : top + 1] + blk[top + 1 : top + 2]
                for w in range(3):
                    at = (s * heads + hh) * HD
                    dw_ref[:, w * width + at : w * width + at + HD] = blk[:n_rows, w * HD : (w + 1) * HD]
                    brow_ref[w : w + 1, at : at + HD] = row[:, w * HD : (w + 1) * HD]
        for r in reds + heads_red:
            r.drain()
        for hh in range(heads):
            for k in range(1, 4):
                give(hh, k).wait_send()
                give_keys(hh, lax.rem(p.s + k, 4)).wait_send()
                give_queries(hh, k).wait_send()


def attend_back(q, k, v, ctx, lse, gm, x, wall, resid, vec, arrays, modes, n, cid):
    heads, _, toks = q.shape
    hi_n = 4 if n % 4 == 0 else 1
    count = len(arrays)
    one = pl.Buffered(1)
    fixed = lambda shape: pl.BlockSpec(shape, lambda h: (0,) * len(shape), pipeline_mode=one)
    anywhere = pl.BlockSpec(memory_space=pl.ANY)
    dma = pltpu.SemaphoreType.DMA
    sums = [(a.shape[-2], a.shape[-1] * (4 if mode == "quarter" else 2)) for a, mode in zip(arrays, modes)]
    part_toks, width = resid.shape
    cols = heads * 3 * HD
    rows = width // n
    high = -(-rows // 16) * 16 + 16
    scratch = [
        pltpu.VMEM((ROWS, toks), bf16),
        pltpu.VMEM((ROWS, toks), bf16),
        pltpu.VMEM((HD, toks), f32),
        pltpu.VMEM((heads * HD, toks), bf16),
        pltpu.VMEM((heads, 3 * HD, toks), bf16),
        pltpu.VMEM((heads, n, high, 3 * HD), bf16),
        pltpu.VMEM((heads, 4, 3 * HD, part_toks), bf16),
        pltpu.VMEM(resid.shape, f32),
        pltpu.VMEM(x.shape, bf16),
        pltpu.VMEM(wall.shape, bf16),
        dma((4 * heads,)), dma((4 * heads,)), dma((heads,)), dma((8 * heads,)), dma((8 * heads,)), dma((3,)),
    ] + VectorSum.scratch(n, vec.shape)
    for a, mode in zip(arrays, modes):
        scratch += Reduce.scratch(n, hi_n, a.shape[-2], a.shape[-1], mode)
    for _ in range(heads):
        scratch += Direct.scratch(n, high, 3 * HD)
    outs = [
        jax.ShapeDtypeStruct(resid.shape, bf16),
        jax.ShapeDtypeStruct((rows, 4 * cols), f32),
        jax.ShapeDtypeStruct((3, width), f32),
        jax.ShapeDtypeStruct(vec.shape, f32),
    ] + [jax.ShapeDtypeStruct(s, f32) for s in sums]
    return pl.pallas_call(
        functools.partial(backward_kernel, n, heads, modes),
        grid=(heads,),
        in_specs=[fixed(a.shape) for a in (q, k, v, ctx, lse)] + [anywhere] * 4 + [fixed(vec.shape)] + [anywhere] * count,
        out_specs=[fixed(o.shape) for o in outs],
        out_shape=outs,
        scratch_shapes=scratch,
        compiler_params=pltpu.CompilerParams(collective_id=cid, has_side_effects=True, vmem_limit_bytes=VMEM_LIMIT),
    )(q, k, v, ctx, lse, gm, x, wall, resid, vec, *arrays)


def norm_parts(value):
    centred = value - jnp.mean(value, axis=-1, keepdims=True)
    inv = lax.rsqrt(jnp.mean(centred * centred, axis=-1, keepdims=True) + epsilon)
    return centred * inv, inv


def norm_back(grad_hat, hat, inv):
    mean_grad = jnp.mean(grad_hat, axis=-1, keepdims=True)
    mean_both = jnp.mean(grad_hat * hat, axis=-1, keepdims=True)
    return inv * (grad_hat - mean_grad - hat * mean_both)


def ffn_kernel(
    n, chunks, scale_ref, merged_ref, tok_ref, teach_ref, live_ref, wo_ref, vec_ref, bup_ref, up_ref, down_ref,
    wt_ref, result_ref, resid_ref, gm_ref, dout_ref, dup_ref, ddown_ref, dvec_ref, dbup_ref, wall_ref,
    low, hat, inv, acc, grad_low, act, slope, down_own, down_got, up_got, out_own, out_got, send, recv, wsend, wrecv,
):
    i = pl.program_id(0)
    p = Place(n)
    row = lambda k: vec_ref[k : k + 1]
    col_sum = lambda v: jnp.sum(v, axis=0, keepdims=True)
    c = jnp.where(i < chunks, i, 2 * chunks - 1 - i)

    def swap(own, got, at):
        return rcopy(own.at[:, half(own.shape[1], 1 - p.core)], got, send.at[at], recv.at[at], p.on_seq(p.mate))

    def swap_down(k):
        return swap(down_own.at[k], down_got.at[k], k)

    def swap_up(k):
        return swap(act.at[k], up_got.at[k], chunks + k)

    def swap_out():
        return swap(out_own, out_got, 2 * chunks)

    def total(own, got):
        return own[:, half(own.shape[1], p.core)].astype(f32) + got[...].astype(f32)

    def settle(k):
        swap_down(k).wait_recv()
        rows = down_own.shape[1]
        ddown_ref[pl.ds(pl.multiple_of(k * rows, 16), rows)] = total(down_own.at[k], down_got.at[k]).astype(bf16)
        swap_up(k).wait_recv()
        both = total(act.at[k], up_got.at[k]).astype(bf16)
        cols = both.shape[1] // 2
        for chip in range(2):
            dup_ref[chip, :, pl.ds(pl.multiple_of(k * cols, 128), cols)] = both[:, chip * cols : (chip + 1) * cols]

    def share(k):
        if k == 0:
            return pltpu.make_async_copy(wt_ref, wall_ref.at[p.s], wsend.at[0])
        return rcopy(wt_ref, wall_ref.at[p.s], wsend.at[k], wrecv.at[p.s], p.on_seq(lax.rem(p.s + k, 4)))

    @pl.when(i == 0)
    def _():
        meet([p.on_seq(lax.rem(p.s + k, 4)) for k in range(1, 4)])
        for k in (2, 3, 1, 0):
            share(k).start()
        branch = mm(merged_ref[...], wo_ref[...], TN) + row(0)
        h, r = norm_parts(tok_ref[...].astype(f32) + branch)
        hat[...] = h
        inv[...] = r
        normed = h * row(1) + row(2)
        low[...] = normed.astype(bf16)
        acc[...] = normed + row(3)

    @pl.when(i < chunks)
    def _():
        pre = mm(low[...], up_ref[...]) + bup_ref[pl.ds(c, 1)]
        cdf = 0.5 + 0.5 * lax.erf(pre * math.sqrt(0.5))
        pdf = jnp.exp(-0.5 * pre * pre) * (1.0 / math.sqrt(2.0 * math.pi))
        a = (pre * cdf).astype(bf16)
        act[c] = a
        slope[c] = cdf + pre * pdf
        acc[...] += mm(a, down_ref[...])

    @pl.when(i == chunks - 1)
    def _():
        h, r = norm_parts(acc[...])
        result = h * row(4) + row(5)
        result_ref[...] = result.astype(bf16)
        grad = (result - teach_ref[...].astype(f32)) * (live_ref[...] * scale_ref[0])
        two = norm_back(grad * row(4), h, r)
        g = two.astype(bf16)
        grad_low[...] = g
        acc[...] = two
        dvec_ref[...] = jnp.zeros_like(dvec_ref)
        dvec_ref[3:4] = col_sum(g.astype(f32))
        dvec_ref[4:5] = col_sum(grad * h)
        dvec_ref[5:6] = col_sum(grad)

    @pl.when(i >= chunks)
    def _():
        g = grad_low[...]
        grad_pre = (mm(g, down_ref[...], NT) * slope[c]).astype(bf16)
        dbup_ref[pl.ds(c, 1)] = col_sum(grad_pre.astype(f32))
        down_own[c] = mm(act[c], g, TN).astype(bf16)
        swap_down(c).start()
        act[c] = mm(low[...], grad_pre, TN).astype(bf16)
        swap_up(c).start()
        acc[...] += mm(grad_pre, up_ref[...], NT)

    @pl.when(i > chunks)
    def _():
        settle(c + 1)

    @pl.when(i == 2 * chunks - 1)
    def _():
        grad = acc[...]
        h = hat[...]
        one = norm_back(grad * row(1), h, inv[...])
        resid_ref[...] = one
        g = one.astype(bf16)
        out_own[...] = mm(merged_ref[...], g).astype(bf16)
        swap_out().start()
        dvec_ref[0:1] = col_sum(g.astype(f32))
        dvec_ref[1:2] = col_sum(grad * h)
        dvec_ref[2:3] = col_sum(grad)
        gm_ref[...] = mm(wo_ref[...], g, NT).astype(bf16)
        settle(0)
        swap_out().wait_recv()
        dout_ref[...] = total(out_own, out_got).astype(bf16)
        swap_out().wait_send()
        for k in range(chunks):
            swap_down(k).wait_send()
            swap_up(k).wait_send()
        for k in range(1, 4):
            frm = lax.rem(p.s + k, 4)
            there = wall_ref.at[frm]
            rcopy(there, there, wsend.at[0], wrecv.at[frm], p.on_seq(frm)).wait_recv()
            share(k).wait_send()
        share(0).wait()


def feed_forward(scale, merged, tokens, teacher, live, w_out, vec, b_up, w_up, w_down, w_t, n, cid):
    toks, width = tokens.shape
    hidden = w_down.shape[0]
    size = 512
    chunks = hidden // size
    one = pl.Buffered(1)
    fixed = lambda shape: pl.BlockSpec(shape, lambda i: (0,) * len(shape), pipeline_mode=one)
    anywhere = pl.BlockSpec(memory_space=pl.ANY)
    turn = lambda i: jnp.where(i < chunks, i, 2 * chunks - 1 - i)
    dma = pltpu.SemaphoreType.DMA
    outs = [
        jax.ShapeDtypeStruct((toks, width), bf16),
        jax.ShapeDtypeStruct((toks, width), f32),
        jax.ShapeDtypeStruct(merged.shape, bf16),
        jax.ShapeDtypeStruct((width, width // 2), bf16),
        jax.ShapeDtypeStruct((2, width, hidden // 4), bf16),
        jax.ShapeDtypeStruct((hidden, width // 2), bf16),
        jax.ShapeDtypeStruct((8, width), f32),
        jax.ShapeDtypeStruct((chunks, size), f32),
    ]
    return pl.pallas_call(
        functools.partial(ffn_kernel, n, chunks),
        grid=(2 * chunks,),
        in_specs=[
            pl.BlockSpec(memory_space=pltpu.SMEM),
            fixed(merged.shape), fixed(tokens.shape), fixed(teacher.shape), fixed(live.shape), fixed(w_out.shape),
            fixed(vec.shape), fixed(b_up.shape),
            pl.BlockSpec((width, size), lambda i: (0, turn(i))),
            pl.BlockSpec((size, width), lambda i: (turn(i), 0)),
            anywhere,
        ],
        out_specs=[fixed(o.shape) for o in outs] + [anywhere],
        out_shape=outs + [jax.ShapeDtypeStruct((4,) + w_t.shape, bf16)],
        scratch_shapes=[
            pltpu.VMEM((toks, width), bf16),
            pltpu.VMEM((toks, width), f32),
            pltpu.VMEM((toks, 1), f32),
            pltpu.VMEM((toks, width), f32),
            pltpu.VMEM((toks, width), bf16),
            pltpu.VMEM((chunks, toks, size), bf16),
            pltpu.VMEM((chunks, toks, size), f32),
            pltpu.VMEM((chunks, size, width), bf16),
            pltpu.VMEM((chunks, size, width // 2), bf16),
            pltpu.VMEM((chunks, width, size // 2), bf16),
            pltpu.VMEM((width, width), bf16),
            pltpu.VMEM((width, width // 2), bf16),
            dma((2 * chunks + 1,)),
            dma((2 * chunks + 1,)),
            dma((4,)),
            dma((4,)),
        ],
        compiler_params=pltpu.CompilerParams(collective_id=cid, has_side_effects=True, vmem_limit_bytes=VMEM_LIMIT),
    )(scale, merged, tokens, teacher, live, w_out, vec, b_up, w_up, w_down, w_t)


def deliver_kernel(count, vsum_ref, brow_ref, *refs):
    srcs, outs, small, sem = refs[:count], refs[count : 2 * count], refs[2 * count : -1], refs[-1]
    copies = [pltpu.make_async_copy(a, b, sem.at[k]) for k, (a, b) in enumerate(zip(srcs, outs))]
    for cp in copies:
        cp.start()
    i = lax.axis_index("shard")
    width = vsum_ref.shape[1]

    def own(row, out):
        size = out.shape[1]
        shift = lax.rem(width - lax.rem(i * size, width), width)
        out[...] = pltpu.roll(jnp.broadcast_to(row, (8, width)), shift, 1)[:1, :size]

    own(brow_ref[0:1], small[0])
    own(brow_ref[2:3], small[1])
    for r in range(6):
        own(vsum_ref[r : r + 1], small[2 + r])
    row = 8 + (i * small[8].shape[1]) // width
    own(vsum_ref[pl.ds(row, 1)], small[8])
    for cp in copies:
        cp.wait()


def deliver(arrays, vsum, brow, rows, up_rows):
    count = len(arrays)
    vm = pl.BlockSpec(memory_space=pltpu.VMEM)
    anywhere = pl.BlockSpec(memory_space=pl.ANY)
    sizes = [rows] * 8 + [up_rows]
    got = pl.pallas_call(
        functools.partial(deliver_kernel, count),
        in_specs=[vm] * (2 + count),
        out_specs=[anywhere] * count + [vm] * len(sizes),
        out_shape=[jax.ShapeDtypeStruct(a.shape, a.dtype) for a in arrays] + [jax.ShapeDtypeStruct((1, s), f32) for s in sizes],
        scratch_shapes=[pltpu.SemaphoreType.DMA((count,))],
        compiler_params=pltpu.CompilerParams(vmem_limit_bytes=VMEM_LIMIT),
    )(vsum, brow, *arrays)
    return got[:count], [v.reshape(-1) for v in got[count:]]


def on_device(
    inputs, teacher, seq_lengths, w_qkv, q_bias, v_bias, w_out, out_bias, attn_gain, attn_shift, w_up, up_bias,
    w_down, down_bias, ffn_gain, ffn_shift,
):
    n = lax.axis_size("shard")
    s = lax.axis_index("seq")
    i = lax.axis_index("shard")
    toks, width = inputs.shape[1:]
    group = 4 * toks
    hidden = w_up.shape[1]
    rows = w_qkv.shape[0]
    heads = HEADS // 4
    folds = hidden // width
    tokens = inputs[0]
    lens = seq_lengths[0]
    ends = [lens[0], lens[0] + lens[1], lens[0] + lens[1] + lens[2]]

    own_w = lax.dynamic_index_in_dim(w_qkv.reshape(rows, 3, 4, heads, HD), s, 2, keepdims=False)
    own_w = jnp.transpose(own_w, (0, 2, 1, 3)).reshape(rows, heads * 3 * HD)
    live = jnp.stack([ends[2] // 64, lax.rem(ends[2], 64)]).astype(bf16)
    small = jnp.concatenate(
        [out_bias[None], attn_gain[None], attn_shift[None], down_bias[None], ffn_gain[None], ffn_shift[None], q_bias[None],
         v_bias[None], up_bias.reshape(folds, rows), jnp.broadcast_to(live[:, None], (2, rows))], axis=0
    )
    small = jnp.pad(small, ((0, 16 - small.shape[0]), (0, -rows % 128)))
    xg, wq_g, small_g = gather_all(tokens, (own_w, small), ("whole", "whole"), n, 1)
    x_all = xg.reshape(group, width)
    wq = wq_g.reshape(width, heads * 3 * HD)
    vecs = jnp.transpose(small_g[:, :, :rows], (1, 0, 2)).astype(f32)
    eight = vecs[:8].reshape(8, width)
    b_up = jnp.transpose(vecs[8 : 8 + folds], (1, 0, 2)).reshape(hidden // 512, 512)
    live_total = jnp.sum(vecs[8 + folds, :, 0]) * 64.0 + jnp.sum(vecs[9 + folds, :, 0])

    own_q, own_v = [
        lax.dynamic_slice_in_dim(eight[r], s * heads * HD, heads * HD).reshape(heads, 1, HD) for r in (6, 7)
    ]
    bias = jnp.concatenate([own_q, jnp.zeros_like(own_q), own_v], axis=1).reshape(heads, 3 * HD, 1)

    q, k, v, ctx, lse, w_t, merged, wo_g, down_g, up_g = attend(
        x_all, wq, bias, jnp.stack(ends), (w_out, w_down, w_up), ("half", "half", "quarter"), n, 2
    )
    own_pos = s * toks + lax.iota(jnp.int32, toks)
    live_rows = (own_pos < ends[2]).astype(f32)[:, None]
    scale = (float(group * n) / live_total).reshape(1)
    result, grad_resid_one, gm, d_out, d_up, d_down, dvec, d_bup, wall = feed_forward(
        scale, merged, tokens, teacher[0], live_rows, wo_g.reshape(width, width), eight, b_up,
        up_g.reshape(width, hidden),        down_g.reshape(hidden, width), w_t, n, 4,
    )
    vec = jnp.concatenate([dvec, d_bup.reshape(folds, width), jnp.zeros((8 - folds, width), f32)], axis=0)
    grad_in, d_qkv, brow, vsum, d_up_r, d_down_r, d_out_r = attend_back(
        q, k, v, ctx, lse, gm, x_all, wall, grad_resid_one, vec,
        (d_up.reshape(2, n, rows, hidden // 4), d_down.reshape(n, hidden // n, width // 2), d_out.reshape(n, rows, width // 2)),
        ("quarter", "half", "half"), n, 3,
    )

    big, small = deliver((result, grad_in, d_qkv, d_out_r, d_up_r, d_down_r), vsum, brow, rows, hidden // n)
    result, grad_in, d_qkv, d_out_r, d_up_r, d_down_r = big
    d_qb, d_vb, d_ob, d_ag, d_as, d_db, d_fg, d_fs, d_ub = small
    return (
        result[None], grad_in[None], d_qkv, d_qb, d_vb, d_out_r, d_ob, d_ag, d_as, d_up_r, d_ub, d_down_r, d_db, d_fg, d_fs,
    )


def solution(mesh):
    tokens, matrix, vector = P("shard", "seq", None), P("shard", None), P("shard")
    in_specs = (tokens, tokens, matrix, matrix, vector, vector, matrix, vector, vector, vector, matrix, vector, matrix,
                vector, vector, vector)
    out_specs = (tokens, tokens, matrix, vector, vector, matrix, vector, vector, vector, matrix, vector, matrix, vector,
                 vector, vector)
    return jax.shard_map(on_device, mesh=mesh, in_specs=in_specs, out_specs=out_specs, check_vma=False)
```
